32 devices in a mesh: shard: 4 (over z), ctx: 4 (over x, core), tensor: 2 (over y).
Axes of the slice: x: 2, y: 2, z: 4, core: 2. Of those that a mesh axis runs over, the one named last changes fastest.
Arguments:
- inputs: bfloat16 [4, 2048, 1024], P('shard', ('ctx', 'tensor')), may hold values from -6 to 6
- ln1_gain: bfloat16 [1024], P(('shard', 'ctx', 'tensor')), may hold values from 0.25 to 1.75
- ln1_bias: bfloat16 [1024], P(('shard', 'ctx', 'tensor')), may hold values from -3 to 3
- ln2_gain: bfloat16 [1024], P(('shard', 'ctx', 'tensor')), may hold values from 0.25 to 1.75
- ln2_bias: bfloat16 [1024], P(('shard', 'ctx', 'tensor')), may hold values from -3 to 3
- w_qkv: bfloat16 [3, 1024, 1024], P(None, ('shard', 'ctx'), 'tensor'), may hold values from -0.1875 to 0.1875
- b_qkv: bfloat16 [3, 2, 512], P(None, 'tensor', ('shard', 'ctx')), may hold values from -3 to 3
- w_out: bfloat16 [1024, 1024], P('tensor', ('shard', 'ctx')), may hold values from -0.75 to 0.75
- b_out: bfloat16 [1024], P(('shard', 'ctx', 'tensor')), may hold values from -3 to 3
- w_up: bfloat16 [1024, 4096], P(('shard', 'ctx'), 'tensor'), may hold values from -0.1875 to 0.1875
- b_up: bfloat16 [2, 2048], P('tensor', ('shard', 'ctx')), may hold values from -3 to 3
- w_down: bfloat16 [4096, 1024], P('tensor', ('shard', 'ctx')), may hold values from -0.09375 to 0.09375
- b_down: bfloat16 [1024], P(('shard', 'ctx', 'tensor')), may hold values from -3 to 3
- cotangent: bfloat16 [4, 2048, 1024], P('shard', ('ctx', 'tensor')), may hold values from -6 to 6
Outputs:
- output: bfloat16 [4, 2048, 1024], P('shard', ('ctx', 'tensor'))
- grad_inputs: float32 [4, 2048, 1024], P('shard', ('ctx', 'tensor'))
- grad_ln1_gain: float32 [1024], P(('shard', 'ctx', 'tensor'))
- grad_ln1_bias: float32 [1024], P(('shard', 'ctx', 'tensor'))
- grad_ln2_gain: float32 [1024], P(('shard', 'ctx', 'tensor'))
- grad_ln2_bias: float32 [1024], P(('shard', 'ctx', 'tensor'))
- grad_w_qkv: float32 [3, 1024, 1024], P(None, ('shard', 'ctx'), 'tensor')
- grad_b_qkv: float32 [3, 2, 512], P(None, 'tensor', ('shard', 'ctx'))
- grad_w_out: float32 [1024, 1024], P('tensor', ('shard', 'ctx'))
- grad_b_out: float32 [1024], P(('shard', 'ctx', 'tensor'))
- grad_w_up: float32 [1024, 4096], P(('shard', 'ctx'), 'tensor')
- grad_b_up: float32 [2, 2048], P('tensor', ('shard', 'ctx'))
- grad_w_down: float32 [4096, 1024], P('tensor', ('shard', 'ctx'))
- grad_b_down: float32 [1024], P(('shard', 'ctx', 'tensor'))
The draws below stay inside these ranges and needn't reach their ends.
All inputs are finite; a program needn't handle non-finite values.
Results may differ from the reference program's by a relative error of at most 0.0097.
Values may be sent and summed in bfloat16 or wider, within the bound.
A program may use at most 128 MiB of HBM per device.

```python
import jax
import jax.numpy as jnp
from jax import lax

D = 1024
H = 16
HD = 64
ROT = 16
FF = 4096
SEQ = 2048
SEQS = 4
N_TENSOR = 2


def block_levels(own_key, dims, shards, least, high):
    def one(axis_at, shards_of):
        draws = jax.random.uniform(jax.random.fold_in(jax.random.fold_in(own_key, 6), axis_at), (shards_of,), jnp.float32, least / len(shards), high / len(shards))
        return jnp.repeat(jnp.exp(draws), dims[axis_at] // shards_of).reshape((-1,) + (1,) * (len(dims) - axis_at - 1))

    level = one(*shards[0])
    for cut in shards[1:]:
        level = level * one(*cut)
    return level


def noise(stream_key, shape, deviation, limit, split=(), kind=jnp.bfloat16):
    values = jax.random.normal(stream_key, shape, jnp.float32) * deviation
    if len(split) > 0:
        values = block_levels(stream_key, shape, split, -0.22, 0.18) * values
    return jnp.clip(values, min=-limit, max=limit).astype(kind)


def setup_inputs(seed: int = 0) -> dict:
    keys = jax.random.split(jax.random.key(seed), 15)
    return {
        "inputs": noise(keys[0], (SEQS, SEQ, D), 1.0, 6.0, ((0, 4), (1, 8))),
        "ln1_gain": jnp.clip(1.0 + 0.15 * jax.random.normal(keys[1], (D,), jnp.float32), 0.25, 1.75).astype(jnp.bfloat16),
        "ln1_bias": noise(keys[2], (D,), 0.5, 3.0, ((0, 32),)),
        "ln2_gain": jnp.clip(1.0 + 0.15 * jax.random.normal(keys[3], (D,), jnp.float32), 0.25, 1.75).astype(jnp.bfloat16),
        "ln2_bias": noise(keys[4], (D,), 0.5, 3.0, ((0, 32),)),
        "w_qkv": noise(keys[5], (3, D, D), D ** -0.5, 0.1875, ((1, 16), (2, 2))),
        "b_qkv": noise(keys[6], (3, N_TENSOR, D // N_TENSOR), 0.5, 3.0, ((1, 2), (2, 16))),
        "w_out": noise(keys[7], (D, D), (D // 16) ** -0.5, 0.75, ((0, 2), (1, 16))),
        "b_out": noise(keys[8], (D,), 0.5, 3.0, ((0, 32),)),
        "w_up": noise(keys[9], (D, FF), D ** -0.5, 0.1875, ((0, 16), (1, 2))),
        "b_up": noise(keys[10], (N_TENSOR, FF // N_TENSOR), 0.5, 3.0, ((0, 2), (1, 16))),
        "w_down": noise(keys[11], (FF, D), FF ** -0.5, 0.09375, ((0, 2), (1, 16))),
        "b_down": noise(keys[12], (D,), 0.5, 3.0, ((0, 32),)),
        "cotangent": noise(keys[13], (SEQS, SEQ, D), 1.0, 6.0, ((0, 4), (1, 8))),
    }


norm_eps = 1e-05
rope_base = 10000.0
highest = lax.Precision.HIGHEST

@jax.custom_vjp
def low(v):
    return lax.optimization_barrier(v.astype(jnp.bfloat16)).astype(jnp.float32)

@jax.custom_vjp
def low_back(v):
    return v

def low_keep(v):
    return (low(v), None)

def low_pass(kept, grad):
    return (grad,)

def back_keep(v):
    return (v, None)

def back_low(kept, grad):
    return (low(grad),)
low.defvjp(low_keep, low_pass)
low_back.defvjp(back_keep, back_low)

def layer_norm(values, gain, shift):
    centre = values - lax.optimization_barrier(jnp.mean(values, -1, keepdims=True))
    spread = lax.optimization_barrier(jnp.mean(centre * centre, -1, keepdims=True))
    return centre * lax.rsqrt(spread + norm_eps) * gain + shift

def rotary_tables(positions):
    half_dims = ROT // 2
    ladder = jnp.arange(half_dims, dtype=jnp.float32)
    inverse = jnp.exp(ladder * (-2.0 / ROT) * jnp.log(jnp.float32(rope_base)))
    angles = positions.astype(jnp.float32)[:, None] * inverse[None, :]
    angles = jnp.concatenate([angles, angles], -1)
    return (jnp.cos(angles)[:, None, :], jnp.sin(angles)[:, None, :])

def rotate(values, cosine, sine_table):
    rot_dims = cosine.shape[-1]
    half_dims = rot_dims // 2
    turned = values[..., :rot_dims]
    swapped = jnp.concatenate([-turned[..., half_dims:], turned[..., :half_dims]], -1)
    return jnp.concatenate([turned * cosine + swapped * sine_table, values[..., rot_dims:]], -1)

def layer_forward(params, values):
    ln1_gain, ln1_bias, ln2_gain, ln2_bias, w_qkv, b_qkv, w_out, b_out, w_up, b_up, w_down, b_down = params
    first_norm = low(layer_norm(values, ln1_gain, ln1_bias))
    second_norm = low(layer_norm(values, ln2_gain, ln2_bias))
    projected = jnp.einsum('sd,jde->jse', first_norm, w_qkv, precision=highest) + b_qkv.reshape(3, 1, D)
    projected = low_back(projected)
    cosine, sine_table = rotary_tables(jnp.arange(SEQ, dtype=jnp.int32))
    queries = low(low_back(rotate(projected[0].reshape(SEQ, H, HD), cosine, sine_table)))
    key_rows = low(low_back(rotate(projected[1].reshape(SEQ, H, HD), cosine, sine_table)))
    value_rows = low(projected[2].reshape(SEQ, H, HD))
    block_rows = min(512, SEQ)
    block_count = SEQ // block_rows
    score_scale = HD ** (-0.5)
    key_pos = jnp.arange(SEQ, dtype=jnp.int32)

    def attend_block(block_pack):
        query_block, offset = block_pack
        scores = jnp.einsum('qhd,khd->hqk', query_block, key_rows, precision=highest) * score_scale
        scores = low_back(scores)
        causal = key_pos[None, :] <= (offset + jnp.arange(block_rows, dtype=jnp.int32))[:, None]
        scores = jnp.where(causal[None], scores, -1e+30)
        attn_prob = low(jax.nn.softmax(scores, -1))
        return jnp.einsum('hqk,khd->qhd', attn_prob, value_rows, precision=highest)
    offsets = jnp.arange(block_count, dtype=jnp.int32) * block_rows
    mixed_blocks = lax.map(jax.checkpoint(attend_block), (queries.reshape(block_count, block_rows, H, HD), offsets))
    heads_out = low_back(low(mixed_blocks.reshape(SEQ, D)))
    attention = jnp.dot(heads_out, w_out, precision=highest) + b_out
    hidden_pre = low_back(jnp.dot(second_norm, w_up, precision=highest) + b_up.reshape(FF))
    hidden = low(jax.nn.gelu(hidden_pre, approximate=False))
    feed_out = jnp.dot(hidden, w_down, precision=highest) + b_down
    return values + attention + feed_out

def reference(inputs, ln1_gain, ln1_bias, ln2_gain, ln2_bias, w_qkv, b_qkv, w_out, b_out, w_up, b_up, w_down, b_down, cotangent):
    params = tuple((weight.astype(jnp.float32) for weight in (ln1_gain, ln1_bias, ln2_gain, ln2_bias, w_qkv, b_qkv, w_out, b_out, w_up, b_up, w_down, b_down)))

    def one_sequence(totals, seq_pair):
        seq_in, seq_cot = seq_pair
        result, pullback = jax.vjp(layer_forward, params, seq_in.astype(jnp.float32))
        param_grads, input_grad = pullback(seq_cot.astype(jnp.float32))
        totals = jax.tree.map(lambda running, update: running + update, totals, param_grads)
        return (totals, (result.astype(jnp.bfloat16), input_grad))
    zero_state = jax.tree.map(jnp.zeros_like, params)
    totals, (outputs, input_grads) = lax.scan(one_sequence, zero_state, (inputs, cotangent))
    return (outputs, input_grads, totals[0], totals[1], totals[2], totals[3], totals[4], totals[5], totals[6], totals[7], totals[8], totals[9], totals[10], totals[11])
```

```python
import functools

import jax
import jax.numpy as jnp
import numpy as np
from jax import lax
from jax.experimental import pallas as pl
from jax.experimental.pallas import tpu as pltpu
from jax.sharding import PartitionSpec as P

HD = 64
ROT = 16


norm_eps = 1e-05
rope_base = 10000.0
bf16 = jnp.bfloat16
f32 = jnp.float32
GROUP = ("shard", "ctx")


def layer_norm_parts(values):
    centre = values - jnp.mean(values, -1, keepdims=True)
    spread = jnp.mean(centre * centre, -1, keepdims=True)
    inv_std = lax.rsqrt(spread + norm_eps)
    return (centre * inv_std, inv_std)


def rotary_tables(positions):
    half_dims = ROT // 2
    ladder = jnp.arange(half_dims, dtype=f32)
    inverse = jnp.exp(ladder * (-2.0 / ROT) * jnp.log(f32(rope_base)))
    angles = positions.astype(f32)[:, None] * inverse[None, :]
    angles = jnp.concatenate([angles, angles], -1)
    return (jnp.cos(angles)[:, None, :], jnp.sin(angles)[:, None, :])


def rotate(values, cosine, sine_table):
    rot_dims = cosine.shape[-1]
    half_dims = rot_dims // 2
    turned = values[..., :rot_dims]
    swapped = jnp.concatenate([-turned[..., half_dims:], turned[..., :half_dims]], -1)
    return jnp.concatenate([turned * cosine + swapped * sine_table, values[..., rot_dims:]], -1)


def gelu_slope(values):
    return (
        0.5 * (1.0 + lax.erf(values * 0.7071067811865476))
        + values * jnp.exp(-0.5 * values * values) * 0.3989422804014327
    )


def contract_last(left_side, right_side):
    return lax.dot_general(
        left_side, right_side, (((1,), (1,)), ((), ())), preferred_element_type=f32
    )


def contract_first(left_side, right_side):
    return lax.dot_general(
        left_side, right_side, (((0,), (0,)), ((), ())), preferred_element_type=f32
    )


def attention_kernel(lanes, wide, rows, in_ref, out_ref, key_grad, value_grad):
    seq_len = in_ref.shape[0]
    heads = lanes // HD
    parts = wide // rows
    scale = HD ** (-0.5)
    key_grad[...] = jnp.zeros_like(key_grad)
    value_grad[...] = jnp.zeros_like(value_grad)
    out_ref[...] = jnp.zeros_like(out_ref)
    for step in range(seq_len // wide):
        length = (step + 1) * wide

        def one_block(turn, carry, step=step, length=length):
            head = turn % heads
            start = pl.multiple_of(step * wide + (turn // heads) * rows, rows)
            here = pl.ds(start, rows)
            mine = lax.broadcasted_iota(jnp.int32, (rows, lanes), 1) // HD == head
            queries = in_ref[here, 0:lanes].astype(f32) * scale
            queries = jnp.where(mine, queries, 0.0).astype(bf16)
            grads = in_ref[here, 3 * lanes : 4 * lanes].astype(f32)
            grads = jnp.where(mine, grads, 0.0).astype(bf16)
            keys = in_ref[0:length, lanes : 2 * lanes]
            values = in_ref[0:length, 2 * lanes : 3 * lanes]
            scores = contract_last(queries, keys)
            key_at = lax.broadcasted_iota(jnp.int32, scores.shape, 1)
            query_at = start + lax.broadcasted_iota(jnp.int32, scores.shape, 0)
            scores = jnp.where(key_at <= query_at, scores, -1e30)
            exp_scores = jnp.exp(scores - jnp.max(scores, -1, keepdims=True))
            probs = exp_scores * (1.0 / jnp.sum(exp_scores, -1, keepdims=True))
            attn_prob = probs.astype(bf16)
            mixed = jnp.dot(attn_prob, values, preferred_element_type=f32)
            value_grad[0:length, :] += contract_first(attn_prob, grads)
            prob_grad = contract_last(grads, values)
            inner_sum = jnp.sum(probs * prob_grad, -1, keepdims=True)
            score_grad = (probs * (prob_grad - inner_sum)).astype(bf16)
            query_grad = jnp.dot(score_grad, keys, preferred_element_type=f32) * scale
            key_grad[0:length, :] += contract_first(score_grad, queries)
            out_ref[here, 0:lanes] = jnp.where(
                mine, mixed, out_ref[here, 0:lanes].astype(f32)
            ).astype(bf16)
            out_ref[here, lanes : 2 * lanes] = jnp.where(
                mine, query_grad, out_ref[here, lanes : 2 * lanes].astype(f32)
            ).astype(bf16)
            return carry

        lax.fori_loop(0, parts * heads, one_block, 0)
    out_ref[:, 2 * lanes : 3 * lanes] = key_grad[...].astype(bf16)
    out_ref[:, 3 * lanes : 4 * lanes] = value_grad[...].astype(bf16)


def attend(packed):
    seq_len, width = packed.shape
    lanes = width // 4
    wide = min(512, seq_len)
    rows = min(256, wide)
    return pl.pallas_call(
        functools.partial(attention_kernel, lanes, wide, rows),
        out_shape=jax.ShapeDtypeStruct((seq_len, width), bf16),
        in_specs=[pl.BlockSpec(memory_space=pltpu.VMEM)],
        out_specs=pl.BlockSpec(memory_space=pltpu.VMEM),
        scratch_shapes=[pltpu.VMEM((seq_len, lanes), f32), pltpu.VMEM((seq_len, lanes), f32)],
        compiler_params=pltpu.CompilerParams(vmem_limit_bytes=48 << 20),
        cost_estimate=pl.CostEstimate(
            flops=14 * seq_len * seq_len * lanes,
            bytes_accessed=4 * seq_len * width,
            transcendentals=seq_len * seq_len * lanes // HD,
        ),
    )(packed)


def per_device(
    inputs,
    ln1_gain,
    ln1_bias,
    ln2_gain,
    ln2_bias,
    w_qkv,
    b_qkv,
    w_out,
    b_out,
    w_up,
    b_up,
    w_down,
    b_down,
    cotangent,
):
    pair = lax.axis_index("tensor")
    first = pair == 0
    n_ctx = lax.axis_size("ctx")
    n_group = lax.axis_size("shard") * n_ctx
    swap = ((0, 1), (1, 0))

    def exchange(value):
        return lax.ppermute(value, "tensor", swap)

    def in_order(own, other, axis):
        return jnp.where(
            first,
            jnp.concatenate([own, other], axis),
            jnp.concatenate([other, own], axis),
        )

    small_own = jnp.stack([ln1_gain, ln1_bias, ln2_gain, ln2_bias, b_out, b_down])
    small = in_order(small_own, exchange(small_own), 1)
    piece = small.shape[1]
    depth = w_up.shape[0]
    ff_group = w_up.shape[1]
    width = w_qkv.shape[2]
    riders = jnp.concatenate([small.reshape(-1), b_qkv.reshape(-1), b_up.reshape(-1)])
    room = depth * 128
    riders = jnp.pad(riders, (0, room - riders.shape[0])).reshape(depth, 128)
    first_pack = jnp.concatenate([w_qkv[0], w_qkv[1], w_qkv[2], w_out.T, riders], 1)
    second_pack = jnp.concatenate([w_up, w_down.T], 1)
    first_whole = lax.all_gather(first_pack, GROUP, axis=0, tiled=True)
    second_whole = lax.all_gather(second_pack, GROUP, axis=0, tiled=True)
    model = first_whole.shape[0]
    whole_qkv = first_whole[:, : 3 * width]
    whole_out_t = first_whole[:, 3 * width : 4 * width]
    gathered = first_whole[:, 4 * width :].reshape(n_group, room).astype(f32)
    whole_up = second_whole[:, :ff_group]
    whole_down_t = second_whole[:, ff_group:]

    gain_one, shift_one, gain_two, shift_two, bias_out, bias_down = [
        gathered[:, at * piece : (at + 1) * piece].reshape(-1) for at in range(6)
    ]
    at = 6 * piece
    part = b_qkv.shape[2]
    bias_qkv = jnp.concatenate(
        [gathered[:, at + j * part : at + (j + 1) * part].reshape(-1) for j in range(3)]
    )
    at = at + 3 * part
    up_part = b_up.shape[1]
    bias_up = gathered[:, at : at + up_part].reshape(-1)

    both_own = jnp.concatenate([inputs, cotangent], 0)
    both = in_order(both_own, exchange(both_own), 1)
    grad_own = cotangent[0]
    own_rows = inputs[0].astype(f32)
    normed_own, inv_own = layer_norm_parts(own_rows)
    normed, _ = layer_norm_parts(both[0].astype(f32))
    grad_rows = both[1]
    first_norm = (normed * gain_one + shift_one).astype(bf16)
    second_norm = (normed * gain_two + shift_two).astype(bf16)
    block_len = first_norm.shape[0]
    half = block_len // 2

    def own_half(value):
        return jnp.where(first, value[:half], value[half:])

    def other_half(value):
        return jnp.where(first, value[half:], value[:half])

    positions = lax.axis_index("ctx") * block_len + jnp.arange(block_len, dtype=jnp.int32)
    cosine, sine_table = rotary_tables(positions)
    projected = jnp.dot(first_norm, whole_qkv, preferred_element_type=f32) + bias_qkv
    heads = width // HD

    def turned(value, sine):
        return (
            rotate(value.astype(f32).reshape(block_len, heads, HD), cosine, sine)
            .astype(bf16)
            .reshape(block_len, width)
        )

    queries = turned(projected[:, :width], sine_table)
    key_rows = turned(projected[:, width : 2 * width], sine_table)
    value_rows = projected[:, 2 * width :].astype(bf16)
    grad_mixed = jnp.dot(grad_rows, whole_out_t, preferred_element_type=f32).astype(bf16)
    lanes = width // n_ctx
    packed = jnp.stack([queries, key_rows, value_rows, grad_mixed])
    packed = packed.reshape(4, block_len, n_ctx, lanes).transpose(2, 1, 0, 3)
    packed = packed.reshape(n_ctx, block_len, 4 * lanes)
    there = lax.all_to_all(packed, "ctx", split_axis=0, concat_axis=0, tiled=True)

    hidden_pre = jnp.dot(second_norm, whole_up, preferred_element_type=f32) + bias_up
    hidden = jax.nn.gelu(hidden_pre, approximate=False).astype(bf16)
    feed_out = contract_last(hidden, whole_down_t)
    grad_hidden = jnp.dot(grad_rows, whole_down_t, preferred_element_type=f32)
    grad_pre = (grad_hidden * gelu_slope(hidden_pre)).astype(bf16)
    grad_up = contract_first(second_norm, grad_pre).astype(bf16)
    grad_down_t = contract_first(grad_rows, hidden).astype(bf16)
    second_grads = jnp.concatenate([grad_up, grad_down_t], 1)
    there, second_grads = lax.optimization_barrier((there, second_grads))
    second_sum = lax.psum_scatter(second_grads, GROUP, scatter_dimension=0, tiled=True)
    grad_b_up = jnp.sum(grad_pre, 0, dtype=f32)
    grad_second = contract_last(grad_pre, whole_up)

    attended = attend(there.reshape(n_ctx * block_len, 4 * lanes))
    back = lax.all_to_all(
        attended.reshape(n_ctx, block_len, 4 * lanes),
        "ctx",
        split_axis=0,
        concat_axis=0,
        tiled=True,
    )
    back = back.reshape(n_ctx, block_len, 4, lanes).transpose(2, 1, 0, 3)
    mixed_rows, query_back, key_back, value_back = back.reshape(4, block_len, width)
    grad_projected = jnp.concatenate(
        [turned(query_back, -sine_table), turned(key_back, -sine_table), value_back], 1
    )
    grad_qkv = contract_first(first_norm, grad_projected).astype(bf16)
    grad_out_t = contract_first(grad_rows, mixed_rows).astype(bf16)
    grad_b_qkv = jnp.sum(grad_projected, 0, dtype=f32)
    grad_first = contract_last(grad_projected, whole_qkv)

    vectors = jnp.stack(
        [
            jnp.sum(grad_first * normed, 0),
            jnp.sum(grad_first, 0),
            jnp.sum(grad_second * normed, 0),
            jnp.sum(grad_second, 0),
            jnp.sum(grad_own.astype(f32), 0),
        ]
    )
    back_riders = jnp.concatenate(
        [
            vectors.reshape(5, n_group, piece).transpose(1, 0, 2).reshape(n_group, -1),
            grad_b_qkv.reshape(3, n_group, part).transpose(1, 0, 2).reshape(n_group, -1),
            grad_b_up.reshape(n_group, up_part),
        ],
        1,
    )
    back_riders = jnp.pad(back_riders, ((0, 0), (0, room - back_riders.shape[1])))
    back_riders = back_riders.reshape(model, 128).astype(bf16)
    first_grads = jnp.concatenate([grad_qkv, grad_out_t, back_riders], 1)
    first_grads, second_sum = lax.optimization_barrier((first_grads, second_sum))
    first_sum = lax.psum_scatter(first_grads, GROUP, scatter_dimension=0, tiled=True)

    partial_sum = contract_last(mixed_rows, whole_out_t) + feed_out
    branches = own_half(partial_sum) + exchange(other_half(partial_sum).astype(bf16)).astype(f32)
    output = (own_rows + branches + bias_out + bias_down).astype(bf16)
    scaled = grad_first * gain_one + grad_second * gain_two
    scaled = own_half(scaled) + exchange(other_half(scaled).astype(bf16)).astype(f32)
    inner_sum = jnp.mean(scaled, -1, keepdims=True)
    aligned = jnp.mean(scaled * normed_own, -1, keepdims=True)
    grad_input = grad_own.astype(f32) + inv_own * (scaled - inner_sum - normed_own * aligned)

    second_sum = second_sum.astype(f32)
    first_sum = first_sum.astype(f32)
    grad_w_qkv = first_sum[:, : 3 * width].reshape(depth, 3, width).transpose(1, 0, 2)
    grad_w_out = first_sum[:, 3 * width : 4 * width].T
    summed = first_sum[:, 4 * width :].reshape(-1)
    vector_sum = summed[: 5 * piece].reshape(5, piece)
    own = piece // 2
    mine = jnp.where(first, vector_sum[:, :own], vector_sum[:, own:])
    theirs = jnp.where(first, vector_sum[:, own:], vector_sum[:, :own])
    vector_grads = mine + exchange(theirs)
    at = 5 * piece
    out_b_qkv = summed[at : at + 3 * part].reshape(3, 1, part)
    at = at + 3 * part
    out_b_up = summed[at : at + up_part].reshape(1, up_part)
    return (
        output[None],
        grad_input[None],
        vector_grads[0],
        vector_grads[1],
        vector_grads[2],
        vector_grads[3],
        grad_w_qkv,
        out_b_qkv,
        grad_w_out,
        vector_grads[4],
        second_sum[:, :ff_group],
        out_b_up,
        second_sum[:, ff_group:].T,
        vector_grads[4],
    )

def remote(src, dst, sends, recvs, at, to):
    return pltpu.make_async_remote_copy(
        src_ref=src,
        dst_ref=dst,
        send_sem=sends.at[at],
        recv_sem=recvs.at[at],
        device_id=to,
        device_id_type=pl.DeviceIdType.MESH,
    )


class Place:
    def __init__(self):
        self.s = lax.axis_index("shard")
        self.c = lax.axis_index("ctx")
        self.t = lax.axis_index("tensor")
        self.x = self.c // 2
        self.k = self.c % 2
        self.block = 2 * self.c + self.t
        self.core_c = 2 * self.x + (1 - self.k)
        self.x_c = 2 * (1 - self.x) + self.k
        self.far_c = 2 * (1 - self.x) + (1 - self.k)
        self.y_t = 1 - self.t
        self.core = {"ctx": self.core_c}
        self.across_x = {"ctx": self.x_c}
        self.far = {"ctx": self.far_c}
        self.across_y = {"tensor": self.y_t}

    def along(self, step):
        return {"shard": lax.rem(self.s + step + 4, 4)}

    def meet(self):
        barrier = pltpu.get_barrier_semaphore()
        others = [self.core, self.across_x, self.far, self.across_y]
        others += [self.along(step) for step in (1, 2, 3)]
        for other in others:
            pl.semaphore_signal(
                barrier, inc=1, device_id=other, device_id_type=pl.DeviceIdType.MESH
            )
        pl.semaphore_wait(barrier, len(others))

    def cube(self):
        pair = self.s + 1 - 2 * lax.rem(self.s, 2)
        return [
            self.core,
            {"shard": pair},
            self.along(2),
            self.across_x,
            self.across_y,
        ]


class PlaneGather:
    def __init__(self, place, own, full, sends, recvs, local):
        half = own.shape[0] // 2
        b = place.block
        xb = 2 * place.x_c + place.t
        yb = 2 * place.c + place.y_t
        db = 2 * place.x_c + place.y_t
        low, high = pl.ds(0, half), pl.ds(half, half)

        def to(src, dst, at, dev):
            return remote(src, dst, sends, recvs, at, dev)

        self.local = pltpu.make_async_copy(own, full.at[b], local)
        self.to_x = to(own, full.at[b], 0, place.across_x)
        self.to_y = to(own, full.at[b], 1, place.across_y)
        self.low_y = to(full.at[xb, low], full.at[xb, low], 2, place.across_y)
        self.high_x = to(full.at[yb, high], full.at[yb, high], 3, place.across_x)
        self.core_own = to(own, full.at[b], 4, place.core)
        self.core_x = to(full.at[xb], full.at[xb], 5, place.core)
        self.core_y = to(full.at[yb], full.at[yb], 6, place.core)
        self.core_d = to(full.at[db], full.at[db], 7, place.core)
        self.all = [
            self.to_x, self.to_y, self.low_y, self.high_x,
            self.core_own, self.core_x, self.core_y, self.core_d,
        ]

    def start(self):
        self.to_x.start()
        self.to_y.start()
        self.core_own.start()
        self.local.start()

    def second(self):
        self.to_x.wait_recv()
        self.low_y.start()
        self.core_x.start()
        self.to_y.wait_recv()
        self.high_x.start()
        self.core_y.start()

    def third(self):
        self.low_y.wait_recv()
        self.high_x.wait_recv()
        self.core_d.start()

    def finish(self):
        self.local.wait()
        for copy in (self.core_own, self.core_x, self.core_y, self.core_d):
            copy.wait_recv()

    def drain(self):
        for copy in self.all:
            copy.wait_send()


class CtxSwap:
    def __init__(self, place, own, dst, sends, recvs, local):
        c = place.c
        self.copies = []
        for at, (peer, dev) in enumerate(
            ((place.core_c, place.core), (place.x_c, place.across_x), (place.far_c, place.far))
        ):
            self.copies.append(remote(own.at[peer], dst.at[c], sends, recvs, at, dev))
        self.local = pltpu.make_async_copy(own.at[c], dst.at[c], local)

    def start(self):
        for copy in self.copies:
            copy.start()
        self.local.start()

    def finish(self):
        for copy in self.copies:
            copy.wait_recv()
        self.local.wait()

    def drain(self):
        for copy in self.copies:
            copy.wait_send()


class ChainGather:
    def __init__(self, place, full, right, left, recvs):
        self.s = place.s
        s = place.s

        def copy(j, sends, dev):
            return pltpu.make_async_remote_copy(
                src_ref=full.at[j],
                dst_ref=full.at[j],
                send_sem=sends.at[j],
                recv_sem=recvs.at[j],
                device_id=dev,
                device_id_type=pl.DeviceIdType.MESH,
            )

        self.to_right = lambda j: copy(j, right, place.along(1))
        self.to_left = lambda j: copy(j, left, place.along(-1))

    def start(self):
        s = self.s

        @pl.when(s < 3)
        def _():
            self.to_right(s).start()

        @pl.when(s > 0)
        def _():
            self.to_left(s).start()

    def step(self, distance):
        s = self.s

        @pl.when(s >= distance)
        def _():
            self.to_right(s - distance).wait_recv()

            @pl.when(s < 3)
            def _():
                self.to_right(s - distance).start()

        @pl.when(s + distance <= 3)
        def _():
            self.to_left(s + distance).wait_recv()

            @pl.when(s > 0)
            def _():
                self.to_left(s + distance).start()

    def drain(self):
        s = self.s
        for distance in range(4):

            @pl.when((s >= distance) & (s < 3))
            def _():
                self.to_right(s - distance).wait_send()

            @pl.when((s + distance <= 3) & (s > 0))
            def _():
                self.to_left(s + distance).wait_send()


class CubeSum:
    def __init__(self, place, total, slots, sends, recvs):
        self.total, self.slots = total, slots
        self.copies = [
            remote(total, slots.at[at], sends, recvs, at, dev)
            for at, dev in enumerate(place.cube())
        ]

    def start(self, at):
        self.copies[at].start()

    def finish(self, at):
        self.copies[at].wait()
        self.total[...] += self.slots[at]


def gather_kernel(
    x_own, dy_own, wa_own, wm_own, small_own,
    x_all, dy_all, wa_all, wm_all, small_all,
    slots,
    x_send, x_recv, dy_send, dy_recv, wa_send, wa_recv, wm_send, wm_recv,
    ca_right, ca_left, ca_recv, cm_right, cm_left, cm_recv, cube_send, cube_recv, local,
):
    place = Place()
    small_all[...] = small_own[...]
    place.meet()
    xs = PlaneGather(place, x_own, x_all, x_send, x_recv, local.at[0])
    dys = PlaneGather(place, dy_own, dy_all, dy_send, dy_recv, local.at[1])
    swap_a = CtxSwap(place, wa_own, wa_all.at[place.s], wa_send, wa_recv, local.at[2])
    swap_m = CtxSwap(place, wm_own, wm_all.at[place.s], wm_send, wm_recv, local.at[3])
    chain_a = ChainGather(place, wa_all, ca_right, ca_left, ca_recv)
    chain_m = ChainGather(place, wm_all, cm_right, cm_left, cm_recv)
    cube = CubeSum(place, small_all, slots, cube_send, cube_recv)
    cube.start(0)
    swap_a.start()
    swap_m.start()
    xs.start()
    dys.start()
    cube.finish(0)
    cube.start(1)
    cube.finish(1)
    cube.start(2)
    cube.finish(2)
    swap_a.finish()
    chain_a.start()
    cube.start(3)
    swap_m.finish()
    chain_m.start()
    xs.second()
    cube.finish(3)
    cube.start(4)
    chain_a.step(1)
    xs.third()
    chain_a.step(2)
    dys.second()
    chain_m.step(1)
    cube.finish(4)
    chain_a.step(3)
    dys.third()
    xs.finish()
    dys.finish()
    chain_m.step(2)
    chain_m.step(3)
    for part in (xs, dys, swap_a, swap_m, chain_a, chain_m):
        part.drain()


def gather_all(x_own, dy_own, wa_own, wm_own, small_own):
    rows, model = x_own.shape
    n_ctx, depth, wide_a = wa_own.shape
    wide_m = wm_own.shape[2]
    anywhere = pl.BlockSpec(memory_space=pl.ANY)
    vmem = pl.BlockSpec(memory_space=pltpu.VMEM)
    dma = pltpu.SemaphoreType.DMA
    return pl.pallas_call(
        gather_kernel,
        out_shape=(
            jax.ShapeDtypeStruct((8, rows, model), bf16),
            jax.ShapeDtypeStruct((8, rows, model), bf16),
            jax.ShapeDtypeStruct((4, n_ctx, depth, wide_a), bf16),
            jax.ShapeDtypeStruct((4, n_ctx, depth, wide_m), bf16),
            jax.ShapeDtypeStruct(small_own.shape, f32),
        ),
        in_specs=[anywhere] * 4 + [vmem],
        out_specs=[anywhere] * 4 + [vmem],
        scratch_shapes=[pltpu.VMEM((5,) + small_own.shape, f32)]
        + [dma((8,))] * 4
        + [dma((3,))] * 4
        + [dma((4,))] * 6
        + [dma((5,))] * 2
        + [dma((4,))],
        compiler_params=pltpu.CompilerParams(
            collective_id=0, has_side_effects=True, vmem_limit_bytes=16 << 20
        ),
    )(x_own, dy_own, wa_own, wm_own, small_own)


class PlaneReduce:
    def __init__(self, place, parts, came, kept, low_in, high_in, x_in, y_in, sends, recvs):
        self.place, self.parts, self.came, self.kept = place, parts, came, kept
        self.low_in, self.high_in, self.x_in, self.y_in = low_in, high_in, x_in, y_in
        x, t, k = place.x, place.t, place.k
        half = parts.shape[1] // 2
        self.half = half
        self.first = []
        for at in range(4):
            src = parts.at[4 * (at // 2) + 2 * (1 - k) + at % 2]
            self.first.append(remote(src, came.at[at], sends, recvs, at, place.core))
        self.own = 2 * x + t
        self.of_x = 2 * (1 - x) + t
        self.of_y = 2 * x + (1 - t)
        self.of_d = 2 * (1 - x) + (1 - t)
        self.low = remote(
            kept.at[self.of_d, pl.ds(0, half)], low_in, sends, recvs, 4, place.across_x
        )
        self.high = remote(
            kept.at[self.of_d, pl.ds(half, half)], high_in, sends, recvs, 5, place.across_y
        )
        self.to_x = remote(kept.at[self.of_x], x_in, sends, recvs, 6, place.across_x)
        self.to_y = remote(kept.at[self.of_y], y_in, sends, recvs, 7, place.across_y)

    def start(self):
        for copy in self.first:
            copy.start()

    def second(self):
        k = self.place.k
        for copy in self.first:
            copy.wait_recv()

        def add(at, carry):
            mine = self.parts[4 * (at // 2) + 2 * k + at % 2].astype(f32)
            self.kept[at] = (mine + self.came[at].astype(f32)).astype(bf16)
            return carry

        lax.fori_loop(0, 4, add, 0)
        self.low.start()
        self.high.start()

    def third(self):
        half = self.half
        self.low.wait_recv()
        low, high = pl.ds(0, half), pl.ds(half, half)
        self.kept[self.of_y, low] = (
            self.kept[self.of_y, low].astype(f32) + self.low_in[...].astype(f32)
        ).astype(bf16)
        self.to_y.start()
        self.high.wait_recv()
        self.kept[self.of_x, high] = (
            self.kept[self.of_x, high].astype(f32) + self.high_in[...].astype(f32)
        ).astype(bf16)
        self.to_x.start()

    def finish(self):
        self.to_x.wait_recv()
        self.to_y.wait_recv()

    def total(self, rows):
        return (
            self.kept[self.own, rows].astype(f32)
            + self.x_in[rows].astype(f32)
            + self.y_in[rows].astype(f32)
        )

    def drain(self):
        for copy in self.first + [self.low, self.high, self.to_x, self.to_y]:
            copy.wait_send()


class ChainReduce:
    def __init__(self, place, parts, slots, sums, sends, recvs):
        self.s = place.s
        self.parts, self.slots, self.sums = parts, slots, sums

        def copy(src, d, slot, dev):
            return pltpu.make_async_remote_copy(
                src_ref=src,
                dst_ref=slots.at[slot],
                send_sem=sends.at[d],
                recv_sem=recvs.at[slot],
                device_id=dev,
                device_id_type=pl.DeviceIdType.MESH,
            )

        right, left = place.along(1), place.along(-1)
        self.to_right = lambda src, d: copy(src.at[d], d, d, right)
        self.to_left = lambda src, d, k: copy(src.at[d], d, 4 if k == 1 else d, left)

    def step(self, k):
        s = self.s

        def add(d):
            def one(at, carry):
                self.sums[d, at] = (
                    self.parts[d, at].astype(f32) + self.slots[d, at].astype(f32)
                ).astype(bf16)
                return carry

            lax.fori_loop(0, self.parts.shape[1], one, 0)

        @pl.when(s == 0)
        def _():
            self.to_right(self.parts, s + k).start()

        @pl.when(s == 3)
        def _():
            self.to_left(self.parts, s - k, k).start()

        if k < 3:

            @pl.when((s > 0) & (s + k <= 3))
            def _():
                self.to_right(self.parts, s + k).wait_recv()
                add(s + k)
                self.to_right(self.sums, s + k).start()

            @pl.when((s < 3) & (s - k >= 0))
            def _():
                self.to_left(self.parts, s - k, 2).wait_recv()
                add(s - k)
                self.to_left(self.sums, s - k, k).start()

    def finish(self, out):
        s = self.s

        @pl.when(s > 0)
        def _():
            self.to_right(self.parts, s).wait_recv()

        @pl.when(s < 3)
        def _():
            self.to_left(self.parts, s, 1).wait_recv()


        def one(at, carry):
            out[at] = self.parts[s, at]

            @pl.when(s > 0)
            def _():
                out[at] = (out[at].astype(f32) + self.slots[s, at].astype(f32)).astype(bf16)

            @pl.when(s < 3)
            def _():
                out[at] = (out[at].astype(f32) + self.slots[4, at].astype(f32)).astype(bf16)

            return carry

        lax.fori_loop(0, self.parts.shape[1], one, 0)

    def drain(self):
        s = self.s
        for k in (3, 2, 1):

            @pl.when(s + k <= 3)
            def _():
                self.to_right(self.parts, s + k).wait_send()

            @pl.when(s - k >= 0)
            def _():
                self.to_left(self.parts, s - k, k).wait_send()


def reduce_kernel(
    po, ps, ga, gm, vec, x_own, dy_own, small,
    output, grad_in, g_qkv, g_out_t, g_up, g_down_t, vec_sum,
    po_came, po_kept, po_low, po_high, po_x, po_y,
    ps_came, ps_kept, ps_low, ps_high, ps_x, ps_y,
    ga_slots, ga_sums, ga_total, ga_back, gm_slots, gm_sums, gm_total, gm_back, slots,
    po_send, po_recv, ps_send, ps_recv, ga_send, ga_recv, gm_send, gm_recv,
    sa_send, sa_recv, sm_send, sm_recv, cube_send, cube_recv, local,
):
    place = Place()
    vec_sum[...] = vec[...]
    place.meet()
    cube = CubeSum(place, vec_sum, slots, cube_send, cube_recv)
    outs = PlaneReduce(
        place, po, po_came, po_kept, po_low, po_high, po_x, po_y, po_send, po_recv
    )
    scaled = PlaneReduce(
        place, ps, ps_came, ps_kept, ps_low, ps_high, ps_x, ps_y, ps_send, ps_recv
    )
    chain_a = ChainReduce(place, ga, ga_slots, ga_sums, ga_send, ga_recv)
    chain_m = ChainReduce(place, gm, gm_slots, gm_sums, gm_send, gm_recv)
    swap_a = CtxSwap(place, ga_total, ga_back, sa_send, sa_recv, local.at[0])
    swap_m = CtxSwap(place, gm_total, gm_back, sm_send, sm_recv, local.at[1])
    cube.start(0)
    chain_a.step(3)
    chain_m.step(3)
    outs.start()
    scaled.start()
    cube.finish(0)
    cube.start(1)
    outs.second()
    scaled.second()
    chain_a.step(2)
    chain_m.step(2)
    cube.finish(1)
    cube.start(2)
    outs.third()
    scaled.third()
    chain_a.step(1)
    cube.finish(2)
    cube.start(3)
    chain_a.finish(ga_total)
    swap_a.start()
    chain_m.step(1)
    outs.finish()
    scaled.finish()
    cube.finish(3)
    cube.start(4)
    rows = 32

    def final(at, carry):
        here = pl.ds(pl.multiple_of(at * rows, rows), rows)
        values = x_own[here].astype(f32)
        normed, inv = layer_norm_parts(values)
        bias = small[4:5] + small[5:6]
        output[here] = (values + outs.total(here) + bias).astype(bf16)
        part = scaled.total(here)
        inner = jnp.mean(part, -1, keepdims=True)
        aligned = jnp.mean(part * normed, -1, keepdims=True)
        grad_in[here] = dy_own[here].astype(f32) + inv * (part - inner - normed * aligned)
        return carry

    lax.fori_loop(0, x_own.shape[0] // rows, final, 0)
    cube.finish(4)
    chain_m.finish(gm_total)
    swap_m.start()
    swap_a.finish()
    lanes = ga.shape[3] // 4
    for at in range(4):
        cols = slice(at * lanes, (at + 1) * lanes)
        for j in range(3):
            g_qkv[j, :, cols] = ga_back[at, :, j * lanes : (j + 1) * lanes].astype(f32)
        g_out_t[:, cols] = ga_back[at, :, 3 * lanes :].astype(f32)
    swap_m.finish()
    units = gm.shape[3] // 2
    for at in range(4):
        cols = slice(at * units, (at + 1) * units)
        g_up[:, cols] = gm_back[at, :, :units].astype(f32)
        g_down_t[:, cols] = gm_back[at, :, units:].astype(f32)
    for part in (outs, scaled, chain_a, chain_m, swap_a, swap_m):
        part.drain()


def reduce_all(po, ps, ga, gm, vec, x_own, dy_own, small):
    rows, model = x_own.shape
    depth, wide_a = ga.shape[2:]
    wide_m = gm.shape[3]
    vmem = pl.BlockSpec(memory_space=pltpu.VMEM)
    dma = pltpu.SemaphoreType.DMA
    half = (rows // 2, model)
    plane = [
        pltpu.VMEM((4, rows, model), bf16),
        pltpu.VMEM((4, rows, model), bf16),
        pltpu.VMEM(half, bf16),
        pltpu.VMEM(half, bf16),
        pltpu.VMEM((rows, model), bf16),
        pltpu.VMEM((rows, model), bf16),
    ]

    def chain(wide):
        return [
            pltpu.VMEM((5, 4, depth, wide), bf16),
            pltpu.VMEM((4, 4, depth, wide), bf16),
            pltpu.VMEM((4, depth, wide), bf16),
            pltpu.VMEM((4, depth, wide), bf16),
        ]

    return pl.pallas_call(
        reduce_kernel,
        out_shape=(
            jax.ShapeDtypeStruct((rows, model), bf16),
            jax.ShapeDtypeStruct((rows, model), f32),
            jax.ShapeDtypeStruct((3, depth, wide_a), f32),
            jax.ShapeDtypeStruct((depth, wide_a), f32),
            jax.ShapeDtypeStruct((depth, 2 * wide_m), f32),
            jax.ShapeDtypeStruct((depth, 2 * wide_m), f32),
            jax.ShapeDtypeStruct(vec.shape, f32),
        ),
        in_specs=[vmem] * 8,
        out_specs=[vmem] * 7,
        scratch_shapes=plane
        + plane
        + chain(wide_a)
        + chain(wide_m)
        + [pltpu.VMEM((5,) + vec.shape, f32)]
        + [dma((8,))] * 4
        + [dma((4,)), dma((5,))] * 2
        + [dma((3,))] * 4
        + [dma((5,))] * 2
        + [dma((2,))],
        compiler_params=pltpu.CompilerParams(
            collective_id=1, has_side_effects=True, vmem_limit_bytes=52 << 20
        ),
    )(po, ps, ga, gm, vec, x_own, dy_own, small)


def rotary_lanes(seq_len, lanes):
    half = ROT // 2
    inverse = rope_base ** (-np.arange(half) / half)
    angles = np.arange(seq_len)[:, None] * inverse[None, :]
    plain = np.zeros((seq_len, HD - ROT))
    cosine = np.concatenate([np.cos(angles), np.cos(angles), plain + 1], 1)
    sine = np.concatenate([-np.sin(angles), np.sin(angles), plain], 1)
    heads = lanes // HD
    return (
        jnp.asarray(np.tile(cosine, (1, heads)), f32),
        jnp.asarray(np.tile(sine, (1, heads)), f32),
    )


def turn_lanes(value, cosine, sine):
    lane = lax.broadcasted_iota(jnp.int32, value.shape, 1) % HD
    half = ROT // 2
    swapped = jnp.where(lane < half, jnp.roll(value, -half, 1), jnp.roll(value, half, 1))
    return value * cosine + swapped * sine


def per_device_plane(
    inputs, ln1_gain, ln1_bias, ln2_gain, ln2_bias, w_qkv, b_qkv, w_out, b_out,
    w_up, b_up, w_down, b_down, cotangent,
):
    s, c, t = (lax.axis_index(name) for name in ("shard", "ctx", "tensor"))
    n_ctx = 4
    group = 4 * s + c
    depth = w_up.shape[0]
    width = w_qkv.shape[2]
    units = w_up.shape[1]
    lanes, cols = width // n_ctx, units // n_ctx
    x_own, dy_own = inputs[0], cotangent[0]
    rows, model = x_own.shape
    seq_len = rows * 8

    six = jnp.stack([ln1_gain, ln1_bias, ln2_gain, ln2_bias, b_out, b_down]).astype(f32)
    slot = jnp.arange(32)[None, :, None]
    six = jnp.where(slot == 2 * group + t, six[:, None, :], 0.0).reshape(6, model)
    three = jnp.where(slot == 16 * t + group, b_qkv.astype(f32), 0.0).reshape(3, model)
    four = jnp.where(slot == 16 * t + group, b_up.astype(f32)[:, None, :], 0.0)
    four = four.reshape(-1, model)
    small_own = jnp.concatenate([six, three, four, jnp.zeros((3, model), f32)])

    first = jnp.concatenate([w_qkv, w_out.T[None]]).reshape(4, depth, n_ctx, lanes)
    first = first.transpose(2, 1, 0, 3).reshape(n_ctx, depth, 4 * lanes)
    second = jnp.stack([w_up, w_down.T]).reshape(2, depth, n_ctx, cols)
    second = second.transpose(2, 1, 0, 3).reshape(n_ctx, depth, 2 * cols)
    x_all, dy_all, first, second, small = gather_all(x_own, dy_own, first, second, small_own)

    gain_one, shift_one, gain_two, shift_two = (small[at] for at in range(4))
    bias_qkv = lax.dynamic_slice(small, (6, width * t + lanes * c), (3, lanes)).reshape(-1)
    bias_up = lax.dynamic_slice(small[9:13].reshape(-1), (units * t + cols * c,), (cols,))
    first = first.reshape(model, 4 * lanes)
    second = second.reshape(model, 2 * cols)
    dy = dy_all.reshape(seq_len, model)
    normed, _ = layer_norm_parts(x_all.reshape(seq_len, model).astype(f32))
    first_norm = (normed * gain_one + shift_one).astype(bf16)
    second_norm = (normed * gain_two + shift_two).astype(bf16)

    cosine, sine = rotary_lanes(seq_len, lanes)
    projected = jnp.dot(first_norm, first[:, : 3 * lanes], preferred_element_type=f32) + bias_qkv
    queries = turn_lanes(projected[:, :lanes], cosine, sine).astype(bf16)
    keys = turn_lanes(projected[:, lanes : 2 * lanes], cosine, sine).astype(bf16)
    values = projected[:, 2 * lanes :].astype(bf16)
    grad_mixed = jnp.dot(dy, first[:, 3 * lanes :], preferred_element_type=f32).astype(bf16)
    attended = attend(jnp.concatenate([queries, keys, values, grad_mixed], 1))
    mixed = attended[:, :lanes]
    grad_projected = jnp.concatenate(
        [
            turn_lanes(attended[:, lanes : 2 * lanes].astype(f32), cosine, -sine).astype(bf16),
            turn_lanes(attended[:, 2 * lanes : 3 * lanes].astype(f32), cosine, -sine).astype(bf16),
            attended[:, 3 * lanes :],
        ],
        1,
    )
    up, down_t = second[:, :cols], second[:, cols:]
    hidden_pre = jnp.dot(second_norm, up, preferred_element_type=f32) + bias_up
    hidden = jax.nn.gelu(hidden_pre, approximate=False).astype(bf16)
    grad_hidden = jnp.dot(dy, down_t, preferred_element_type=f32)
    grad_pre = (grad_hidden * gelu_slope(hidden_pre)).astype(bf16)
    grad_second = contract_last(grad_pre, up)
    grad_first = contract_last(grad_projected, first[:, : 3 * lanes])
    po = contract_last(mixed, first[:, 3 * lanes :]) + contract_last(hidden, down_t)
    ps = grad_first * gain_one + grad_second * gain_two
    ga = jnp.concatenate(
        [contract_first(first_norm, grad_projected), contract_first(dy, mixed)], 1
    ).astype(bf16)
    gm = jnp.concatenate(
        [contract_first(second_norm, grad_pre), contract_first(dy, hidden)], 1
    ).astype(bf16)
    slot = jnp.arange(8)[None, :, None]
    b_qkv_part = jnp.sum(grad_projected, 0, dtype=f32).reshape(3, 1, lanes)
    b_qkv_part = jnp.where(slot == 4 * t + c, b_qkv_part, 0.0).reshape(3, model)
    b_up_part = jnp.sum(grad_pre, 0, dtype=f32).reshape(1, 1, cols)
    b_up_part = jnp.where(slot == 4 * t + c, b_up_part, 0.0).reshape(-1, model)
    vec = jnp.stack(
        [
            jnp.sum(grad_first * normed, 0),
            jnp.sum(grad_first, 0),
            jnp.sum(grad_second * normed, 0),
            jnp.sum(grad_second, 0),
            jnp.sum(dy_own.astype(f32), 0),
        ]
    )
    vec = jnp.concatenate([vec, b_qkv_part, b_up_part, jnp.zeros((4, model), f32)])
    output, grad_in, g_qkv, g_out_t, g_up, g_down_t, vec = reduce_all(
        po.astype(bf16).reshape(8, rows, model),
        ps.astype(bf16).reshape(8, rows, model),
        ga.reshape(4, n_ctx, depth, 4 * lanes),
        gm.reshape(4, n_ctx, depth, 2 * cols),
        vec,
        x_own,
        dy_own,
        small,
    )
    piece = model // 32
    five = lax.dynamic_slice(vec, (0, (2 * group + t) * piece), (5, piece))
    out_b_qkv = lax.dynamic_slice(vec, (5, width * t + piece * group), (3, piece))
    part = units // 16
    out_b_up = lax.dynamic_slice(vec[8:12].reshape(-1), (units * t + part * group,), (part,))
    return (
        output[None],
        grad_in[None],
        five[0],
        five[1],
        five[2],
        five[3],
        g_qkv,
        out_b_qkv[:, None],
        g_out_t.T,
        five[4],
        g_up,
        out_b_up[None],
        g_down_t.T,
        five[4],
    )


def fits_plane(mesh):
    return tuple(mesh.shape[name] for name in ("shard", "ctx", "tensor")) == (4, 4, 2)


def solution(mesh):
    placed = (
        P("shard", ("ctx", "tensor"), None),
        P(("shard", "ctx", "tensor")),
        P(("shard", "ctx", "tensor")),
        P(("shard", "ctx", "tensor")),
        P(("shard", "ctx", "tensor")),
        P(None, ("shard", "ctx"), "tensor"),
        P(None, "tensor", ("shard", "ctx")),
        P("tensor", ("shard", "ctx")),
        P(("shard", "ctx", "tensor")),
        P(("shard", "ctx"), "tensor"),
        P("tensor", ("shard", "ctx")),
        P("tensor", ("shard", "ctx")),
        P(("shard", "ctx", "tensor")),
        P("shard", ("ctx", "tensor"), None),
    )
    return jax.shard_map(
        per_device_plane if fits_plane(mesh) else per_device,
        mesh=mesh,
        in_specs=placed,
        out_specs=(
            P("shard", ("ctx", "tensor"), None),
            P("shard", ("ctx", "tensor"), None),
            P(("shard", "ctx", "tensor")),
            P(("shard", "ctx", "tensor")),
            P(("shard", "ctx", "tensor")),
            P(("shard", "ctx", "tensor")),
            P(None, ("shard", "ctx"), "tensor"),
            P(None, "tensor", ("shard", "ctx")),
            P("tensor", ("shard", "ctx")),
            P(("shard", "ctx", "tensor")),
            P(("shard", "ctx"), "tensor"),
            P("tensor", ("shard", "ctx")),
            P("tensor", ("shard", "ctx")),
            P(("shard", "ctx", "tensor")),
        ),
        check_vma=False,
    )
```

```python
import functools

import jax
import jax.numpy as jnp
import numpy as np
from jax import lax
from jax.experimental import pallas as pl
from jax.experimental.pallas import tpu as pltpu
from jax.sharding import PartitionSpec as P

HD = 64
ROT = 16


norm_eps = 1e-05
rope_base = 10000.0
bf16 = jnp.bfloat16
f32 = jnp.float32
GROUP = ("shard", "ctx")


def layer_norm_parts(values):
    centre = values - jnp.mean(values, -1, keepdims=True)
    spread = jnp.mean(centre * centre, -1, keepdims=True)
    inv_std = lax.rsqrt(spread + norm_eps)
    return (centre * inv_std, inv_std)


def rotary_tables(positions):
    half_dims = ROT // 2
    ladder = jnp.arange(half_dims, dtype=f32)
    inverse = jnp.exp(ladder * (-2.0 / ROT) * jnp.log(f32(rope_base)))
    angles = positions.astype(f32)[:, None] * inverse[None, :]
    angles = jnp.concatenate([angles, angles], -1)
    return (jnp.cos(angles)[:, None, :], jnp.sin(angles)[:, None, :])


def rotate(values, cosine, sine_table):
    rot_dims = cosine.shape[-1]
    half_dims = rot_dims // 2
    turned = values[..., :rot_dims]
    swapped = jnp.concatenate([-turned[..., half_dims:], turned[..., :half_dims]], -1)
    return jnp.concatenate([turned * cosine + swapped * sine_table, values[..., rot_dims:]], -1)


def gelu_slope(values):
    return (
        0.5 * (1.0 + lax.erf(values * 0.7071067811865476))
        + values * jnp.exp(-0.5 * values * values) * 0.3989422804014327
    )


def contract_last(left_side, right_side):
    return lax.dot_general(
        left_side, right_side, (((1,), (1,)), ((), ())), preferred_element_type=f32
    )


def contract_first(left_side, right_side):
    return lax.dot_general(
        left_side, right_side, (((0,), (0,)), ((), ())), preferred_element_type=f32
    )


def attention_kernel(lanes, wide, rows, in_ref, out_ref, key_grad, value_grad):
    seq_len = in_ref.shape[0]
    heads = lanes // HD
    parts = wide // rows
    scale = HD ** (-0.5)
    key_grad[...] = jnp.zeros_like(key_grad)
    value_grad[...] = jnp.zeros_like(value_grad)
    out_ref[...] = jnp.zeros_like(out_ref)
    for step in range(seq_len // wide):
        length = (step + 1) * wide

        def one_block(turn, carry, step=step, length=length):
            head = turn % heads
            start = pl.multiple_of(step * wide + (turn // heads) * rows, rows)
            here = pl.ds(start, rows)
            mine = lax.broadcasted_iota(jnp.int32, (rows, lanes), 1) // HD == head
            queries = in_ref[here, 0:lanes].astype(f32) * scale
            queries = jnp.where(mine, queries, 0.0).astype(bf16)
            grads = in_ref[here, 3 * lanes : 4 * lanes].astype(f32)
            grads = jnp.where(mine, grads, 0.0).astype(bf16)
            keys = in_ref[0:length, lanes : 2 * lanes]
            values = in_ref[0:length, 2 * lanes : 3 * lanes]
            scores = contract_last(queries, keys)
            key_at = lax.broadcasted_iota(jnp.int32, scores.shape, 1)
            query_at = start + lax.broadcasted_iota(jnp.int32, scores.shape, 0)
            scores = jnp.where(key_at <= query_at, scores, -1e30)
            exp_scores = jnp.exp(scores - jnp.max(scores, -1, keepdims=True))
            probs = exp_scores * (1.0 / jnp.sum(exp_scores, -1, keepdims=True))
            attn_prob = probs.astype(bf16)
            mixed = jnp.dot(attn_prob, values, preferred_element_type=f32)
            value_grad[0:length, :] += contract_first(attn_prob, grads)
            prob_grad = contract_last(grads, values)
            inner_sum = jnp.sum(probs * prob_grad, -1, keepdims=True)
            score_grad = (probs * (prob_grad - inner_sum)).astype(bf16)
            query_grad = jnp.dot(score_grad, keys, preferred_element_type=f32) * scale
            key_grad[0:length, :] += contract_first(score_grad, queries)
            out_ref[here, 0:lanes] = jnp.where(
                mine, mixed, out_ref[here, 0:lanes].astype(f32)
            ).astype(bf16)
            out_ref[here, lanes : 2 * lanes] = jnp.where(
                mine, query_grad, out_ref[here, lanes : 2 * lanes].astype(f32)
            ).astype(bf16)
            return carry

        lax.fori_loop(0, parts * heads, one_block, 0)
    out_ref[:, 2 * lanes : 3 * lanes] = key_grad[...].astype(bf16)
    out_ref[:, 3 * lanes : 4 * lanes] = value_grad[...].astype(bf16)


def attend(packed):
    seq_len, width = packed.shape
    lanes = width // 4
    wide = min(512, seq_len)
    rows = min(256, wide)
    return pl.pallas_call(
        functools.partial(attention_kernel, lanes, wide, rows),
        out_shape=jax.ShapeDtypeStruct((seq_len, width), bf16),
        in_specs=[pl.BlockSpec(memory_space=pltpu.VMEM)],
        out_specs=pl.BlockSpec(memory_space=pltpu.VMEM),
        scratch_shapes=[pltpu.VMEM((seq_len, lanes), f32), pltpu.VMEM((seq_len, lanes), f32)],
        compiler_params=pltpu.CompilerParams(vmem_limit_bytes=48 << 20),
        cost_estimate=pl.CostEstimate(
            flops=14 * seq_len * seq_len * lanes,
            bytes_accessed=4 * seq_len * width,
            transcendentals=seq_len * seq_len * lanes // HD,
        ),
    )(packed)


def per_device(
    inputs,
    ln1_gain,
    ln1_bias,
    ln2_gain,
    ln2_bias,
    w_qkv,
    b_qkv,
    w_out,
    b_out,
    w_up,
    b_up,
    w_down,
    b_down,
    cotangent,
):
    pair = lax.axis_index("tensor")
    first = pair == 0
    n_ctx = lax.axis_size("ctx")
    n_group = lax.axis_size("shard") * n_ctx
    swap = ((0, 1), (1, 0))

    def exchange(value):
        return lax.ppermute(value, "tensor", swap)

    def in_order(own, other, axis):
        return jnp.where(
            first,
            jnp.concatenate([own, other], axis),
            jnp.concatenate([other, own], axis),
        )

    small_own = jnp.stack([ln1_gain, ln1_bias, ln2_gain, ln2_bias, b_out, b_down])
    small = in_order(small_own, exchange(small_own), 1)
    piece = small.shape[1]
    depth = w_up.shape[0]
    ff_group = w_up.shape[1]
    width = w_qkv.shape[2]
    riders = jnp.concatenate([small.reshape(-1), b_qkv.reshape(-1), b_up.reshape(-1)])
    room = depth * 128
    riders = jnp.pad(riders, (0, room - riders.shape[0])).reshape(depth, 128)
    first_pack = jnp.concatenate([w_qkv[0], w_qkv[1], w_qkv[2], w_out.T, riders], 1)
    second_pack = jnp.concatenate([w_up, w_down.T], 1)
    first_whole = lax.all_gather(first_pack, GROUP, axis=0, tiled=True)
    second_whole = lax.all_gather(second_pack, GROUP, axis=0, tiled=True)
    model = first_whole.shape[0]
    whole_qkv = first_whole[:, : 3 * width]
    whole_out_t = first_whole[:, 3 * width : 4 * width]
    gathered = first_whole[:, 4 * width :].reshape(n_group, room).astype(f32)
    whole_up = second_whole[:, :ff_group]
    whole_down_t = second_whole[:, ff_group:]

    gain_one, shift_one, gain_two, shift_two, bias_out, bias_down = [
        gathered[:, at * piece : (at + 1) * piece].reshape(-1) for at in range(6)
    ]
    at = 6 * piece
    part = b_qkv.shape[2]
    bias_qkv = jnp.concatenate(
        [gathered[:, at + j * part : at + (j + 1) * part].reshape(-1) for j in range(3)]
    )
    at = at + 3 * part
    up_part = b_up.shape[1]
    bias_up = gathered[:, at : at + up_part].reshape(-1)

    both_own = jnp.concatenate([inputs, cotangent], 0)
    both = in_order(both_own, exchange(both_own), 1)
    grad_own = cotangent[0]
    own_rows = inputs[0].astype(f32)
    normed_own, inv_own = layer_norm_parts(own_rows)
    normed, _ = layer_norm_parts(both[0].astype(f32))
    grad_rows = both[1]
    first_norm = (normed * gain_one + shift_one).astype(bf16)
    second_norm = (normed * gain_two + shift_two).astype(bf16)
    block_len = first_norm.shape[0]
    half = block_len // 2

    def own_half(value):
        return jnp.where(first, value[:half], value[half:])

    def other_half(value):
        return jnp.where(first, value[half:], value[:half])

    positions = lax.axis_index("ctx") * block_len + jnp.arange(block_len, dtype=jnp.int32)
    cosine, sine_table = rotary_tables(positions)
    projected = jnp.dot(first_norm, whole_qkv, preferred_element_type=f32) + bias_qkv
    heads = width // HD

    def turned(value, sine):
        return (
            rotate(value.astype(f32).reshape(block_len, heads, HD), cosine, sine)
            .astype(bf16)
            .reshape(block_len, width)
        )

    queries = turned(projected[:, :width], sine_table)
    key_rows = turned(projected[:, width : 2 * width], sine_table)
    value_rows = projected[:, 2 * width :].astype(bf16)
    grad_mixed = jnp.dot(grad_rows, whole_out_t, preferred_element_type=f32).astype(bf16)
    lanes = width // n_ctx
    packed = jnp.stack([queries, key_rows, value_rows, grad_mixed])
    packed = packed.reshape(4, block_len, n_ctx, lanes).transpose(2, 1, 0, 3)
    packed = packed.reshape(n_ctx, block_len, 4 * lanes)
    there = lax.all_to_all(packed, "ctx", split_axis=0, concat_axis=0, tiled=True)

    hidden_pre = jnp.dot(second_norm, whole_up, preferred_element_type=f32) + bias_up
    hidden = jax.nn.gelu(hidden_pre, approximate=False).astype(bf16)
    feed_out = contract_last(hidden, whole_down_t)
    grad_hidden = jnp.dot(grad_rows, whole_down_t, preferred_element_type=f32)
    grad_pre = (grad_hidden * gelu_slope(hidden_pre)).astype(bf16)
    grad_up = contract_first(second_norm, grad_pre).astype(bf16)
    grad_down_t = contract_first(grad_rows, hidden).astype(bf16)
    second_grads = jnp.concatenate([grad_up, grad_down_t], 1)
    there, second_grads = lax.optimization_barrier((there, second_grads))
    second_sum = lax.psum_scatter(second_grads, GROUP, scatter_dimension=0, tiled=True)
    grad_b_up = jnp.sum(grad_pre, 0, dtype=f32)
    grad_second = contract_last(grad_pre, whole_up)

    attended = attend(there.reshape(n_ctx * block_len, 4 * lanes))
    back = lax.all_to_all(
        attended.reshape(n_ctx, block_len, 4 * lanes),
        "ctx",
        split_axis=0,
        concat_axis=0,
        tiled=True,
    )
    back = back.reshape(n_ctx, block_len, 4, lanes).transpose(2, 1, 0, 3)
    mixed_rows, query_back, key_back, value_back = back.reshape(4, block_len, width)
    grad_projected = jnp.concatenate(
        [turned(query_back, -sine_table), turned(key_back, -sine_table), value_back], 1
    )
    grad_qkv = contract_first(first_norm, grad_projected).astype(bf16)
    grad_out_t = contract_first(grad_rows, mixed_rows).astype(bf16)
    grad_b_qkv = jnp.sum(grad_projected, 0, dtype=f32)
    grad_first = contract_last(grad_projected, whole_qkv)

    vectors = jnp.stack(
        [
            jnp.sum(grad_first * normed, 0),
            jnp.sum(grad_first, 0),
            jnp.sum(grad_second * normed, 0),
            jnp.sum(grad_second, 0),
            jnp.sum(grad_own.astype(f32), 0),
        ]
    )
    back_riders = jnp.concatenate(
        [
            vectors.reshape(5, n_group, piece).transpose(1, 0, 2).reshape(n_group, -1),
            grad_b_qkv.reshape(3, n_group, part).transpose(1, 0, 2).reshape(n_group, -1),
            grad_b_up.reshape(n_group, up_part),
        ],
        1,
    )
    back_riders = jnp.pad(back_riders, ((0, 0), (0, room - back_riders.shape[1])))
    back_riders = back_riders.reshape(model, 128).astype(bf16)
    first_grads = jnp.concatenate([grad_qkv, grad_out_t, back_riders], 1)
    first_grads, second_sum = lax.optimization_barrier((first_grads, second_sum))
    first_sum = lax.psum_scatter(first_grads, GROUP, scatter_dimension=0, tiled=True)

    partial_sum = contract_last(mixed_rows, whole_out_t) + feed_out
    branches = own_half(partial_sum) + exchange(other_half(partial_sum).astype(bf16)).astype(f32)
    output = (own_rows + branches + bias_out + bias_down).astype(bf16)
    scaled = grad_first * gain_one + grad_second * gain_two
    scaled = own_half(scaled) + exchange(other_half(scaled).astype(bf16)).astype(f32)
    inner_sum = jnp.mean(scaled, -1, keepdims=True)
    aligned = jnp.mean(scaled * normed_own, -1, keepdims=True)
    grad_input = grad_own.astype(f32) + inv_own * (scaled - inner_sum - normed_own * aligned)

    second_sum = second_sum.astype(f32)
    first_sum = first_sum.astype(f32)
    grad_w_qkv = first_sum[:, : 3 * width].reshape(depth, 3, width).transpose(1, 0, 2)
    grad_w_out = first_sum[:, 3 * width : 4 * width].T
    summed = first_sum[:, 4 * width :].reshape(-1)
    vector_sum = summed[: 5 * piece].reshape(5, piece)
    own = piece // 2
    mine = jnp.where(first, vector_sum[:, :own], vector_sum[:, own:])
    theirs = jnp.where(first, vector_sum[:, own:], vector_sum[:, :own])
    vector_grads = mine + exchange(theirs)
    at = 5 * piece
    out_b_qkv = summed[at : at + 3 * part].reshape(3, 1, part)
    at = at + 3 * part
    out_b_up = summed[at : at + up_part].reshape(1, up_part)
    return (
        output[None],
        grad_input[None],
        vector_grads[0],
        vector_grads[1],
        vector_grads[2],
        vector_grads[3],
        grad_w_qkv,
        out_b_qkv,
        grad_w_out,
        vector_grads[4],
        second_sum[:, :ff_group],
        out_b_up,
        second_sum[:, ff_group:].T,
        vector_grads[4],
    )

def remote(src, dst, sends, recvs, at, to):
    return pltpu.make_async_remote_copy(
        src_ref=src,
        dst_ref=dst,
        send_sem=sends.at[at],
        recv_sem=recvs.at[at],
        device_id=to,
        device_id_type=pl.DeviceIdType.MESH,
    )


class Place:
    def __init__(self):
        self.s = lax.axis_index("shard")
        self.c = lax.axis_index("ctx")
        self.t = lax.axis_index("tensor")
        self.x = self.c // 2
        self.k = self.c % 2
        self.block = 2 * self.c + self.t
        self.core_c = 2 * self.x + (1 - self.k)
        self.x_c = 2 * (1 - self.x) + self.k
        self.far_c = 2 * (1 - self.x) + (1 - self.k)
        self.y_t = 1 - self.t
        self.core = {"ctx": self.core_c}
        self.across_x = {"ctx": self.x_c}
        self.far = {"ctx": self.far_c}
        self.across_y = {"tensor": self.y_t}

    def along(self, step):
        return {"shard": lax.rem(self.s + step + 4, 4)}

    def meet(self):
        barrier = pltpu.get_barrier_semaphore()
        others = [self.core, self.across_x, self.far, self.across_y]
        others += [self.along(step) for step in (1, 2, 3)]
        for other in others:
            pl.semaphore_signal(
                barrier, inc=1, device_id=other, device_id_type=pl.DeviceIdType.MESH
            )
        pl.semaphore_wait(barrier, len(others))

    def cube(self):
        pair = self.s + 1 - 2 * lax.rem(self.s, 2)
        return [
            self.core,
            {"shard": pair},
            self.along(2),
            self.across_x,
            self.across_y,
        ]


class PlaneGather:
    def __init__(self, place, own, full, sends, recvs, local):
        half = own.shape[0] // 2
        b = place.block
        xb = 2 * place.x_c + place.t
        yb = 2 * place.c + place.y_t
        db = 2 * place.x_c + place.y_t
        low, high = pl.ds(0, half), pl.ds(half, half)

        def to(src, dst, at, dev):
            return remote(src, dst, sends, recvs, at, dev)

        self.local = pltpu.make_async_copy(own, full.at[b], local)
        self.to_x = to(own, full.at[b], 0, place.across_x)
        self.to_y = to(own, full.at[b], 1, place.across_y)
        self.low_y = to(full.at[xb, low], full.at[xb, low], 2, place.across_y)
        self.high_x = to(full.at[yb, high], full.at[yb, high], 3, place.across_x)
        self.core_own = to(own, full.at[b], 4, place.core)
        self.core_x = to(full.at[xb], full.at[xb], 5, place.core)
        self.core_y = to(full.at[yb], full.at[yb], 6, place.core)
        self.core_d = to(full.at[db], full.at[db], 7, place.core)
        self.all = [
            self.to_x, self.to_y, self.low_y, self.high_x,
            self.core_own, self.core_x, self.core_y, self.core_d,
        ]

    def start(self):
        self.to_x.start()
        self.to_y.start()
        self.core_own.start()
        self.local.start()

    def second(self):
        self.to_x.wait_recv()
        self.low_y.start()
        self.core_x.start()
        self.to_y.wait_recv()
        self.high_x.start()
        self.core_y.start()

    def third(self):
        self.low_y.wait_recv()
        self.high_x.wait_recv()
        self.core_d.start()

    def finish(self):
        self.local.wait()
        for copy in (self.core_own, self.core_x, self.core_y, self.core_d):
            copy.wait_recv()

    def drain(self):
        for copy in self.all:
            copy.wait_send()


class CtxSwap:
    def __init__(self, place, own, dst, sends, recvs, local):
        c = place.c
        self.copies = []
        for at, (peer, dev) in enumerate(
            ((place.core_c, place.core), (place.x_c, place.across_x), (place.far_c, place.far))
        ):
            self.copies.append(remote(own.at[peer], dst.at[c], sends, recvs, at, dev))
        self.local = pltpu.make_async_copy(own.at[c], dst.at[c], local)

    def start(self):
        for copy in self.copies:
            copy.start()
        self.local.start()

    def finish(self):
        for copy in self.copies:
            copy.wait_recv()
        self.local.wait()

    def drain(self):
        for copy in self.copies:
            copy.wait_send()


class ChainGather:
    def __init__(self, place, full, right, left, recvs):
        self.s = place.s
        s = place.s

        def copy(j, sends, dev):
            return pltpu.make_async_remote_copy(
                src_ref=full.at[j],
                dst_ref=full.at[j],
                send_sem=sends.at[j],
                recv_sem=recvs.at[j],
                device_id=dev,
                device_id_type=pl.DeviceIdType.MESH,
            )

        self.to_right = lambda j: copy(j, right, place.along(1))
        self.to_left = lambda j: copy(j, left, place.along(-1))

    def start(self):
        s = self.s

        @pl.when(s < 3)
        def _():
            self.to_right(s).start()

        @pl.when(s > 0)
        def _():
            self.to_left(s).start()

    def step(self, distance):
        s = self.s

        @pl.when(s >= distance)
        def _():
            self.to_right(s - distance).wait_recv()

            @pl.when(s < 3)
            def _():
                self.to_right(s - distance).start()

        @pl.when(s + distance <= 3)
        def _():
            self.to_left(s + distance).wait_recv()

            @pl.when(s > 0)
            def _():
                self.to_left(s + distance).start()

    def drain(self):
        s = self.s
        for distance in range(4):

            @pl.when((s >= distance) & (s < 3))
            def _():
                self.to_right(s - distance).wait_send()

            @pl.when((s + distance <= 3) & (s > 0))
            def _():
                self.to_left(s + distance).wait_send()


class CubeSum:
    def __init__(self, place, total, slots, sends, recvs):
        self.total, self.slots = total, slots
        self.copies = [
            remote(total, slots.at[at], sends, recvs, at, dev)
            for at, dev in enumerate(place.cube())
        ]

    def start(self, at):
        self.copies[at].start()

    def finish(self, at):
        self.copies[at].wait()
        self.total[...] += self.slots[at]


def half_mask(rows, lanes, head):
    lane = lax.broadcasted_iota(jnp.int32, (rows, lanes), 1)
    return (lane < HD) if head == 0 else (lane >= HD)


def stack_heads(value):
    rows, lanes = value.shape
    parts = [jnp.where(half_mask(rows, lanes, head), value, 0.0) for head in range(2)]
    return jnp.concatenate(parts, 0)


def join_heads(value):
    rows, lanes = value.shape[0] // 2, value.shape[1]
    return jnp.where(half_mask(rows, lanes, 0), value[:rows], value[rows:])


def turn_block(value, cosine, sine):
    lanes = value.shape[1]
    lane = lax.broadcasted_iota(jnp.int32, value.shape, 1) % HD
    half = ROT // 2
    up = pltpu.roll(value, lanes - half, 1)
    down = pltpu.roll(value, half, 1)
    return value * cosine + jnp.where(lane < half, up, down) * sine


def attention_rows(at, rows, q_all, k_all, v_all, g_all, scores, key_grad, value_grad):
    length = (at + 1) * rows
    here = pl.ds(at * rows, rows)
    seen = pl.ds(0, length)
    queries = stack_heads(q_all[here].astype(f32)).astype(bf16)
    scores[:, seen] = contract_last(queries, k_all[seen])
    edge = pl.ds(at * rows, rows)
    key_at = lax.broadcasted_iota(jnp.int32, (rows, rows), 1)
    query_at = lax.broadcasted_iota(jnp.int32, (rows, rows), 0)
    keep = key_at <= query_at
    for head in range(2):
        part = pl.ds(head * rows, rows)
        scores[part, edge] = jnp.where(keep, scores[part, edge], -1e30)
    top = jnp.max(scores[:, seen], -1, keepdims=True)
    weights = jnp.exp(scores[:, seen] - top)
    scores[:, seen] = weights
    inverse = 1.0 / jnp.sum(weights, -1, keepdims=True)
    low = weights.astype(bf16)
    mixed = jnp.dot(low, v_all[seen], preferred_element_type=f32) * inverse
    grads = (stack_heads(g_all[here].astype(f32)) * inverse).astype(bf16)
    inner = jnp.sum(grads.astype(f32) * mixed, -1, keepdims=True)
    value_grad[:, seen] += contract_first(grads, low)
    prob_grad = contract_last(grads, v_all[seen])
    score_grad = (scores[:, seen] * (prob_grad - inner)).astype(bf16)
    key_grad[:, seen] += contract_first(queries, score_grad)
    query_grad = jnp.dot(score_grad, k_all[seen], preferred_element_type=f32)
    return join_heads(mixed), join_heads(query_grad) * (HD ** (-0.5))


def gather_kernel(
    x_own, dy_own, wa_own, wm_own, small_own, cosine, sine,
    x_all, dy_all, wa_all, wm_all, small_all, mixed_all, grads_all, ga_all,
    slots, first_norm, q_all, k_all, v_all, g_all, scores, key_grad, value_grad, flipped,
    x_send, x_recv, dy_send, dy_recv, wa_send, wa_recv, wm_send, wm_recv,
    ca_right, ca_left, ca_recv, cm_right, cm_left, cm_recv, cube_send, cube_recv, local,
):
    place = Place()
    small_all[...] = small_own[...]
    place.meet()
    xs = PlaneGather(place, x_own, x_all, x_send, x_recv, local.at[0])
    dys = PlaneGather(place, dy_own, dy_all, dy_send, dy_recv, local.at[1])
    swap_a = CtxSwap(place, wa_own, wa_all.at[place.s], wa_send, wa_recv, local.at[2])
    swap_m = CtxSwap(place, wm_own, wm_all.at[place.s], wm_send, wm_recv, local.at[3])
    chain_a = ChainGather(place, wa_all, ca_right, ca_left, ca_recv)
    chain_m = ChainGather(place, wm_all, cm_right, cm_left, cm_recv)
    cube = CubeSum(place, small_all, slots, cube_send, cube_recv)
    blocks, rows, model = x_all.shape
    lanes = q_all.shape[1]
    width = 4 * lanes
    first = place.t * width + place.c * lanes
    first = pl.ds(pl.multiple_of(first, lanes), lanes)

    cube.start(0)
    swap_a.start()
    xs.start()
    swap_m.start()
    key_grad[...] = jnp.zeros_like(key_grad)
    value_grad[...] = jnp.zeros_like(value_grad)
    cube.finish(0)
    cube.start(1)
    cube.finish(1)
    cube.start(2)
    cube.finish(2)
    swap_a.finish()
    chain_a.start()
    cube.start(3)
    xs.second()
    dys.start()
    chain_a.step(1)
    swap_m.finish()
    chain_m.start()
    cube.finish(3)
    cube.start(4)
    chain_a.step(2)
    xs.third()
    cube.finish(4)
    xs.finish()

    def norm(at, carry):
        normed, _ = layer_norm_parts(x_all[at].astype(f32))
        first_norm[at] = (normed * small_all[0:1] + small_all[1:2]).astype(bf16)
        return carry

    lax.fori_loop(0, blocks, norm, 0)
    chain_a.step(3)

    def weights_of(j, count=1):
        return wa_all[:, :, :, j * lanes : (j + count) * lanes].reshape(model, count * lanes)

    def project(at, carry):
        here = pl.ds(pl.multiple_of(at * rows, rows), rows)
        both = jnp.dot(first_norm[at], weights_of(0, 3), preferred_element_type=f32)
        cos_here, sin_here = cosine[here], sine[here]
        parts = [both[:, j * lanes : (j + 1) * lanes] + small_all[6 + j : 7 + j, first] for j in range(3)]
        queries = turn_block(parts[0], cos_here, sin_here).astype(bf16)
        q_all[here] = (queries.astype(f32) * (HD ** (-0.5))).astype(bf16)
        k_all[here] = turn_block(parts[1], cos_here, sin_here).astype(bf16)
        v_all[here] = parts[2].astype(bf16)
        return carry

    lax.fori_loop(0, blocks, project, 0)
    dys.second()
    chain_m.step(1)
    dys.third()
    dys.finish()

    def back(at, carry):
        here = pl.ds(pl.multiple_of(at * rows, rows), rows)
        g_all[here] = jnp.dot(
            dy_all[at], weights_of(3), preferred_element_type=f32
        ).astype(bf16)
        return carry

    lax.fori_loop(0, blocks, back, 0)
    for at in range(blocks):
        here = pl.ds(at * rows, rows)
        mixed, query_grad = attention_rows(
            at, rows, q_all, k_all, v_all, g_all, scores, key_grad, value_grad
        )
        mixed_all[here] = mixed.astype(bf16)
        query_grad = query_grad.astype(bf16).astype(f32)
        query_grad = turn_block(query_grad, cosine[here], -sine[here])
        grads_all[here, 0:lanes] = query_grad.astype(bf16)
        flipped[0:lanes, here] = query_grad.T.astype(bf16)
        flipped[3 * lanes : 4 * lanes, here] = mixed.T.astype(bf16)
        if at == 4:
            chain_m.step(2)

    for at in range(blocks):
        here = pl.ds(at * rows, rows)
        turned = key_grad[:, here].T.astype(bf16).astype(f32)
        turned = turn_block(turned, cosine[here], -sine[here])
        grads_all[here, lanes : 2 * lanes] = turned.astype(bf16)
        flipped[lanes : 2 * lanes, here] = turned.T.astype(bf16)
        grads_all[here, 2 * lanes : 3 * lanes] = value_grad[:, here].T.astype(bf16)
        flipped[2 * lanes : 3 * lanes, here] = value_grad[:, here].astype(bf16)
    piece = model // 4
    for d in range(4):
        cols = slice(d * piece, (d + 1) * piece)
        normed = first_norm[:, :, cols].reshape(blocks * rows, piece)
        ga_all[d, 0 : 3 * lanes] = jnp.dot(
            flipped[0 : 3 * lanes], normed, preferred_element_type=f32
        ).astype(bf16)
        grads = dy_all[:, :, cols].reshape(blocks * rows, piece)
        ga_all[d, 3 * lanes :] = jnp.dot(
            flipped[3 * lanes :], grads, preferred_element_type=f32
        ).astype(bf16)
    chain_m.step(3)
    for part in (xs, dys, swap_a, swap_m, chain_a, chain_m):
        part.drain()


def gather_all(x_own, dy_own, wa_own, wm_own, small_own, cosine, sine):
    rows, model = x_own.shape
    n_ctx, depth, wide_a = wa_own.shape
    wide_m = wm_own.shape[2]
    seq_len, lanes = cosine.shape
    anywhere = pl.BlockSpec(memory_space=pl.ANY)
    vmem = pl.BlockSpec(memory_space=pltpu.VMEM)
    dma = pltpu.SemaphoreType.DMA
    return pl.pallas_call(
        gather_kernel,
        out_shape=(
            jax.ShapeDtypeStruct((8, rows, model), bf16),
            jax.ShapeDtypeStruct((8, rows, model), bf16),
            jax.ShapeDtypeStruct((4, n_ctx, depth, wide_a), bf16),
            jax.ShapeDtypeStruct((4, n_ctx, depth, wide_m), bf16),
            jax.ShapeDtypeStruct(small_own.shape, f32),
            jax.ShapeDtypeStruct((seq_len, lanes), bf16),
            jax.ShapeDtypeStruct((seq_len, 3 * lanes), bf16),
            jax.ShapeDtypeStruct((4, wide_a, model // 4), bf16),
        ),
        in_specs=[anywhere] * 4 + [vmem] * 3,
        out_specs=[vmem] * 3 + [anywhere] + [vmem] * 4,
        scratch_shapes=[
            pltpu.VMEM((5,) + small_own.shape, f32),
            pltpu.VMEM((8, rows, model), bf16),
            pltpu.VMEM((seq_len, lanes), bf16),
            pltpu.VMEM((seq_len, lanes), bf16),
            pltpu.VMEM((seq_len, lanes), bf16),
            pltpu.VMEM((seq_len, lanes), bf16),
            pltpu.VMEM((2 * rows, seq_len), f32),
            pltpu.VMEM((lanes, seq_len), f32),
            pltpu.VMEM((lanes, seq_len), f32),
            pltpu.VMEM((4 * lanes, seq_len), bf16),
        ]
        + [dma((8,))] * 4
        + [dma((3,))] * 4
        + [dma((4,))] * 6
        + [dma((5,))] * 2
        + [dma((4,))],
        compiler_params=pltpu.CompilerParams(
            collective_id=0, has_side_effects=True, vmem_limit_bytes=56 << 20
        ),
    )(x_own, dy_own, wa_own, wm_own, small_own, cosine, sine)


class PlaneReduce:
    def __init__(self, place, parts, came, kept, low_in, high_in, x_in, y_in, sends, recvs):
        self.place, self.parts, self.came, self.kept = place, parts, came, kept
        self.low_in, self.high_in, self.x_in, self.y_in = low_in, high_in, x_in, y_in
        x, t, k = place.x, place.t, place.k
        half = parts.shape[1] // 2
        self.half = half
        self.first = []
        for at in range(4):
            src = parts.at[4 * (at // 2) + 2 * (1 - k) + at % 2]
            self.first.append(remote(src, came.at[at], sends, recvs, at, place.core))
        self.own = 2 * x + t
        self.of_x = 2 * (1 - x) + t
        self.of_y = 2 * x + (1 - t)
        self.of_d = 2 * (1 - x) + (1 - t)
        self.low = remote(
            kept.at[self.of_d, pl.ds(0, half)], low_in, sends, recvs, 4, place.across_x
        )
        self.high = remote(
            kept.at[self.of_d, pl.ds(half, half)], high_in, sends, recvs, 5, place.across_y
        )
        self.to_x = remote(kept.at[self.of_x], x_in, sends, recvs, 6, place.across_x)
        self.to_y = remote(kept.at[self.of_y], y_in, sends, recvs, 7, place.across_y)

    def start(self):
        for copy in self.first:
            copy.start()

    def second(self):
        k = self.place.k
        for copy in self.first:
            copy.wait_recv()

        def add(at, carry):
            mine = self.parts[4 * (at // 2) + 2 * k + at % 2].astype(f32)
            self.kept[at] = (mine + self.came[at].astype(f32)).astype(bf16)
            return carry

        lax.fori_loop(0, 4, add, 0)
        self.low.start()
        self.high.start()

    def third(self):
        half = self.half
        self.low.wait_recv()
        low, high = pl.ds(0, half), pl.ds(half, half)
        self.kept[self.of_y, low] = (
            self.kept[self.of_y, low].astype(f32) + self.low_in[...].astype(f32)
        ).astype(bf16)
        self.to_y.start()
        self.high.wait_recv()
        self.kept[self.of_x, high] = (
            self.kept[self.of_x, high].astype(f32) + self.high_in[...].astype(f32)
        ).astype(bf16)
        self.to_x.start()

    def finish(self):
        self.to_x.wait_recv()
        self.to_y.wait_recv()

    def total(self, rows):
        return (
            self.kept[self.own, rows].astype(f32)
            + self.x_in[rows].astype(f32)
            + self.y_in[rows].astype(f32)
        )

    def drain(self):
        for copy in self.first + [self.low, self.high, self.to_x, self.to_y]:
            copy.wait_send()


class ChainReduce:
    def __init__(self, place, parts, slots, sums, sends, recvs):
        self.s = place.s
        self.parts, self.slots, self.sums = parts, slots, sums

        def copy(src, d, slot, dev):
            return pltpu.make_async_remote_copy(
                src_ref=src,
                dst_ref=slots.at[slot],
                send_sem=sends.at[d],
                recv_sem=recvs.at[slot],
                device_id=dev,
                device_id_type=pl.DeviceIdType.MESH,
            )

        right, left = place.along(1), place.along(-1)
        self.to_right = lambda src, d: copy(src.at[d], d, d, right)
        self.to_left = lambda src, d, k: copy(src.at[d], d, 4 if k == 1 else d, left)

    def step(self, k):
        s = self.s

        def add(d):
            def one(at, carry):
                self.sums[d, at] = (
                    self.parts[d, at].astype(f32) + self.slots[d, at].astype(f32)
                ).astype(bf16)
                return carry

            lax.fori_loop(0, self.parts.shape[1], one, 0)

        @pl.when(s == 0)
        def _():
            self.to_right(self.parts, s + k).start()

        @pl.when(s == 3)
        def _():
            self.to_left(self.parts, s - k, k).start()

        if k < 3:

            @pl.when((s > 0) & (s + k <= 3))
            def _():
                self.to_right(self.parts, s + k).wait_recv()
                add(s + k)
                self.to_right(self.sums, s + k).start()

            @pl.when((s < 3) & (s - k >= 0))
            def _():
                self.to_left(self.parts, s - k, 2).wait_recv()
                add(s - k)
                self.to_left(self.sums, s - k, k).start()

    def finish(self, out):
        s = self.s

        @pl.when(s > 0)
        def _():
            self.to_right(self.parts, s).wait_recv()

        @pl.when(s < 3)
        def _():
            self.to_left(self.parts, s, 1).wait_recv()


        def one(at, carry):
            out[at] = self.parts[s, at]

            @pl.when(s > 0)
            def _():
                out[at] = (out[at].astype(f32) + self.slots[s, at].astype(f32)).astype(bf16)

            @pl.when(s < 3)
            def _():
                out[at] = (out[at].astype(f32) + self.slots[4, at].astype(f32)).astype(bf16)

            return carry

        lax.fori_loop(0, self.parts.shape[1], one, 0)

    def drain(self):
        s = self.s
        for k in (3, 2, 1):

            @pl.when(s + k <= 3)
            def _():
                self.to_right(self.parts, s + k).wait_send()

            @pl.when(s - k >= 0)
            def _():
                self.to_left(self.parts, s - k, k).wait_send()


def turn_parts(flat, turned):
    pieces, rows, wide = flat.shape
    n_ctx, depth, _ = turned.shape
    for at in range(pieces):
        part = flat[at].astype(f32).T.astype(bf16)
        turned[:, :, at * rows : (at + 1) * rows] = part.reshape(n_ctx, depth, rows)


def reduce_kernel(
    po, ps, ga, gm, vec, x_own, dy_own, small,
    output, grad_in, g_qkv, g_out_t, g_up, g_down_t, vec_sum,
    po_came, po_kept, po_low, po_high, po_x, po_y,
    ps_came, ps_kept, ps_low, ps_high, ps_x, ps_y,
    ga_slots, ga_sums, ga_flat, ga_total, ga_back, gm_slots, gm_sums, gm_total, gm_back, slots,
    po_send, po_recv, ps_send, ps_recv, ga_send, ga_recv, gm_send, gm_recv,
    sa_send, sa_recv, sm_send, sm_recv, cube_send, cube_recv, local,
):
    place = Place()
    vec_sum[...] = vec[...]
    place.meet()
    cube = CubeSum(place, vec_sum, slots, cube_send, cube_recv)
    outs = PlaneReduce(
        place, po, po_came, po_kept, po_low, po_high, po_x, po_y, po_send, po_recv
    )
    scaled = PlaneReduce(
        place, ps, ps_came, ps_kept, ps_low, ps_high, ps_x, ps_y, ps_send, ps_recv
    )
    chain_a = ChainReduce(place, ga, ga_slots, ga_sums, ga_send, ga_recv)
    chain_m = ChainReduce(place, gm, gm_slots, gm_sums, gm_send, gm_recv)
    swap_a = CtxSwap(place, ga_total, ga_back, sa_send, sa_recv, local.at[0])
    swap_m = CtxSwap(place, gm_total, gm_back, sm_send, sm_recv, local.at[1])
    cube.start(0)
    chain_a.step(3)
    chain_m.step(3)
    outs.start()
    scaled.start()
    cube.finish(0)
    cube.start(1)
    outs.second()
    scaled.second()
    chain_a.step(2)
    chain_m.step(2)
    cube.finish(1)
    cube.start(2)
    outs.third()
    scaled.third()
    chain_a.step(1)
    cube.finish(2)
    cube.start(3)
    chain_a.finish(ga_flat)
    turn_parts(ga_flat, ga_total)
    swap_a.start()
    chain_m.step(1)
    outs.finish()
    scaled.finish()
    cube.finish(3)
    cube.start(4)
    rows = 32

    def final(at, carry):
        here = pl.ds(pl.multiple_of(at * rows, rows), rows)
        values = x_own[here].astype(f32)
        normed, inv = layer_norm_parts(values)
        bias = small[4:5] + small[5:6]
        output[here] = (values + outs.total(here) + bias).astype(bf16)
        part = scaled.total(here)
        inner = jnp.mean(part, -1, keepdims=True)
        aligned = jnp.mean(part * normed, -1, keepdims=True)
        grad_in[here] = dy_own[here].astype(f32) + inv * (part - inner - normed * aligned)
        return carry

    lax.fori_loop(0, x_own.shape[0] // rows, final, 0)
    cube.finish(4)
    chain_m.finish(gm_total)
    swap_m.start()
    swap_a.finish()
    lanes = ga.shape[2]
    for at in range(4):
        cols = slice(at * lanes, (at + 1) * lanes)
        for j in range(3):
            g_qkv[j, :, cols] = ga_back[at, :, j * lanes : (j + 1) * lanes].astype(f32)
        g_out_t[:, cols] = ga_back[at, :, 3 * lanes :].astype(f32)
    swap_m.finish()
    units = gm.shape[3] // 2
    for at in range(4):
        cols = slice(at * units, (at + 1) * units)
        g_up[:, cols] = gm_back[at, :, :units].astype(f32)
        g_down_t[:, cols] = gm_back[at, :, units:].astype(f32)
    for part in (outs, scaled, chain_a, chain_m, swap_a, swap_m):
        part.drain()


def reduce_all(po, ps, ga, gm, vec, x_own, dy_own, small):
    rows, model = x_own.shape
    depth, wide_m = gm.shape[2:]
    lanes = ga.shape[2]
    wide_a = 4 * lanes
    vmem = pl.BlockSpec(memory_space=pltpu.VMEM)
    dma = pltpu.SemaphoreType.DMA
    half = (rows // 2, model)
    plane = [
        pltpu.VMEM((4, rows, model), bf16),
        pltpu.VMEM((4, rows, model), bf16),
        pltpu.VMEM(half, bf16),
        pltpu.VMEM(half, bf16),
        pltpu.VMEM((rows, model), bf16),
        pltpu.VMEM((rows, model), bf16),
    ]

    def chain(parts):
        return [
            pltpu.VMEM((5,) + parts.shape[1:], bf16),
            pltpu.VMEM((4,) + parts.shape[1:], bf16),
            pltpu.VMEM(parts.shape[1:], bf16),
        ]

    def swapped(wide):
        return [pltpu.VMEM((4, depth, wide), bf16)]

    return pl.pallas_call(
        reduce_kernel,
        out_shape=(
            jax.ShapeDtypeStruct((rows, model), bf16),
            jax.ShapeDtypeStruct((rows, model), f32),
            jax.ShapeDtypeStruct((3, depth, wide_a), f32),
            jax.ShapeDtypeStruct((depth, wide_a), f32),
            jax.ShapeDtypeStruct((depth, 2 * wide_m), f32),
            jax.ShapeDtypeStruct((depth, 2 * wide_m), f32),
            jax.ShapeDtypeStruct(vec.shape, f32),
        ),
        in_specs=[vmem] * 8,
        out_specs=[vmem] * 7,
        scratch_shapes=plane
        + plane
        + chain(ga)
        + swapped(wide_a) * 2
        + chain(gm)
        + swapped(wide_m)
        + [pltpu.VMEM((5,) + vec.shape, f32)]
        + [dma((8,))] * 4
        + [dma((4,)), dma((5,))] * 2
        + [dma((3,))] * 4
        + [dma((5,))] * 2
        + [dma((2,))],
        compiler_params=pltpu.CompilerParams(
            collective_id=1, has_side_effects=True, vmem_limit_bytes=52 << 20
        ),
    )(po, ps, ga, gm, vec, x_own, dy_own, small)


def rotary_lanes(seq_len, lanes):
    half = ROT // 2
    inverse = rope_base ** (-np.arange(half) / half)
    angles = np.arange(seq_len)[:, None] * inverse[None, :]
    plain = np.zeros((seq_len, HD - ROT))
    cosine = np.concatenate([np.cos(angles), np.cos(angles), plain + 1], 1)
    sine = np.concatenate([-np.sin(angles), np.sin(angles), plain], 1)
    heads = lanes // HD
    return (
        jnp.asarray(np.tile(cosine, (1, heads)), f32),
        jnp.asarray(np.tile(sine, (1, heads)), f32),
    )


def turn_lanes(value, cosine, sine):
    lane = lax.broadcasted_iota(jnp.int32, value.shape, 1) % HD
    half = ROT // 2
    swapped = jnp.where(lane < half, jnp.roll(value, -half, 1), jnp.roll(value, half, 1))
    return value * cosine + swapped * sine


def per_device_plane(
    inputs, ln1_gain, ln1_bias, ln2_gain, ln2_bias, w_qkv, b_qkv, w_out, b_out,
    w_up, b_up, w_down, b_down, cotangent,
):
    s, c, t = (lax.axis_index(name) for name in ("shard", "ctx", "tensor"))
    n_ctx = 4
    group = 4 * s + c
    depth = w_up.shape[0]
    width = w_qkv.shape[2]
    units = w_up.shape[1]
    lanes, cols = width // n_ctx, units // n_ctx
    x_own, dy_own = inputs[0], cotangent[0]
    rows, model = x_own.shape
    seq_len = rows * 8

    six = jnp.stack([ln1_gain, ln1_bias, ln2_gain, ln2_bias, b_out, b_down]).astype(f32)
    slot = jnp.arange(32)[None, :, None]
    six = jnp.where(slot == 2 * group + t, six[:, None, :], 0.0).reshape(6, model)
    three = jnp.where(slot == 16 * t + group, b_qkv.astype(f32), 0.0).reshape(3, model)
    four = jnp.where(slot == 16 * t + group, b_up.astype(f32)[:, None, :], 0.0)
    four = four.reshape(-1, model)
    small_own = jnp.concatenate([six, three, four, jnp.zeros((3, model), f32)])

    first = jnp.concatenate([w_qkv, w_out.T[None]]).reshape(4, depth, n_ctx, lanes)
    first = first.transpose(2, 1, 0, 3).reshape(n_ctx, depth, 4 * lanes)
    second = jnp.stack([w_up, w_down.T]).reshape(2, depth, n_ctx, cols)
    second = second.transpose(2, 1, 0, 3).reshape(n_ctx, depth, 2 * cols)
    cosine, sine = rotary_lanes(seq_len, lanes)
    x_all, dy_all, first, second, small, mixed, grad_projected, ga = gather_all(
        x_own, dy_own, first, second, small_own, cosine, sine
    )
    gain_one, gain_two, shift_two = small[0], small[2], small[3]
    bias_up = lax.dynamic_slice(small[9:13].reshape(-1), (units * t + cols * c,), (cols,))
    first = first.reshape(model, 4 * lanes)
    second = second.reshape(model, 2 * cols)
    dy = dy_all.reshape(seq_len, model)
    normed, _ = layer_norm_parts(x_all.reshape(seq_len, model).astype(f32))
    second_norm = (normed * gain_two + shift_two).astype(bf16)
    up, down_t = second[:, :cols], second[:, cols:]
    hidden_pre = jnp.dot(second_norm, up, preferred_element_type=f32) + bias_up
    hidden = jax.nn.gelu(hidden_pre, approximate=False).astype(bf16)
    grad_hidden = jnp.dot(dy, down_t, preferred_element_type=f32)
    grad_pre = (grad_hidden * gelu_slope(hidden_pre)).astype(bf16)
    grad_second = contract_last(grad_pre, up)
    grad_first = contract_last(grad_projected, first[:, : 3 * lanes])
    po = contract_last(mixed, first[:, 3 * lanes :]) + contract_last(hidden, down_t)
    ps = grad_first * gain_one + grad_second * gain_two
    gm = jnp.concatenate(
        [contract_first(second_norm, grad_pre), contract_first(dy, hidden)], 1
    ).astype(bf16)
    slot = jnp.arange(8)[None, :, None]
    b_qkv_part = jnp.sum(grad_projected, 0, dtype=f32).reshape(3, 1, lanes)
    b_qkv_part = jnp.where(slot == 4 * t + c, b_qkv_part, 0.0).reshape(3, model)
    b_up_part = jnp.sum(grad_pre, 0, dtype=f32).reshape(1, 1, cols)
    b_up_part = jnp.where(slot == 4 * t + c, b_up_part, 0.0).reshape(-1, model)
    vec = jnp.stack(
        [
            jnp.sum(grad_first * normed, 0),
            jnp.sum(grad_first, 0),
            jnp.sum(grad_second * normed, 0),
            jnp.sum(grad_second, 0),
            jnp.sum(dy_own.astype(f32), 0),
        ]
    )
    vec = jnp.concatenate([vec, b_qkv_part, b_up_part, jnp.zeros((4, model), f32)])
    output, grad_in, g_qkv, g_out_t, g_up, g_down_t, vec = reduce_all(
        po.astype(bf16).reshape(8, rows, model),
        ps.astype(bf16).reshape(8, rows, model),
        ga.reshape(4, n_ctx, lanes, 4 * depth),
        gm.reshape(4, n_ctx, depth, 2 * cols),
        vec,
        x_own,
        dy_own,
        small,
    )
    piece = model // 32
    five = lax.dynamic_slice(vec, (0, (2 * group + t) * piece), (5, piece))
    out_b_qkv = lax.dynamic_slice(vec, (5, width * t + piece * group), (3, piece))
    part = units // 16
    out_b_up = lax.dynamic_slice(vec[8:12].reshape(-1), (units * t + part * group,), (part,))
    return (
        output[None],
        grad_in[None],
        five[0],
        five[1],
        five[2],
        five[3],
        g_qkv,
        out_b_qkv[:, None],
        g_out_t.T,
        five[4],
        g_up,
        out_b_up[None],
        g_down_t.T,
        five[4],
    )


def fits_plane(mesh):
    return tuple(mesh.shape[name] for name in ("shard", "ctx", "tensor")) == (4, 4, 2)


def solution(mesh):
    placed = (
        P("shard", ("ctx", "tensor"), None),
        P(("shard", "ctx", "tensor")),
        P(("shard", "ctx", "tensor")),
        P(("shard", "ctx", "tensor")),
        P(("shard", "ctx", "tensor")),
        P(None, ("shard", "ctx"), "tensor"),
        P(None, "tensor", ("shard", "ctx")),
        P("tensor", ("shard", "ctx")),
        P(("shard", "ctx", "tensor")),
        P(("shard", "ctx"), "tensor"),
        P("tensor", ("shard", "ctx")),
        P("tensor", ("shard", "ctx")),
        P(("shard", "ctx", "tensor")),
        P("shard", ("ctx", "tensor"), None),
    )
    return jax.shard_map(
        per_device_plane if fits_plane(mesh) else per_device,
        mesh=mesh,
        in_specs=placed,
        out_specs=(
            P("shard", ("ctx", "tensor"), None),
            P("shard", ("ctx", "tensor"), None),
            P(("shard", "ctx", "tensor")),
            P(("shard", "ctx", "tensor")),
            P(("shard", "ctx", "tensor")),
            P(("shard", "ctx", "tensor")),
            P(None, ("shard", "ctx"), "tensor"),
            P(None, "tensor", ("shard", "ctx")),
            P("tensor", ("shard", "ctx")),
            P(("shard", "ctx", "tensor")),
            P(("shard", "ctx"), "tensor"),
            P("tensor", ("shard", "ctx")),
            P("tensor", ("shard", "ctx")),
            P(("shard", "ctx", "tensor")),
        ),
        check_vma=False,
    )
```

```python
import functools

import jax
import jax.numpy as jnp
import numpy as np
from jax import lax
from jax.experimental import pallas as pl
from jax.experimental.pallas import tpu as pltpu
from jax.sharding import PartitionSpec as P

HD = 64
ROT = 16


norm_eps = 1e-05
rope_base = 10000.0
bf16 = jnp.bfloat16
f32 = jnp.float32
GROUP = ("shard", "ctx")


def layer_norm_parts(values):
    centre = values - jnp.mean(values, -1, keepdims=True)
    spread = jnp.mean(centre * centre, -1, keepdims=True)
    inv_std = lax.rsqrt(spread + norm_eps)
    return (centre * inv_std, inv_std)


def rotary_tables(positions):
    half_dims = ROT // 2
    ladder = jnp.arange(half_dims, dtype=f32)
    inverse = jnp.exp(ladder * (-2.0 / ROT) * jnp.log(f32(rope_base)))
    angles = positions.astype(f32)[:, None] * inverse[None, :]
    angles = jnp.concatenate([angles, angles], -1)
    return (jnp.cos(angles)[:, None, :], jnp.sin(angles)[:, None, :])


def rotate(values, cosine, sine_table):
    rot_dims = cosine.shape[-1]
    half_dims = rot_dims // 2
    turned = values[..., :rot_dims]
    swapped = jnp.concatenate([-turned[..., half_dims:], turned[..., :half_dims]], -1)
    return jnp.concatenate([turned * cosine + swapped * sine_table, values[..., rot_dims:]], -1)


def gelu_slope(values):
    return (
        0.5 * (1.0 + lax.erf(values * 0.7071067811865476))
        + values * jnp.exp(-0.5 * values * values) * 0.3989422804014327
    )


def contract_last(left_side, right_side):
    return lax.dot_general(
        left_side, right_side, (((1,), (1,)), ((), ())), preferred_element_type=f32
    )


def contract_first(left_side, right_side):
    return lax.dot_general(
        left_side, right_side, (((0,), (0,)), ((), ())), preferred_element_type=f32
    )


def attention_kernel(lanes, wide, rows, in_ref, out_ref, key_grad, value_grad):
    seq_len = in_ref.shape[0]
    heads = lanes // HD
    parts = wide // rows
    scale = HD ** (-0.5)
    key_grad[...] = jnp.zeros_like(key_grad)
    value_grad[...] = jnp.zeros_like(value_grad)
    out_ref[...] = jnp.zeros_like(out_ref)
    for step in range(seq_len // wide):
        length = (step + 1) * wide

        def one_block(turn, carry, step=step, length=length):
            head = turn % heads
            start = pl.multiple_of(step * wide + (turn // heads) * rows, rows)
            here = pl.ds(start, rows)
            mine = lax.broadcasted_iota(jnp.int32, (rows, lanes), 1) // HD == head
            queries = in_ref[here, 0:lanes].astype(f32) * scale
            queries = jnp.where(mine, queries, 0.0).astype(bf16)
            grads = in_ref[here, 3 * lanes : 4 * lanes].astype(f32)
            grads = jnp.where(mine, grads, 0.0).astype(bf16)
            keys = in_ref[0:length, lanes : 2 * lanes]
            values = in_ref[0:length, 2 * lanes : 3 * lanes]
            scores = contract_last(queries, keys)
            key_at = lax.broadcasted_iota(jnp.int32, scores.shape, 1)
            query_at = start + lax.broadcasted_iota(jnp.int32, scores.shape, 0)
            scores = jnp.where(key_at <= query_at, scores, -1e30)
            exp_scores = jnp.exp(scores - jnp.max(scores, -1, keepdims=True))
            probs = exp_scores * (1.0 / jnp.sum(exp_scores, -1, keepdims=True))
            attn_prob = probs.astype(bf16)
            mixed = jnp.dot(attn_prob, values, preferred_element_type=f32)
            value_grad[0:length, :] += contract_first(attn_prob, grads)
            prob_grad = contract_last(grads, values)
            inner_sum = jnp.sum(probs * prob_grad, -1, keepdims=True)
            score_grad = (probs * (prob_grad - inner_sum)).astype(bf16)
            query_grad = jnp.dot(score_grad, keys, preferred_element_type=f32) * scale
            key_grad[0:length, :] += contract_first(score_grad, queries)
            out_ref[here, 0:lanes] = jnp.where(
                mine, mixed, out_ref[here, 0:lanes].astype(f32)
            ).astype(bf16)
            out_ref[here, lanes : 2 * lanes] = jnp.where(
                mine, query_grad, out_ref[here, lanes : 2 * lanes].astype(f32)
            ).astype(bf16)
            return carry

        lax.fori_loop(0, parts * heads, one_block, 0)
    out_ref[:, 2 * lanes : 3 * lanes] = key_grad[...].astype(bf16)
    out_ref[:, 3 * lanes : 4 * lanes] = value_grad[...].astype(bf16)


def attend(packed):
    seq_len, width = packed.shape
    lanes = width // 4
    wide = min(512, seq_len)
    rows = min(256, wide)
    return pl.pallas_call(
        functools.partial(attention_kernel, lanes, wide, rows),
        out_shape=jax.ShapeDtypeStruct((seq_len, width), bf16),
        in_specs=[pl.BlockSpec(memory_space=pltpu.VMEM)],
        out_specs=pl.BlockSpec(memory_space=pltpu.VMEM),
        scratch_shapes=[pltpu.VMEM((seq_len, lanes), f32), pltpu.VMEM((seq_len, lanes), f32)],
        compiler_params=pltpu.CompilerParams(vmem_limit_bytes=48 << 20),
        cost_estimate=pl.CostEstimate(
            flops=14 * seq_len * seq_len * lanes,
            bytes_accessed=4 * seq_len * width,
            transcendentals=seq_len * seq_len * lanes // HD,
        ),
    )(packed)


def per_device(
    inputs,
    ln1_gain,
    ln1_bias,
    ln2_gain,
    ln2_bias,
    w_qkv,
    b_qkv,
    w_out,
    b_out,
    w_up,
    b_up,
    w_down,
    b_down,
    cotangent,
):
    pair = lax.axis_index("tensor")
    first = pair == 0
    n_ctx = lax.axis_size("ctx")
    n_group = lax.axis_size("shard") * n_ctx
    swap = ((0, 1), (1, 0))

    def exchange(value):
        return lax.ppermute(value, "tensor", swap)

    def in_order(own, other, axis):
        return jnp.where(
            first,
            jnp.concatenate([own, other], axis),
            jnp.concatenate([other, own], axis),
        )

    small_own = jnp.stack([ln1_gain, ln1_bias, ln2_gain, ln2_bias, b_out, b_down])
    small = in_order(small_own, exchange(small_own), 1)
    piece = small.shape[1]
    depth = w_up.shape[0]
    ff_group = w_up.shape[1]
    width = w_qkv.shape[2]
    riders = jnp.concatenate([small.reshape(-1), b_qkv.reshape(-1), b_up.reshape(-1)])
    room = depth * 128
    riders = jnp.pad(riders, (0, room - riders.shape[0])).reshape(depth, 128)
    first_pack = jnp.concatenate([w_qkv[0], w_qkv[1], w_qkv[2], w_out.T, riders], 1)
    second_pack = jnp.concatenate([w_up, w_down.T], 1)
    first_whole = lax.all_gather(first_pack, GROUP, axis=0, tiled=True)
    second_whole = lax.all_gather(second_pack, GROUP, axis=0, tiled=True)
    model = first_whole.shape[0]
    whole_qkv = first_whole[:, : 3 * width]
    whole_out_t = first_whole[:, 3 * width : 4 * width]
    gathered = first_whole[:, 4 * width :].reshape(n_group, room).astype(f32)
    whole_up = second_whole[:, :ff_group]
    whole_down_t = second_whole[:, ff_group:]

    gain_one, shift_one, gain_two, shift_two, bias_out, bias_down = [
        gathered[:, at * piece : (at + 1) * piece].reshape(-1) for at in range(6)
    ]
    at = 6 * piece
    part = b_qkv.shape[2]
    bias_qkv = jnp.concatenate(
        [gathered[:, at + j * part : at + (j + 1) * part].reshape(-1) for j in range(3)]
    )
    at = at + 3 * part
    up_part = b_up.shape[1]
    bias_up = gathered[:, at : at + up_part].reshape(-1)

    both_own = jnp.concatenate([inputs, cotangent], 0)
    both = in_order(both_own, exchange(both_own), 1)
    grad_own = cotangent[0]
    own_rows = inputs[0].astype(f32)
    normed_own, inv_own = layer_norm_parts(own_rows)
    normed, _ = layer_norm_parts(both[0].astype(f32))
    grad_rows = both[1]
    first_norm = (normed * gain_one + shift_one).astype(bf16)
    second_norm = (normed * gain_two + shift_two).astype(bf16)
    block_len = first_norm.shape[0]
    half = block_len // 2

    def own_half(value):
        return jnp.where(first, value[:half], value[half:])

    def other_half(value):
        return jnp.where(first, value[half:], value[:half])

    positions = lax.axis_index("ctx") * block_len + jnp.arange(block_len, dtype=jnp.int32)
    cosine, sine_table = rotary_tables(positions)
    projected = jnp.dot(first_norm, whole_qkv, preferred_element_type=f32) + bias_qkv
    heads = width // HD

    def turned(value, sine):
        return (
            rotate(value.astype(f32).reshape(block_len, heads, HD), cosine, sine)
            .astype(bf16)
            .reshape(block_len, width)
        )

    queries = turned(projected[:, :width], sine_table)
    key_rows = turned(projected[:, width : 2 * width], sine_table)
    value_rows = projected[:, 2 * width :].astype(bf16)
    grad_mixed = jnp.dot(grad_rows, whole_out_t, preferred_element_type=f32).astype(bf16)
    lanes = width // n_ctx
    packed = jnp.stack([queries, key_rows, value_rows, grad_mixed])
    packed = packed.reshape(4, block_len, n_ctx, lanes).transpose(2, 1, 0, 3)
    packed = packed.reshape(n_ctx, block_len, 4 * lanes)
    there = lax.all_to_all(packed, "ctx", split_axis=0, concat_axis=0, tiled=True)

    hidden_pre = jnp.dot(second_norm, whole_up, preferred_element_type=f32) + bias_up
    hidden = jax.nn.gelu(hidden_pre, approximate=False).astype(bf16)
    feed_out = contract_last(hidden, whole_down_t)
    grad_hidden = jnp.dot(grad_rows, whole_down_t, preferred_element_type=f32)
    grad_pre = (grad_hidden * gelu_slope(hidden_pre)).astype(bf16)
    grad_up = contract_first(second_norm, grad_pre).astype(bf16)
    grad_down_t = contract_first(grad_rows, hidden).astype(bf16)
    second_grads = jnp.concatenate([grad_up, grad_down_t], 1)
    there, second_grads = lax.optimization_barrier((there, second_grads))
    second_sum = lax.psum_scatter(second_grads, GROUP, scatter_dimension=0, tiled=True)
    grad_b_up = jnp.sum(grad_pre, 0, dtype=f32)
    grad_second = contract_last(grad_pre, whole_up)

    attended = attend(there.reshape(n_ctx * block_len, 4 * lanes))
    back = lax.all_to_all(
        attended.reshape(n_ctx, block_len, 4 * lanes),
        "ctx",
        split_axis=0,
        concat_axis=0,
        tiled=True,
    )
    back = back.reshape(n_ctx, block_len, 4, lanes).transpose(2, 1, 0, 3)
    mixed_rows, query_back, key_back, value_back = back.reshape(4, block_len, width)
    grad_projected = jnp.concatenate(
        [turned(query_back, -sine_table), turned(key_back, -sine_table), value_back], 1
    )
    grad_qkv = contract_first(first_norm, grad_projected).astype(bf16)
    grad_out_t = contract_first(grad_rows, mixed_rows).astype(bf16)
    grad_b_qkv = jnp.sum(grad_projected, 0, dtype=f32)
    grad_first = contract_last(grad_projected, whole_qkv)

    vectors = jnp.stack(
        [
            jnp.sum(grad_first * normed, 0),
            jnp.sum(grad_first, 0),
            jnp.sum(grad_second * normed, 0),
            jnp.sum(grad_second, 0),
            jnp.sum(grad_own.astype(f32), 0),
        ]
    )
    back_riders = jnp.concatenate(
        [
            vectors.reshape(5, n_group, piece).transpose(1, 0, 2).reshape(n_group, -1),
            grad_b_qkv.reshape(3, n_group, part).transpose(1, 0, 2).reshape(n_group, -1),
            grad_b_up.reshape(n_group, up_part),
        ],
        1,
    )
    back_riders = jnp.pad(back_riders, ((0, 0), (0, room - back_riders.shape[1])))
    back_riders = back_riders.reshape(model, 128).astype(bf16)
    first_grads = jnp.concatenate([grad_qkv, grad_out_t, back_riders], 1)
    first_grads, second_sum = lax.optimization_barrier((first_grads, second_sum))
    first_sum = lax.psum_scatter(first_grads, GROUP, scatter_dimension=0, tiled=True)

    partial_sum = contract_last(mixed_rows, whole_out_t) + feed_out
    branches = own_half(partial_sum) + exchange(other_half(partial_sum).astype(bf16)).astype(f32)
    output = (own_rows + branches + bias_out + bias_down).astype(bf16)
    scaled = grad_first * gain_one + grad_second * gain_two
    scaled = own_half(scaled) + exchange(other_half(scaled).astype(bf16)).astype(f32)
    inner_sum = jnp.mean(scaled, -1, keepdims=True)
    aligned = jnp.mean(scaled * normed_own, -1, keepdims=True)
    grad_input = grad_own.astype(f32) + inv_own * (scaled - inner_sum - normed_own * aligned)

    second_sum = second_sum.astype(f32)
    first_sum = first_sum.astype(f32)
    grad_w_qkv = first_sum[:, : 3 * width].reshape(depth, 3, width).transpose(1, 0, 2)
    grad_w_out = first_sum[:, 3 * width : 4 * width].T
    summed = first_sum[:, 4 * width :].reshape(-1)
    vector_sum = summed[: 5 * piece].reshape(5, piece)
    own = piece // 2
    mine = jnp.where(first, vector_sum[:, :own], vector_sum[:, own:])
    theirs = jnp.where(first, vector_sum[:, own:], vector_sum[:, :own])
    vector_grads = mine + exchange(theirs)
    at = 5 * piece
    out_b_qkv = summed[at : at + 3 * part].reshape(3, 1, part)
    at = at + 3 * part
    out_b_up = summed[at : at + up_part].reshape(1, up_part)
    return (
        output[None],
        grad_input[None],
        vector_grads[0],
        vector_grads[1],
        vector_grads[2],
        vector_grads[3],
        grad_w_qkv,
        out_b_qkv,
        grad_w_out,
        vector_grads[4],
        second_sum[:, :ff_group],
        out_b_up,
        second_sum[:, ff_group:].T,
        vector_grads[4],
    )

def remote(src, dst, sends, recvs, at, to):
    return pltpu.make_async_remote_copy(
        src_ref=src,
        dst_ref=dst,
        send_sem=sends.at[at],
        recv_sem=recvs.at[at],
        device_id=to,
        device_id_type=pl.DeviceIdType.MESH,
    )


class Place:
    def __init__(self):
        self.s = lax.axis_index("shard")
        self.c = lax.axis_index("ctx")
        self.t = lax.axis_index("tensor")
        self.x = self.c // 2
        self.k = self.c % 2
        self.block = 2 * self.c + self.t
        self.core_c = 2 * self.x + (1 - self.k)
        self.x_c = 2 * (1 - self.x) + self.k
        self.far_c = 2 * (1 - self.x) + (1 - self.k)
        self.y_t = 1 - self.t
        self.core = {"ctx": self.core_c}
        self.across_x = {"ctx": self.x_c}
        self.far = {"ctx": self.far_c}
        self.across_y = {"tensor": self.y_t}

    def along(self, step):
        return {"shard": lax.rem(self.s + step + 4, 4)}

    def meet(self):
        barrier = pltpu.get_barrier_semaphore()
        others = [self.core, self.across_x, self.far, self.across_y]
        others += [self.along(step) for step in (1, 2, 3)]
        for other in others:
            pl.semaphore_signal(
                barrier, inc=1, device_id=other, device_id_type=pl.DeviceIdType.MESH
            )
        pl.semaphore_wait(barrier, len(others))

    def cube(self):
        pair = self.s + 1 - 2 * lax.rem(self.s, 2)
        return [
            self.core,
            {"shard": pair},
            self.along(2),
            self.across_x,
            self.across_y,
        ]


class PlaneGather:
    def __init__(self, place, own, full, sends, recvs, local):
        half = own.shape[0] // 2
        b = place.block
        xb = 2 * place.x_c + place.t
        yb = 2 * place.c + place.y_t
        db = 2 * place.x_c + place.y_t
        low, high = pl.ds(0, half), pl.ds(half, half)

        def to(src, dst, at, dev):
            return remote(src, dst, sends, recvs, at, dev)

        self.local = pltpu.make_async_copy(own, full.at[b], local)
        self.to_x = to(own, full.at[b], 0, place.across_x)
        self.to_y = to(own, full.at[b], 1, place.across_y)
        self.low_y = to(full.at[xb, low], full.at[xb, low], 2, place.across_y)
        self.high_x = to(full.at[yb, high], full.at[yb, high], 3, place.across_x)
        self.core_own = to(own, full.at[b], 4, place.core)
        self.core_x = to(full.at[xb], full.at[xb], 5, place.core)
        self.core_y = to(full.at[yb], full.at[yb], 6, place.core)
        self.core_d = to(full.at[db], full.at[db], 7, place.core)
        self.all = [
            self.to_x, self.to_y, self.low_y, self.high_x,
            self.core_own, self.core_x, self.core_y, self.core_d,
        ]

    def start(self):
        self.to_x.start()
        self.to_y.start()
        self.core_own.start()
        self.local.start()

    def second(self):
        self.to_x.wait_recv()
        self.low_y.start()
        self.core_x.start()
        self.to_y.wait_recv()
        self.high_x.start()
        self.core_y.start()

    def third(self):
        self.low_y.wait_recv()
        self.high_x.wait_recv()
        self.core_d.start()

    def finish(self):
        self.local.wait()
        for copy in (self.core_own, self.core_x, self.core_y, self.core_d):
            copy.wait_recv()

    def drain(self):
        for copy in self.all:
            copy.wait_send()


class CtxSwap:
    def __init__(self, place, own, dst, sends, recvs, local):
        c = place.c
        self.copies = []
        for at, (peer, dev) in enumerate(
            ((place.core_c, place.core), (place.x_c, place.across_x), (place.far_c, place.far))
        ):
            self.copies.append(remote(own.at[peer], dst.at[c], sends, recvs, at, dev))
        self.local = pltpu.make_async_copy(own.at[c], dst.at[c], local)

    def start(self):
        for copy in self.copies:
            copy.start()
        self.local.start()

    def finish(self):
        for copy in self.copies:
            copy.wait_recv()
        self.local.wait()

    def drain(self):
        for copy in self.copies:
            copy.wait_send()


class ChainGather:
    def __init__(self, place, full, right, left, recvs):
        self.s = place.s
        s = place.s

        def copy(j, sends, dev):
            return pltpu.make_async_remote_copy(
                src_ref=full.at[j],
                dst_ref=full.at[j],
                send_sem=sends.at[j],
                recv_sem=recvs.at[j],
                device_id=dev,
                device_id_type=pl.DeviceIdType.MESH,
            )

        self.to_right = lambda j: copy(j, right, place.along(1))
        self.to_left = lambda j: copy(j, left, place.along(-1))

    def start(self):
        s = self.s

        @pl.when(s < 3)
        def _():
            self.to_right(s).start()

        @pl.when(s > 0)
        def _():
            self.to_left(s).start()

    def step(self, distance):
        s = self.s

        @pl.when(s >= distance)
        def _():
            self.to_right(s - distance).wait_recv()

            @pl.when(s < 3)
            def _():
                self.to_right(s - distance).start()

        @pl.when(s + distance <= 3)
        def _():
            self.to_left(s + distance).wait_recv()

            @pl.when(s > 0)
            def _():
                self.to_left(s + distance).start()

    def drain(self):
        s = self.s
        for distance in range(4):

            @pl.when((s >= distance) & (s < 3))
            def _():
                self.to_right(s - distance).wait_send()

            @pl.when((s + distance <= 3) & (s > 0))
            def _():
                self.to_left(s + distance).wait_send()


class CubeSum:
    def __init__(self, place, total, slots, sends, recvs):
        self.total, self.slots = total, slots
        self.copies = [
            remote(total, slots.at[at], sends, recvs, at, dev)
            for at, dev in enumerate(place.cube())
        ]

    def start(self, at):
        self.copies[at].start()

    def finish(self, at):
        self.copies[at].wait()
        self.total[...] += self.slots[at]


def half_mask(rows, lanes, head):
    lane = lax.broadcasted_iota(jnp.int32, (rows, lanes), 1)
    return (lane < HD) if head == 0 else (lane >= HD)


def stack_heads(value):
    rows, lanes = value.shape
    parts = [jnp.where(half_mask(rows, lanes, head), value, 0.0) for head in range(2)]
    return jnp.concatenate(parts, 0)


def join_heads(value):
    rows, lanes = value.shape[0] // 2, value.shape[1]
    return jnp.where(half_mask(rows, lanes, 0), value[:rows], value[rows:])


def turn_block(value, cosine, sine):
    lanes = value.shape[1]
    lane = lax.broadcasted_iota(jnp.int32, value.shape, 1) % HD
    half = ROT // 2
    up = pltpu.roll(value, lanes - half, 1)
    down = pltpu.roll(value, half, 1)
    return value * cosine + jnp.where(lane < half, up, down) * sine


def attention_rows(at, rows, q_all, k_all, v_all, g_all, scores, key_grad, value_grad):
    length = (at + 1) * rows
    here = pl.ds(at * rows, rows)
    seen = pl.ds(0, length)
    queries = stack_heads(q_all[here].astype(f32)).astype(bf16)
    scores[:, seen] = contract_last(queries, k_all[seen])
    edge = pl.ds(at * rows, rows)
    key_at = lax.broadcasted_iota(jnp.int32, (rows, rows), 1)
    query_at = lax.broadcasted_iota(jnp.int32, (rows, rows), 0)
    keep = key_at <= query_at
    for head in range(2):
        part = pl.ds(head * rows, rows)
        scores[part, edge] = jnp.where(keep, scores[part, edge], -1e30)
    top = jnp.max(scores[:, seen], -1, keepdims=True)
    weights = jnp.exp(scores[:, seen] - top)
    scores[:, seen] = weights
    inverse = 1.0 / jnp.sum(weights, -1, keepdims=True)
    low = weights.astype(bf16)
    mixed = jnp.dot(low, v_all[seen], preferred_element_type=f32) * inverse
    grads = (stack_heads(g_all[here].astype(f32)) * inverse).astype(bf16)
    inner = jnp.sum(grads.astype(f32) * mixed, -1, keepdims=True)
    value_grad[:, seen] += contract_first(grads, low)
    prob_grad = contract_last(grads, v_all[seen])
    score_grad = (scores[:, seen] * (prob_grad - inner)).astype(bf16)
    key_grad[:, seen] += contract_first(queries, score_grad)
    query_grad = jnp.dot(score_grad, k_all[seen], preferred_element_type=f32)
    return join_heads(mixed), join_heads(query_grad) * (HD ** (-0.5))


def gather_kernel(
    x_own, dy_own, wa_own, wm_own, small_own, cosine, sine,
    x_all, dy_all, wa_all, wm_all, small_all, mixed_all, grads_all, ga_all,
    slots, first_norm, q_all, k_all, v_all, g_all, scores, key_grad, value_grad, flipped,
    x_send, x_recv, dy_send, dy_recv, wa_send, wa_recv, wm_send, wm_recv,
    ca_right, ca_left, ca_recv, cm_right, cm_left, cm_recv, cube_send, cube_recv, local,
):
    place = Place()
    small_all[...] = small_own[...]
    place.meet()
    xs = PlaneGather(place, x_own, x_all, x_send, x_recv, local.at[0])
    dys = PlaneGather(place, dy_own, dy_all, dy_send, dy_recv, local.at[1])
    swap_a = CtxSwap(place, wa_own, wa_all.at[place.s], wa_send, wa_recv, local.at[2])
    swap_m = CtxSwap(place, wm_own, wm_all.at[place.s], wm_send, wm_recv, local.at[3])
    chain_a = ChainGather(place, wa_all, ca_right, ca_left, ca_recv)
    chain_m = ChainGather(place, wm_all, cm_right, cm_left, cm_recv)
    cube = CubeSum(place, small_all, slots, cube_send, cube_recv)
    blocks, rows, model = x_all.shape
    lanes = q_all.shape[1]
    width = 4 * lanes
    first = place.t * width + place.c * lanes
    first = pl.ds(pl.multiple_of(first, lanes), lanes)

    cube.start(0)
    swap_a.start()
    xs.start()
    swap_m.start()
    key_grad[...] = jnp.zeros_like(key_grad)
    value_grad[...] = jnp.zeros_like(value_grad)
    cube.finish(0)
    cube.start(1)
    cube.finish(1)
    cube.start(2)
    cube.finish(2)
    swap_a.finish()
    chain_a.start()
    cube.start(3)
    xs.second()
    dys.start()
    chain_a.step(1)
    swap_m.finish()
    chain_m.start()
    cube.finish(3)
    cube.start(4)
    chain_a.step(2)
    xs.third()
    cube.finish(4)
    xs.finish()

    def norm(at, carry):
        normed, _ = layer_norm_parts(x_all[at].astype(f32))
        first_norm[at] = (normed * small_all[0:1] + small_all[1:2]).astype(bf16)
        return carry

    lax.fori_loop(0, blocks, norm, 0)
    chain_a.step(3)

    def weights_of(j, count=1):
        return wa_all[:, :, :, j * lanes : (j + count) * lanes].reshape(model, count * lanes)

    def project(at, carry):
        here = pl.ds(pl.multiple_of(at * rows, rows), rows)
        both = jnp.dot(first_norm[at], weights_of(0, 3), preferred_element_type=f32)
        cos_here, sin_here = cosine[here], sine[here]
        parts = [both[:, j * lanes : (j + 1) * lanes] + small_all[6 + j : 7 + j, first] for j in range(3)]
        queries = turn_block(parts[0], cos_here, sin_here).astype(bf16)
        q_all[here] = (queries.astype(f32) * (HD ** (-0.5))).astype(bf16)
        k_all[here] = turn_block(parts[1], cos_here, sin_here).astype(bf16)
        v_all[here] = parts[2].astype(bf16)
        return carry

    lax.fori_loop(0, blocks, project, 0)
    dys.second()
    chain_m.step(1)
    dys.third()
    dys.finish()

    def back(at, carry):
        here = pl.ds(pl.multiple_of(at * rows, rows), rows)
        g_all[here] = jnp.dot(
            dy_all[at], weights_of(3), preferred_element_type=f32
        ).astype(bf16)
        return carry

    lax.fori_loop(0, blocks, back, 0)
    for at in range(blocks):
        here = pl.ds(at * rows, rows)
        mixed, query_grad = attention_rows(
            at, rows, q_all, k_all, v_all, g_all, scores, key_grad, value_grad
        )
        mixed_all[here] = mixed.astype(bf16)
        query_grad = query_grad.astype(bf16).astype(f32)
        query_grad = turn_block(query_grad, cosine[here], -sine[here])
        grads_all[here, 0:lanes] = query_grad.astype(bf16)
        flipped[0:lanes, here] = query_grad.T.astype(bf16)
        flipped[3 * lanes : 4 * lanes, here] = mixed.T.astype(bf16)
        if at == 4:
            chain_m.step(2)

    for at in range(blocks):
        here = pl.ds(at * rows, rows)
        turned = key_grad[:, here].T.astype(bf16).astype(f32)
        turned = turn_block(turned, cosine[here], -sine[here])
        grads_all[here, lanes : 2 * lanes] = turned.astype(bf16)
        flipped[lanes : 2 * lanes, here] = turned.T.astype(bf16)
        grads_all[here, 2 * lanes : 3 * lanes] = value_grad[:, here].T.astype(bf16)
        flipped[2 * lanes : 3 * lanes, here] = value_grad[:, here].astype(bf16)
    piece = model // 4
    for d in range(4):
        cols = slice(d * piece, (d + 1) * piece)
        normed = first_norm[:, :, cols].reshape(blocks * rows, piece)
        ga_all[d, 0 : 3 * lanes] = jnp.dot(
            flipped[0 : 3 * lanes], normed, preferred_element_type=f32
        ).astype(bf16)
        grads = dy_all[:, :, cols].reshape(blocks * rows, piece)
        ga_all[d, 3 * lanes :] = jnp.dot(
            flipped[3 * lanes :], grads, preferred_element_type=f32
        ).astype(bf16)
    chain_m.step(3)
    for part in (xs, dys, swap_a, swap_m, chain_a, chain_m):
        part.drain()


def gather_all(x_own, dy_own, wa_own, wm_own, small_own, cosine, sine):
    rows, model = x_own.shape
    n_ctx, depth, wide_a = wa_own.shape
    wide_m = wm_own.shape[2]
    seq_len, lanes = cosine.shape
    anywhere = pl.BlockSpec(memory_space=pl.ANY)
    vmem = pl.BlockSpec(memory_space=pltpu.VMEM)
    dma = pltpu.SemaphoreType.DMA
    return pl.pallas_call(
        gather_kernel,
        out_shape=(
            jax.ShapeDtypeStruct((8, rows, model), bf16),
            jax.ShapeDtypeStruct((8, rows, model), bf16),
            jax.ShapeDtypeStruct((4, n_ctx, depth, wide_a), bf16),
            jax.ShapeDtypeStruct((4, n_ctx, depth, wide_m), bf16),
            jax.ShapeDtypeStruct(small_own.shape, f32),
            jax.ShapeDtypeStruct((seq_len, lanes), bf16),
            jax.ShapeDtypeStruct((seq_len, 3 * lanes), bf16),
            jax.ShapeDtypeStruct((4, wide_a, model // 4), bf16),
        ),
        in_specs=[anywhere] * 4 + [vmem] * 3,
        out_specs=[vmem] * 3 + [anywhere] + [vmem] * 4,
        scratch_shapes=[
            pltpu.VMEM((5,) + small_own.shape, f32),
            pltpu.VMEM((8, rows, model), bf16),
            pltpu.VMEM((seq_len, lanes), bf16),
            pltpu.VMEM((seq_len, lanes), bf16),
            pltpu.VMEM((seq_len, lanes), bf16),
            pltpu.VMEM((seq_len, lanes), bf16),
            pltpu.VMEM((2 * rows, seq_len), f32),
            pltpu.VMEM((lanes, seq_len), f32),
            pltpu.VMEM((lanes, seq_len), f32),
            pltpu.VMEM((4 * lanes, seq_len), bf16),
        ]
        + [dma((8,))] * 4
        + [dma((3,))] * 4
        + [dma((4,))] * 6
        + [dma((5,))] * 2
        + [dma((4,))],
        compiler_params=pltpu.CompilerParams(
            collective_id=0, has_side_effects=True, vmem_limit_bytes=56 << 20
        ),
    )(x_own, dy_own, wa_own, wm_own, small_own, cosine, sine)


class PlaneReduce:
    def __init__(self, place, parts, came, low_in, high_in, x_in, y_in, sends, recvs):
        self.place, self.parts, self.came = place, parts, came
        self.low_in, self.high_in, self.x_in, self.y_in = low_in, high_in, x_in, y_in
        x, t, k = place.x, place.t, place.k
        half = parts.shape[1] // 2
        self.half = half
        self.first = []
        for at in range(4):
            src = parts.at[4 * (at // 2) + 2 * (1 - k) + at % 2]
            self.first.append(remote(src, came.at[at], sends, recvs, at, place.core))
        self.sends, self.recvs = sends, recvs
        self.own = 4 * x + 2 * k + t
        self.of_x = 4 * (1 - x) + 2 * k + t
        self.of_y = 4 * x + 2 * k + (1 - t)
        self.of_d = 4 * (1 - x) + 2 * k + (1 - t)
        self.low = remote(
            parts.at[self.of_d, pl.ds(0, half)], low_in, sends, recvs, 4, place.across_x
        )
        self.high = remote(
            parts.at[self.of_d, pl.ds(half, half)], high_in, sends, recvs, 5, place.across_y
        )
        self.to_x = remote(parts.at[self.of_x], x_in, sends, recvs, 6, place.across_x)
        self.to_y = remote(parts.at[self.of_y], y_in, sends, recvs, 7, place.across_y)

    def source(self, at, core):
        return 4 * (at // 2) + 2 * core + at % 2

    def start_one(self, at):
        src = self.parts.at[self.source(at, 1 - self.place.k)]
        remote(src, self.came.at[at], self.sends, self.recvs, at, self.place.core).start()

    def second(self):
        k = self.place.k
        for copy in self.first:
            copy.wait_recv()

        def add(at, carry):
            mine = self.parts[4 * (at // 2) + 2 * k + at % 2].astype(f32)
            here = 4 * (at // 2) + 2 * k + at % 2
            self.parts[here] = (mine + self.came[at].astype(f32)).astype(bf16)
            return carry

        lax.fori_loop(0, 4, add, 0)
        self.low.start()
        self.high.start()

    def third(self):
        half = self.half
        self.low.wait_recv()
        low, high = pl.ds(0, half), pl.ds(half, half)
        self.parts[self.of_y, low] = (
            self.parts[self.of_y, low].astype(f32) + self.low_in[...].astype(f32)
        ).astype(bf16)
        self.to_y.start()
        self.high.wait_recv()
        self.parts[self.of_x, high] = (
            self.parts[self.of_x, high].astype(f32) + self.high_in[...].astype(f32)
        ).astype(bf16)
        self.to_x.start()

    def finish(self):
        self.to_x.wait_recv()
        self.to_y.wait_recv()

    def total(self, rows):
        return (
            self.parts[self.own, rows].astype(f32)
            + self.x_in[rows].astype(f32)
            + self.y_in[rows].astype(f32)
        )

    def drain(self):
        for copy in self.first + [self.low, self.high, self.to_x, self.to_y]:
            copy.wait_send()


class ChainReduce:
    def __init__(self, place, parts, slots, sums, sends, recvs):
        self.s = place.s
        self.parts, self.slots, self.sums = parts, slots, sums

        def copy(src, d, slot, dev):
            return pltpu.make_async_remote_copy(
                src_ref=src,
                dst_ref=slots.at[slot],
                send_sem=sends.at[d],
                recv_sem=recvs.at[slot],
                device_id=dev,
                device_id_type=pl.DeviceIdType.MESH,
            )

        right, left = place.along(1), place.along(-1)
        self.to_right = lambda src, d: copy(src.at[d], d, d, right)
        self.to_left = lambda src, d, k: copy(src.at[d], d, 4 if k == 1 else d, left)

    def step(self, k):
        s = self.s

        def add(d):
            def one(at, carry):
                self.sums[d, at] = (
                    self.parts[d, at].astype(f32) + self.slots[d, at].astype(f32)
                ).astype(bf16)
                return carry

            lax.fori_loop(0, self.parts.shape[1], one, 0)

        @pl.when((s > 0) & (s + k <= 3))
        def _():
            self.to_right(self.parts, s + k).wait_recv()
            add(s + k)
            self.to_right(self.sums, s + k).start()

        @pl.when((s < 3) & (s - k >= 0))
        def _():
            self.to_left(self.parts, s - k, 2).wait_recv()
            add(s - k)
            self.to_left(self.sums, s - k, k).start()

    def edge(self, k):
        s = self.s

        @pl.when(s == 0)
        def _():
            self.to_right(self.parts, s + k).start()

        @pl.when(s == 3)
        def _():
            self.to_left(self.parts, s - k, k).start()

    def finish(self, out):
        s = self.s

        @pl.when(s > 0)
        def _():
            self.to_right(self.parts, s).wait_recv()

        @pl.when(s < 3)
        def _():
            self.to_left(self.parts, s, 1).wait_recv()


        def one(at, carry):
            out[at] = self.parts[s, at]

            @pl.when(s > 0)
            def _():
                out[at] = (out[at].astype(f32) + self.slots[s, at].astype(f32)).astype(bf16)

            @pl.when(s < 3)
            def _():
                out[at] = (out[at].astype(f32) + self.slots[4, at].astype(f32)).astype(bf16)

            return carry

        lax.fori_loop(0, self.parts.shape[1], one, 0)

    def drain(self):
        s = self.s
        for k in (3, 2, 1):

            @pl.when(s + k <= 3)
            def _():
                self.to_right(self.parts, s + k).wait_send()

            @pl.when(s - k >= 0)
            def _():
                self.to_left(self.parts, s - k, k).wait_send()


def turn_parts(flat, turned):
    pieces, rows, wide = flat.shape
    n_ctx, depth, _ = turned.shape
    for at in range(pieces):
        part = flat[at].astype(f32).T.astype(bf16)
        turned[:, :, at * rows : (at + 1) * rows] = part.reshape(n_ctx, depth, rows)


def far_first(s, at):
    d = jnp.where(s == 1, (3, 2, 0, 1)[at], (0, 1, 3, 2)[at])
    return jnp.where(s == 0, 3 - at, jnp.where(s == 3, at, d))


def reduce_kernel(
    x_all, dy_all, wa, wm, small, mixed_all, grads_all, ga,
    output, grad_in, g_qkv, g_out_t, g_up, g_down_t, vec_sum,
    second_norm, grad_pre_all, flipped, gm,
    po, po_came, po_low, po_high, po_x, po_y,
    ps, ps_came, ps_low, ps_high, ps_x, ps_y,
    ga_slots, ga_sums, ga_flat, ga_total, ga_back, gm_slots, gm_flat, gm_total, gm_back, slots,
    po_send, po_recv, ps_send, ps_recv, ga_send, ga_recv, gm_send, gm_recv,
    sa_send, sa_recv, sm_send, sm_recv, cube_send, cube_recv, local,
):
    place = Place()
    place.meet()
    cube = CubeSum(place, vec_sum, slots, cube_send, cube_recv)
    outs = PlaneReduce(place, po, po_came, po_low, po_high, po_x, po_y, po_send, po_recv)
    scaled = PlaneReduce(place, ps, ps_came, ps_low, ps_high, ps_x, ps_y, ps_send, ps_recv)
    chain_a = ChainReduce(place, ga, ga_slots, ga_sums, ga_send, ga_recv)
    chain_m = ChainReduce(place, gm, gm_slots, gm, gm_send, gm_recv)
    swap_a = CtxSwap(place, ga_total, ga_back, sa_send, sa_recv, local.at[0])
    swap_m = CtxSwap(place, gm_total, gm_back, sm_send, sm_recv, local.at[1])
    blocks, rows, model = x_all.shape
    lanes = ga.shape[2]
    units = grad_pre_all.shape[2]
    s, c, t = place.s, place.c, place.t
    for k in (3, 2, 1):
        chain_a.edge(k)
    vec_sum[...] = jnp.zeros_like(vec_sum)
    up_row = pl.ds(8 + 2 * t + c // 2, 1)
    up_cols = pl.ds(pl.multiple_of((c % 2) * units, units), units)
    in_up_row = pl.ds(9 + 2 * t + c // 2, 1)

    def up():
        return wm[:, :, :, 0:units].reshape(model, units)

    def down_t():
        return wm[:, :, :, units : 2 * units].reshape(model, units)

    def block_of(at):
        late = at // 4
        core = late * place.k + (1 - late) * (1 - place.k)
        return outs.source(at - 4 * late, core)

    def forward(at, carry):
        b = block_of(at)
        here = pl.ds(pl.multiple_of(b * rows, rows), rows)
        normed, _ = layer_norm_parts(x_all[b].astype(f32))
        second = (normed * small[2:3] + small[3:4]).astype(bf16)
        second_norm[b] = second
        pre = jnp.dot(second, up(), preferred_element_type=f32) + small[in_up_row, up_cols]
        phi = 0.5 * (1.0 + lax.erf(pre * 0.7071067811865476))
        hidden = (pre * phi).astype(bf16)
        flipped[units : 2 * units, here] = hidden.astype(f32).T.astype(bf16)
        slope = phi + pre * jnp.exp(-0.5 * pre * pre) * 0.3989422804014327
        grad_hidden = jnp.dot(dy_all[b], down_t(), preferred_element_type=f32)
        grad_pre = grad_hidden * slope
        flipped[0:units, here] = grad_pre.T.astype(bf16)
        grad_pre = grad_pre.astype(bf16)
        grad_pre_all[b] = grad_pre
        vec_sum[up_row, up_cols] += jnp.sum(grad_pre.astype(f32), 0, keepdims=True)
        out_t = wa[:, :, :, 3 * lanes :].reshape(model, lanes)
        po[b] = (
            contract_last(hidden, down_t()) + contract_last(mixed_all[here], out_t)
        ).astype(bf16)

        @pl.when(at < 4)
        def _():
            outs.start_one(at)

        @pl.when(at == 1)
        def _():
            chain_a.step(2)

        @pl.when(at == 4)
        def _():
            chain_a.step(1)

        @pl.when(at == 7)
        def _():
            chain_a.finish(ga_flat)
            turn_parts(ga_flat, ga_total)
            swap_a.start()

        return carry

    lax.fori_loop(0, blocks, forward, 0)
    outs.second()
    piece = model // 4
    for at in range(4):
        d = far_first(s, at)
        cols = pl.ds(pl.multiple_of(d * piece, piece), piece)
        normed = second_norm[:, :, cols].reshape(blocks * rows, piece)
        grads = dy_all[:, :, cols].reshape(blocks * rows, piece)
        half = gm.shape[1] // 2
        shape = (half,) + gm.shape[2:]
        gm[d, 0:half] = (
            jnp.dot(flipped[0:units], normed, preferred_element_type=f32)
            .astype(bf16)
            .reshape(shape)
        )
        gm[d, half:] = (
            jnp.dot(flipped[units:], grads, preferred_element_type=f32)
            .astype(bf16)
            .reshape(shape)
        )
        if at < 3:
            chain_m.edge(3 - at)
    outs.third()

    def backward(at, carry):
        b = block_of(at)
        here = pl.ds(pl.multiple_of(b * rows, rows), rows)
        normed, _ = layer_norm_parts(x_all[b].astype(f32))
        grad_second = contract_last(grad_pre_all[b], up())
        vec_sum[2:3] += jnp.sum(grad_second * normed, 0, keepdims=True)
        vec_sum[3:4] += jnp.sum(grad_second, 0, keepdims=True)
        w_qkv = wa[:, :, :, 0 : 3 * lanes].reshape(model, 3 * lanes)
        grad_first = contract_last(grads_all[here], w_qkv)
        vec_sum[0:1] += jnp.sum(grad_first * normed, 0, keepdims=True)
        vec_sum[1:2] += jnp.sum(grad_first, 0, keepdims=True)
        ps[b] = (grad_first * small[0:1] + grad_second * small[2:3]).astype(bf16)

        @pl.when(at < 4)
        def _():
            scaled.start_one(at)

        @pl.when(at == 3)
        def _():
            chain_m.step(2)

        return carry

    lax.fori_loop(0, blocks, backward, 0)
    vec_sum[4:5] = jnp.sum(dy_all[place.block].astype(f32), 0, keepdims=True)
    first = pl.ds(pl.multiple_of((4 * t + c) * lanes, lanes), lanes)
    for j in range(3):
        part = grads_all[:, j * lanes : (j + 1) * lanes].astype(f32)
        vec_sum[5 + j : 6 + j, first] = jnp.sum(part, 0, keepdims=True)
    cube.start(0)
    scaled.second()
    cube.finish(0)
    cube.start(1)
    outs.finish()
    chain_m.step(1)
    scaled.third()
    cube.finish(1)
    cube.start(2)
    step = 64
    mine = place.block

    def final_out(at, carry):
        here = pl.ds(pl.multiple_of(at * step, step), step)
        bias = small[4:5] + small[5:6]
        output[here] = (x_all[mine, here].astype(f32) + outs.total(here) + bias).astype(bf16)
        return carry

    lax.fori_loop(0, rows // step, final_out, 0)
    swap_a.finish()
    for at in range(4):
        cols = slice(at * lanes, (at + 1) * lanes)
        for j in range(3):
            g_qkv[j, :, cols] = ga_back[at, :, j * lanes : (j + 1) * lanes].astype(f32)
        g_out_t[:, cols] = ga_back[at, :, 3 * lanes :].astype(f32)
    cube.finish(2)
    cube.start(3)
    chain_m.finish(gm_flat)
    turn_parts(gm_flat, gm_total)
    swap_m.start()
    scaled.finish()
    cube.finish(3)
    cube.start(4)

    def final_in(at, carry):
        here = pl.ds(pl.multiple_of(at * step, step), step)
        normed, inv = layer_norm_parts(x_all[mine, here].astype(f32))
        part = scaled.total(here)
        inner = jnp.mean(part, -1, keepdims=True)
        aligned = jnp.mean(part * normed, -1, keepdims=True)
        grad_in[here] = dy_all[mine, here].astype(f32) + inv * (part - inner - normed * aligned)
        return carry

    lax.fori_loop(0, rows // step, final_in, 0)
    cube.finish(4)
    swap_m.finish()
    for at in range(4):
        cols = slice(at * units, (at + 1) * units)
        g_up[:, cols] = gm_back[at, :, :units].astype(f32)
        g_down_t[:, cols] = gm_back[at, :, units:].astype(f32)
    for part in (outs, scaled, chain_a, chain_m, swap_a, swap_m):
        part.drain()


def reduce_all(x_all, dy_all, wa, wm, small, mixed, grads, ga):
    blocks, rows, model = x_all.shape
    depth, wide_a = wa.shape[2:]
    wide_m = wm.shape[3]
    units, lanes = wide_m // 2, wide_a // 4
    seq_len = blocks * rows
    vmem = pl.BlockSpec(memory_space=pltpu.VMEM)
    dma = pltpu.SemaphoreType.DMA
    plane = [
        pltpu.VMEM((blocks, rows, model), bf16),
        pltpu.VMEM((4, rows, model), bf16),
        pltpu.VMEM((rows // 2, model), bf16),
        pltpu.VMEM((rows // 2, model), bf16),
        pltpu.VMEM((rows, model), bf16),
        pltpu.VMEM((rows, model), bf16),
    ]
    parts_a = ga.shape[1:]
    parts_m = (wide_m // lanes,) + ga.shape[2:]

    def swapped(wide):
        return [pltpu.VMEM((4, depth, wide), bf16)] * 2

    vec = (16, model)
    return pl.pallas_call(
        reduce_kernel,
        out_shape=(
            jax.ShapeDtypeStruct((rows, model), bf16),
            jax.ShapeDtypeStruct((rows, model), f32),
            jax.ShapeDtypeStruct((3, depth, wide_a), f32),
            jax.ShapeDtypeStruct((depth, wide_a), f32),
            jax.ShapeDtypeStruct((depth, 2 * wide_m), f32),
            jax.ShapeDtypeStruct((depth, 2 * wide_m), f32),
            jax.ShapeDtypeStruct(vec, f32),
        ),
        in_specs=[vmem] * 8,
        out_specs=[vmem] * 7,
        scratch_shapes=[
            pltpu.VMEM((blocks, rows, model), bf16),
            pltpu.VMEM((blocks, rows, units), bf16),
            pltpu.VMEM((wide_m, seq_len), bf16),
            pltpu.VMEM((4,) + parts_m, bf16),
        ]
        + plane
        + plane
        + [
            pltpu.VMEM((5,) + parts_a, bf16),
            pltpu.VMEM((4,) + parts_a, bf16),
            pltpu.VMEM(parts_a, bf16),
        ]
        + swapped(wide_a)
        + [pltpu.VMEM((5,) + parts_m, bf16), pltpu.VMEM(parts_m, bf16)]
        + swapped(wide_m)
        + [pltpu.VMEM((5,) + vec, f32)]
        + [dma((8,))] * 4
        + [dma((4,)), dma((5,))] * 2
        + [dma((3,))] * 4
        + [dma((5,))] * 2
        + [dma((2,))],
        compiler_params=pltpu.CompilerParams(
            collective_id=1, has_side_effects=True, vmem_limit_bytes=60 << 20
        ),
    )(x_all, dy_all, wa, wm, small, mixed, grads, ga)


def rotary_lanes(seq_len, lanes):
    half = ROT // 2
    inverse = rope_base ** (-np.arange(half) / half)
    angles = np.arange(seq_len)[:, None] * inverse[None, :]
    plain = np.zeros((seq_len, HD - ROT))
    cosine = np.concatenate([np.cos(angles), np.cos(angles), plain + 1], 1)
    sine = np.concatenate([-np.sin(angles), np.sin(angles), plain], 1)
    heads = lanes // HD
    return (
        jnp.asarray(np.tile(cosine, (1, heads)), f32),
        jnp.asarray(np.tile(sine, (1, heads)), f32),
    )


def turn_lanes(value, cosine, sine):
    lane = lax.broadcasted_iota(jnp.int32, value.shape, 1) % HD
    half = ROT // 2
    swapped = jnp.where(lane < half, jnp.roll(value, -half, 1), jnp.roll(value, half, 1))
    return value * cosine + swapped * sine


def per_device_plane(
    inputs, ln1_gain, ln1_bias, ln2_gain, ln2_bias, w_qkv, b_qkv, w_out, b_out,
    w_up, b_up, w_down, b_down, cotangent,
):
    s, c, t = (lax.axis_index(name) for name in ("shard", "ctx", "tensor"))
    n_ctx = 4
    group = 4 * s + c
    depth = w_up.shape[0]
    width = w_qkv.shape[2]
    units = w_up.shape[1]
    lanes, cols = width // n_ctx, units // n_ctx
    x_own, dy_own = inputs[0], cotangent[0]
    rows, model = x_own.shape
    seq_len = rows * 8

    six = jnp.stack([ln1_gain, ln1_bias, ln2_gain, ln2_bias, b_out, b_down]).astype(f32)
    slot = jnp.arange(32)[None, :, None]
    six = jnp.where(slot == 2 * group + t, six[:, None, :], 0.0).reshape(6, model)
    three = jnp.where(slot == 16 * t + group, b_qkv.astype(f32), 0.0).reshape(3, model)
    four = jnp.where(slot == 16 * t + group, b_up.astype(f32)[:, None, :], 0.0)
    four = four.reshape(-1, model)
    small_own = jnp.concatenate([six, three, four, jnp.zeros((3, model), f32)])

    first = jnp.concatenate([w_qkv, w_out.T[None]]).reshape(4, depth, n_ctx, lanes)
    first = first.transpose(2, 1, 0, 3).reshape(n_ctx, depth, 4 * lanes)
    second = jnp.stack([w_up, w_down.T]).reshape(2, depth, n_ctx, cols)
    second = second.transpose(2, 1, 0, 3).reshape(n_ctx, depth, 2 * cols)
    cosine, sine = rotary_lanes(seq_len, lanes)
    x_all, dy_all, first, second, small, mixed, grad_projected, ga = gather_all(
        x_own, dy_own, first, second, small_own, cosine, sine
    )
    output, grad_in, g_qkv, g_out_t, g_up, g_down_t, vec = reduce_all(
        x_all, dy_all, first, second, small, mixed, grad_projected,
        ga.reshape(4, 4, lanes, 4 * depth),
    )
    piece = model // 32
    five = lax.dynamic_slice(vec, (0, (2 * group + t) * piece), (5, piece))
    out_b_qkv = lax.dynamic_slice(vec, (5, width * t + piece * group), (3, piece))
    part = units // 16
    out_b_up = lax.dynamic_slice(vec[8:12].reshape(-1), (units * t + part * group,), (part,))
    return (
        output[None],
        grad_in[None],
        five[0],
        five[1],
        five[2],
        five[3],
        g_qkv,
        out_b_qkv[:, None],
        g_out_t.T,
        five[4],
        g_up,
        out_b_up[None],
        g_down_t.T,
        five[4],
    )


def fits_plane(mesh):
    return tuple(mesh.shape[name] for name in ("shard", "ctx", "tensor")) == (4, 4, 2)


def solution(mesh):
    placed = (
        P("shard", ("ctx", "tensor"), None),
        P(("shard", "ctx", "tensor")),
        P(("shard", "ctx", "tensor")),
        P(("shard", "ctx", "tensor")),
        P(("shard", "ctx", "tensor")),
        P(None, ("shard", "ctx"), "tensor"),
        P(None, "tensor", ("shard", "ctx")),
        P("tensor", ("shard", "ctx")),
        P(("shard", "ctx", "tensor")),
        P(("shard", "ctx"), "tensor"),
        P("tensor", ("shard", "ctx")),
        P("tensor", ("shard", "ctx")),
        P(("shard", "ctx", "tensor")),
        P("shard", ("ctx", "tensor"), None),
    )
    return jax.shard_map(
        per_device_plane if fits_plane(mesh) else per_device,
        mesh=mesh,
        in_specs=placed,
        out_specs=(
            P("shard", ("ctx", "tensor"), None),
            P("shard", ("ctx", "tensor"), None),
            P(("shard", "ctx", "tensor")),
            P(("shard", "ctx", "tensor")),
            P(("shard", "ctx", "tensor")),
            P(("shard", "ctx", "tensor")),
            P(None, ("shard", "ctx"), "tensor"),
            P(None, "tensor", ("shard", "ctx")),
            P("tensor", ("shard", "ctx")),
            P(("shard", "ctx", "tensor")),
            P(("shard", "ctx"), "tensor"),
            P("tensor", ("shard", "ctx")),
            P("tensor", ("shard", "ctx")),
            P(("shard", "ctx", "tensor")),
        ),
        check_vma=False,
    )
```

```python
import functools

import jax
import jax.numpy as jnp
import numpy as np
from jax import lax
from jax.experimental import pallas as pl
from jax.experimental.pallas import tpu as pltpu
from jax.sharding import PartitionSpec as P

HD = 64
ROT = 16


norm_eps = 1e-05
rope_base = 10000.0
bf16 = jnp.bfloat16
f32 = jnp.float32
GROUP = ("shard", "ctx")


def layer_norm_parts(values):
    centre = values - jnp.mean(values, -1, keepdims=True)
    spread = jnp.mean(centre * centre, -1, keepdims=True)
    inv_std = lax.rsqrt(spread + norm_eps)
    return (centre * inv_std, inv_std)


def rotary_tables(positions):
    half_dims = ROT // 2
    ladder = jnp.arange(half_dims, dtype=f32)
    inverse = jnp.exp(ladder * (-2.0 / ROT) * jnp.log(f32(rope_base)))
    angles = positions.astype(f32)[:, None] * inverse[None, :]
    angles = jnp.concatenate([angles, angles], -1)
    return (jnp.cos(angles)[:, None, :], jnp.sin(angles)[:, None, :])


def rotate(values, cosine, sine_table):
    rot_dims = cosine.shape[-1]
    half_dims = rot_dims // 2
    turned = values[..., :rot_dims]
    swapped = jnp.concatenate([-turned[..., half_dims:], turned[..., :half_dims]], -1)
    return jnp.concatenate([turned * cosine + swapped * sine_table, values[..., rot_dims:]], -1)


def gelu_slope(values):
    return (
        0.5 * (1.0 + lax.erf(values * 0.7071067811865476))
        + values * jnp.exp(-0.5 * values * values) * 0.3989422804014327
    )


def contract_last(left_side, right_side):
    return lax.dot_general(
        left_side, right_side, (((1,), (1,)), ((), ())), preferred_element_type=f32
    )


def contract_first(left_side, right_side):
    return lax.dot_general(
        left_side, right_side, (((0,), (0,)), ((), ())), preferred_element_type=f32
    )


def attention_kernel(lanes, wide, rows, in_ref, out_ref, key_grad, value_grad):
    seq_len = in_ref.shape[0]
    heads = lanes // HD
    parts = wide // rows
    scale = HD ** (-0.5)
    key_grad[...] = jnp.zeros_like(key_grad)
    value_grad[...] = jnp.zeros_like(value_grad)
    out_ref[...] = jnp.zeros_like(out_ref)
    for step in range(seq_len // wide):
        length = (step + 1) * wide

        def one_block(turn, carry, step=step, length=length):
            head = turn % heads
            start = pl.multiple_of(step * wide + (turn // heads) * rows, rows)
            here = pl.ds(start, rows)
            mine = lax.broadcasted_iota(jnp.int32, (rows, lanes), 1) // HD == head
            queries = in_ref[here, 0:lanes].astype(f32) * scale
            queries = jnp.where(mine, queries, 0.0).astype(bf16)
            grads = in_ref[here, 3 * lanes : 4 * lanes].astype(f32)
            grads = jnp.where(mine, grads, 0.0).astype(bf16)
            keys = in_ref[0:length, lanes : 2 * lanes]
            values = in_ref[0:length, 2 * lanes : 3 * lanes]
            scores = contract_last(queries, keys)
            key_at = lax.broadcasted_iota(jnp.int32, scores.shape, 1)
            query_at = start + lax.broadcasted_iota(jnp.int32, scores.shape, 0)
            scores = jnp.where(key_at <= query_at, scores, -1e30)
            exp_scores = jnp.exp(scores - jnp.max(scores, -1, keepdims=True))
            probs = exp_scores * (1.0 / jnp.sum(exp_scores, -1, keepdims=True))
            attn_prob = probs.astype(bf16)
            mixed = jnp.dot(attn_prob, values, preferred_element_type=f32)
            value_grad[0:length, :] += contract_first(attn_prob, grads)
            prob_grad = contract_last(grads, values)
            inner_sum = jnp.sum(probs * prob_grad, -1, keepdims=True)
            score_grad = (probs * (prob_grad - inner_sum)).astype(bf16)
            query_grad = jnp.dot(score_grad, keys, preferred_element_type=f32) * scale
            key_grad[0:length, :] += contract_first(score_grad, queries)
            out_ref[here, 0:lanes] = jnp.where(
                mine, mixed, out_ref[here, 0:lanes].astype(f32)
            ).astype(bf16)
            out_ref[here, lanes : 2 * lanes] = jnp.where(
                mine, query_grad, out_ref[here, lanes : 2 * lanes].astype(f32)
            ).astype(bf16)
            return carry

        lax.fori_loop(0, parts * heads, one_block, 0)
    out_ref[:, 2 * lanes : 3 * lanes] = key_grad[...].astype(bf16)
    out_ref[:, 3 * lanes : 4 * lanes] = value_grad[...].astype(bf16)


def attend(packed):
    seq_len, width = packed.shape
    lanes = width // 4
    wide = min(512, seq_len)
    rows = min(256, wide)
    return pl.pallas_call(
        functools.partial(attention_kernel, lanes, wide, rows),
        out_shape=jax.ShapeDtypeStruct((seq_len, width), bf16),
        in_specs=[pl.BlockSpec(memory_space=pltpu.VMEM)],
        out_specs=pl.BlockSpec(memory_space=pltpu.VMEM),
        scratch_shapes=[pltpu.VMEM((seq_len, lanes), f32), pltpu.VMEM((seq_len, lanes), f32)],
        compiler_params=pltpu.CompilerParams(vmem_limit_bytes=48 << 20),
        cost_estimate=pl.CostEstimate(
            flops=14 * seq_len * seq_len * lanes,
            bytes_accessed=4 * seq_len * width,
            transcendentals=seq_len * seq_len * lanes // HD,
        ),
    )(packed)


def per_device(
    inputs,
    ln1_gain,
    ln1_bias,
    ln2_gain,
    ln2_bias,
    w_qkv,
    b_qkv,
    w_out,
    b_out,
    w_up,
    b_up,
    w_down,
    b_down,
    cotangent,
):
    pair = lax.axis_index("tensor")
    first = pair == 0
    n_ctx = lax.axis_size("ctx")
    n_group = lax.axis_size("shard") * n_ctx
    swap = ((0, 1), (1, 0))

    def exchange(value):
        return lax.ppermute(value, "tensor", swap)

    def in_order(own, other, axis):
        return jnp.where(
            first,
            jnp.concatenate([own, other], axis),
            jnp.concatenate([other, own], axis),
        )

    small_own = jnp.stack([ln1_gain, ln1_bias, ln2_gain, ln2_bias, b_out, b_down])
    small = in_order(small_own, exchange(small_own), 1)
    piece = small.shape[1]
    depth = w_up.shape[0]
    ff_group = w_up.shape[1]
    width = w_qkv.shape[2]
    riders = jnp.concatenate([small.reshape(-1), b_qkv.reshape(-1), b_up.reshape(-1)])
    room = depth * 128
    riders = jnp.pad(riders, (0, room - riders.shape[0])).reshape(depth, 128)
    first_pack = jnp.concatenate([w_qkv[0], w_qkv[1], w_qkv[2], w_out.T, riders], 1)
    second_pack = jnp.concatenate([w_up, w_down.T], 1)
    first_whole = lax.all_gather(first_pack, GROUP, axis=0, tiled=True)
    second_whole = lax.all_gather(second_pack, GROUP, axis=0, tiled=True)
    model = first_whole.shape[0]
    whole_qkv = first_whole[:, : 3 * width]
    whole_out_t = first_whole[:, 3 * width : 4 * width]
    gathered = first_whole[:, 4 * width :].reshape(n_group, room).astype(f32)
    whole_up = second_whole[:, :ff_group]
    whole_down_t = second_whole[:, ff_group:]

    gain_one, shift_one, gain_two, shift_two, bias_out, bias_down = [
        gathered[:, at * piece : (at + 1) * piece].reshape(-1) for at in range(6)
    ]
    at = 6 * piece
    part = b_qkv.shape[2]
    bias_qkv = jnp.concatenate(
        [gathered[:, at + j * part : at + (j + 1) * part].reshape(-1) for j in range(3)]
    )
    at = at + 3 * part
    up_part = b_up.shape[1]
    bias_up = gathered[:, at : at + up_part].reshape(-1)

    both_own = jnp.concatenate([inputs, cotangent], 0)
    both = in_order(both_own, exchange(both_own), 1)
    grad_own = cotangent[0]
    own_rows = inputs[0].astype(f32)
    normed_own, inv_own = layer_norm_parts(own_rows)
    normed, _ = layer_norm_parts(both[0].astype(f32))
    grad_rows = both[1]
    first_norm = (normed * gain_one + shift_one).astype(bf16)
    second_norm = (normed * gain_two + shift_two).astype(bf16)
    block_len = first_norm.shape[0]
    half = block_len // 2

    def own_half(value):
        return jnp.where(first, value[:half], value[half:])

    def other_half(value):
        return jnp.where(first, value[half:], value[:half])

    positions = lax.axis_index("ctx") * block_len + jnp.arange(block_len, dtype=jnp.int32)
    cosine, sine_table = rotary_tables(positions)
    projected = jnp.dot(first_norm, whole_qkv, preferred_element_type=f32) + bias_qkv
    heads = width // HD

    def turned(value, sine):
        return (
            rotate(value.astype(f32).reshape(block_len, heads, HD), cosine, sine)
            .astype(bf16)
            .reshape(block_len, width)
        )

    queries = turned(projected[:, :width], sine_table)
    key_rows = turned(projected[:, width : 2 * width], sine_table)
    value_rows = projected[:, 2 * width :].astype(bf16)
    grad_mixed = jnp.dot(grad_rows, whole_out_t, preferred_element_type=f32).astype(bf16)
    lanes = width // n_ctx
    packed = jnp.stack([queries, key_rows, value_rows, grad_mixed])
    packed = packed.reshape(4, block_len, n_ctx, lanes).transpose(2, 1, 0, 3)
    packed = packed.reshape(n_ctx, block_len, 4 * lanes)
    there = lax.all_to_all(packed, "ctx", split_axis=0, concat_axis=0, tiled=True)

    hidden_pre = jnp.dot(second_norm, whole_up, preferred_element_type=f32) + bias_up
    hidden = jax.nn.gelu(hidden_pre, approximate=False).astype(bf16)
    feed_out = contract_last(hidden, whole_down_t)
    grad_hidden = jnp.dot(grad_rows, whole_down_t, preferred_element_type=f32)
    grad_pre = (grad_hidden * gelu_slope(hidden_pre)).astype(bf16)
    grad_up = contract_first(second_norm, grad_pre).astype(bf16)
    grad_down_t = contract_first(grad_rows, hidden).astype(bf16)
    second_grads = jnp.concatenate([grad_up, grad_down_t], 1)
    there, second_grads = lax.optimization_barrier((there, second_grads))
    second_sum = lax.psum_scatter(second_grads, GROUP, scatter_dimension=0, tiled=True)
    grad_b_up = jnp.sum(grad_pre, 0, dtype=f32)
    grad_second = contract_last(grad_pre, whole_up)

    attended = attend(there.reshape(n_ctx * block_len, 4 * lanes))
    back = lax.all_to_all(
        attended.reshape(n_ctx, block_len, 4 * lanes),
        "ctx",
        split_axis=0,
        concat_axis=0,
        tiled=True,
    )
    back = back.reshape(n_ctx, block_len, 4, lanes).transpose(2, 1, 0, 3)
    mixed_rows, query_back, key_back, value_back = back.reshape(4, block_len, width)
    grad_projected = jnp.concatenate(
        [turned(query_back, -sine_table), turned(key_back, -sine_table), value_back], 1
    )
    grad_qkv = contract_first(first_norm, grad_projected).astype(bf16)
    grad_out_t = contract_first(grad_rows, mixed_rows).astype(bf16)
    grad_b_qkv = jnp.sum(grad_projected, 0, dtype=f32)
    grad_first = contract_last(grad_projected, whole_qkv)

    vectors = jnp.stack(
        [
            jnp.sum(grad_first * normed, 0),
            jnp.sum(grad_first, 0),
            jnp.sum(grad_second * normed, 0),
            jnp.sum(grad_second, 0),
            jnp.sum(grad_own.astype(f32), 0),
        ]
    )
    back_riders = jnp.concatenate(
        [
            vectors.reshape(5, n_group, piece).transpose(1, 0, 2).reshape(n_group, -1),
            grad_b_qkv.reshape(3, n_group, part).transpose(1, 0, 2).reshape(n_group, -1),
            grad_b_up.reshape(n_group, up_part),
        ],
        1,
    )
    back_riders = jnp.pad(back_riders, ((0, 0), (0, room - back_riders.shape[1])))
    back_riders = back_riders.reshape(model, 128).astype(bf16)
    first_grads = jnp.concatenate([grad_qkv, grad_out_t, back_riders], 1)
    first_grads, second_sum = lax.optimization_barrier((first_grads, second_sum))
    first_sum = lax.psum_scatter(first_grads, GROUP, scatter_dimension=0, tiled=True)

    partial_sum = contract_last(mixed_rows, whole_out_t) + feed_out
    branches = own_half(partial_sum) + exchange(other_half(partial_sum).astype(bf16)).astype(f32)
    output = (own_rows + branches + bias_out + bias_down).astype(bf16)
    scaled = grad_first * gain_one + grad_second * gain_two
    scaled = own_half(scaled) + exchange(other_half(scaled).astype(bf16)).astype(f32)
    inner_sum = jnp.mean(scaled, -1, keepdims=True)
    aligned = jnp.mean(scaled * normed_own, -1, keepdims=True)
    grad_input = grad_own.astype(f32) + inv_own * (scaled - inner_sum - normed_own * aligned)

    second_sum = second_sum.astype(f32)
    first_sum = first_sum.astype(f32)
    grad_w_qkv = first_sum[:, : 3 * width].reshape(depth, 3, width).transpose(1, 0, 2)
    grad_w_out = first_sum[:, 3 * width : 4 * width].T
    summed = first_sum[:, 4 * width :].reshape(-1)
    vector_sum = summed[: 5 * piece].reshape(5, piece)
    own = piece // 2
    mine = jnp.where(first, vector_sum[:, :own], vector_sum[:, own:])
    theirs = jnp.where(first, vector_sum[:, own:], vector_sum[:, :own])
    vector_grads = mine + exchange(theirs)
    at = 5 * piece
    out_b_qkv = summed[at : at + 3 * part].reshape(3, 1, part)
    at = at + 3 * part
    out_b_up = summed[at : at + up_part].reshape(1, up_part)
    return (
        output[None],
        grad_input[None],
        vector_grads[0],
        vector_grads[1],
        vector_grads[2],
        vector_grads[3],
        grad_w_qkv,
        out_b_qkv,
        grad_w_out,
        vector_grads[4],
        second_sum[:, :ff_group],
        out_b_up,
        second_sum[:, ff_group:].T,
        vector_grads[4],
    )

def remote(src, dst, sends, recvs, at, to):
    return pltpu.make_async_remote_copy(
        src_ref=src,
        dst_ref=dst,
        send_sem=sends.at[at],
        recv_sem=recvs.at[at],
        device_id=to,
        device_id_type=pl.DeviceIdType.MESH,
    )


class Place:
    def __init__(self):
        self.s = lax.axis_index("shard")
        self.c = lax.axis_index("ctx")
        self.t = lax.axis_index("tensor")
        self.x = self.c // 2
        self.k = self.c % 2
        self.block = 2 * self.c + self.t
        self.core_c = 2 * self.x + (1 - self.k)
        self.x_c = 2 * (1 - self.x) + self.k
        self.far_c = 2 * (1 - self.x) + (1 - self.k)
        self.y_t = 1 - self.t
        self.core = {"ctx": self.core_c}
        self.across_x = {"ctx": self.x_c}
        self.far = {"ctx": self.far_c}
        self.across_y = {"tensor": self.y_t}

    def along(self, step):
        return {"shard": lax.rem(self.s + step + 4, 4)}

    def meet(self):
        barrier = pltpu.get_barrier_semaphore()
        others = [self.core, self.across_x, self.far, self.across_y]
        others += [self.along(step) for step in (1, 2, 3)]
        for other in others:
            pl.semaphore_signal(
                barrier, inc=1, device_id=other, device_id_type=pl.DeviceIdType.MESH
            )
        pl.semaphore_wait(barrier, len(others))

    def cube(self):
        pair = self.s + 1 - 2 * lax.rem(self.s, 2)
        return [
            self.core,
            {"shard": pair},
            self.along(2),
            self.across_x,
            self.across_y,
        ]


class PlaneGather:
    def __init__(self, place, own, full, sends, recvs, local):
        cut = own.shape[0] * 3 // 4
        b = place.block
        xb = 2 * place.x_c + place.t
        yb = 2 * place.c + place.y_t
        db = 2 * place.x_c + place.y_t
        low, high = pl.ds(0, cut), pl.ds(cut, own.shape[0] - cut)

        def to(src, dst, at, dev):
            return remote(src, dst, sends, recvs, at, dev)

        self.local = pltpu.make_async_copy(own, full.at[b], local)
        self.to_x = to(own, full.at[b], 0, place.across_x)
        self.to_y = to(own, full.at[b], 1, place.across_y)
        self.low_y = to(full.at[xb, low], full.at[xb, low], 2, place.across_y)
        self.high_x = to(full.at[yb, high], full.at[yb, high], 3, place.across_x)
        self.core_own = to(own, full.at[b], 4, place.core)
        self.core_x = to(full.at[xb], full.at[xb], 5, place.core)
        self.core_y = to(full.at[yb], full.at[yb], 6, place.core)
        self.core_d = to(full.at[db], full.at[db], 7, place.core)
        self.all = [
            self.to_x, self.to_y, self.low_y, self.high_x,
            self.core_own, self.core_x, self.core_y, self.core_d,
        ]

    def start(self):
        self.to_x.start()
        self.to_y.start()
        self.core_own.start()
        self.local.start()

    def second(self):
        self.to_x.wait_recv()
        self.low_y.start()
        self.core_x.start()
        self.to_y.wait_recv()
        self.high_x.start()
        self.core_y.start()

    def third(self):
        self.low_y.wait_recv()
        self.high_x.wait_recv()
        self.core_d.start()

    def finish(self):
        self.local.wait()
        for copy in (self.core_own, self.core_x, self.core_y, self.core_d):
            copy.wait_recv()

    def drain(self):
        for copy in self.all:
            copy.wait_send()


class CtxSwap:
    def __init__(self, place, own, dst, sends, recvs, local):
        c = place.c
        self.copies = []
        for at, (peer, dev) in enumerate(
            ((place.core_c, place.core), (place.x_c, place.across_x), (place.far_c, place.far))
        ):
            self.copies.append(remote(own.at[peer], dst.at[c], sends, recvs, at, dev))
        self.local = pltpu.make_async_copy(own.at[c], dst.at[c], local)

    def start(self):
        for copy in self.copies:
            copy.start()
        self.local.start()

    def finish(self):
        for copy in self.copies:
            copy.wait_recv()
        self.local.wait()

    def drain(self):
        for copy in self.copies:
            copy.wait_send()


class ChainGather:
    def __init__(self, place, full, right, left, recvs):
        self.s = place.s
        s = place.s

        def copy(j, sends, dev):
            return pltpu.make_async_remote_copy(
                src_ref=full.at[j],
                dst_ref=full.at[j],
                send_sem=sends.at[j],
                recv_sem=recvs.at[j],
                device_id=dev,
                device_id_type=pl.DeviceIdType.MESH,
            )

        self.to_right = lambda j: copy(j, right, place.along(1))
        self.to_left = lambda j: copy(j, left, place.along(-1))

    def start(self):
        s = self.s

        @pl.when(s < 3)
        def _():
            self.to_right(s).start()

        @pl.when(s > 0)
        def _():
            self.to_left(s).start()

    def step(self, distance):
        s = self.s

        @pl.when(s >= distance)
        def _():
            self.to_right(s - distance).wait_recv()

            @pl.when(s < 3)
            def _():
                self.to_right(s - distance).start()

        @pl.when(s + distance <= 3)
        def _():
            self.to_left(s + distance).wait_recv()

            @pl.when(s > 0)
            def _():
                self.to_left(s + distance).start()

    def drain(self):
        s = self.s
        for distance in range(4):

            @pl.when((s >= distance) & (s < 3))
            def _():
                self.to_right(s - distance).wait_send()

            @pl.when((s + distance <= 3) & (s > 0))
            def _():
                self.to_left(s + distance).wait_send()


class CubeSum:
    def __init__(self, place, total, slots, sends, recvs):
        self.total, self.slots = total, slots
        self.copies = [
            remote(total, slots.at[at], sends, recvs, at, dev)
            for at, dev in enumerate(place.cube())
        ]

    def start(self, at):
        self.copies[at].start()

    def finish(self, at):
        self.copies[at].wait()
        self.total[...] += self.slots[at]


def half_mask(rows, lanes, head):
    lane = lax.broadcasted_iota(jnp.int32, (rows, lanes), 1)
    return (lane < HD) if head == 0 else (lane >= HD)


def stack_heads(value):
    rows, lanes = value.shape
    parts = [jnp.where(half_mask(rows, lanes, head), value, 0.0) for head in range(2)]
    return jnp.concatenate(parts, 0)


def join_heads(value):
    rows, lanes = value.shape[0] // 2, value.shape[1]
    return jnp.where(half_mask(rows, lanes, 0), value[:rows], value[rows:])


def turn_block(value, cosine, sine):
    lanes = value.shape[1]
    lane = lax.broadcasted_iota(jnp.int32, value.shape, 1) % HD
    half = ROT // 2
    up = pltpu.roll(value, lanes - half, 1)
    down = pltpu.roll(value, half, 1)
    return value * cosine + jnp.where(lane < half, up, down) * sine


def attention_rows(at, rows, q_all, k_all, v_all, g_all, scores, key_grad, value_grad):
    length = (at + 1) * rows
    here = pl.ds(at * rows, rows)
    seen = pl.ds(0, length)
    queries = stack_heads(q_all[here].astype(f32)).astype(bf16)
    scores[:, seen] = contract_last(queries, k_all[seen])
    edge = pl.ds(at * rows, rows)
    key_at = lax.broadcasted_iota(jnp.int32, (rows, rows), 1)
    query_at = lax.broadcasted_iota(jnp.int32, (rows, rows), 0)
    keep = key_at <= query_at
    for head in range(2):
        part = pl.ds(head * rows, rows)
        scores[part, edge] = jnp.where(keep, scores[part, edge], -1e30)
    top = jnp.max(scores[:, seen], -1, keepdims=True)
    weights = jnp.exp(scores[:, seen] - top)
    scores[:, seen] = weights
    inverse = 1.0 / jnp.sum(weights, -1, keepdims=True)
    low = weights.astype(bf16)
    mixed = jnp.dot(low, v_all[seen], preferred_element_type=f32) * inverse
    grads = (stack_heads(g_all[here].astype(f32)) * inverse).astype(bf16)
    inner = jnp.sum(grads.astype(f32) * mixed, -1, keepdims=True)
    value_grad[:, seen] += contract_first(grads, low)
    prob_grad = contract_last(grads, v_all[seen])
    score_grad = (scores[:, seen] * (prob_grad - inner)).astype(bf16)
    key_grad[:, seen] += contract_first(queries, score_grad)
    query_grad = jnp.dot(score_grad, k_all[seen], preferred_element_type=f32)
    return join_heads(mixed), join_heads(query_grad) * (HD ** (-0.5))


def pack_weights(w_qkv, w_out, w_up, w_down, wa_own, wm_own):
    n_ctx, _, wide_a = wa_own.shape
    lanes, units = wide_a // 4, wm_own.shape[2] // 2
    for at in range(n_ctx):
        cols = slice(at * lanes, (at + 1) * lanes)
        for j in range(3):
            wa_own[at, :, j * lanes : (j + 1) * lanes] = w_qkv[j, :, cols]
        wa_own[at, :, 3 * lanes :] = w_out[:, cols]
        cols = slice(at * units, (at + 1) * units)
        wm_own[at, :, :units] = w_up[:, cols]
        wm_own[at, :, units:] = w_down[:, cols]


def place_vectors(place, nine, b_up, small):
    model = small.shape[1]
    group = 4 * place.s + place.c
    part = nine.shape[1]
    four = jnp.concatenate([nine[...]] * (128 // part), 1)
    spread = jnp.concatenate([four] * (model // 128), 1)
    slot = lax.broadcasted_iota(jnp.int32, spread.shape, 1) // part
    row = lax.broadcasted_iota(jnp.int32, spread.shape, 0)
    owner = jnp.where(row < 6, 2 * group + place.t, 16 * place.t + group)
    small[0:9] = jnp.where(slot == owner, spread, 0.0)
    width = b_up.shape[1]
    spread = jnp.concatenate([b_up[...].astype(f32)] * (model // width), 1)
    shape = (4, model)
    slot = lax.broadcasted_iota(jnp.int32, shape, 1) // width
    slot = slot + lax.broadcasted_iota(jnp.int32, shape, 0) * (model // width)
    small[9:13] = jnp.where(slot == 16 * place.t + group, spread, 0.0)
    small[13:16] = jnp.zeros((3, model), f32)


def gather_kernel(
    x_own, dy_own, w_qkv, w_out, w_up, w_down, nine, b_up, cosine, sine,
    x_out, dy_out, wa_all, wm_all, small_all, mixed_all, grads_all, ga_all,
    x_all, dy_all, wa_own, wm_own, slots, first_norm, q_all, k_all, v_all, g_all, scores, key_grad, value_grad, flipped,
    x_send, x_recv, dy_send, dy_recv, wa_send, wa_recv, wm_send, wm_recv,
    ca_right, ca_left, ca_recv, cm_right, cm_left, cm_recv, cube_send, cube_recv, local,
):
    place = Place()
    pack_weights(w_qkv, w_out, w_up, w_down, wa_own, wm_own)
    place_vectors(place, nine, b_up, small_all)
    place.meet()
    xs = PlaneGather(place, x_own, x_all, x_send, x_recv, local.at[0])
    dys = PlaneGather(place, dy_own, dy_all, dy_send, dy_recv, local.at[1])
    swap_a = CtxSwap(place, wa_own, wa_all.at[place.s], wa_send, wa_recv, local.at[2])
    swap_m = CtxSwap(place, wm_own, wm_all.at[place.s], wm_send, wm_recv, local.at[3])
    chain_a = ChainGather(place, wa_all, ca_right, ca_left, ca_recv)
    chain_m = ChainGather(place, wm_all, cm_right, cm_left, cm_recv)
    cube = CubeSum(place, small_all, slots, cube_send, cube_recv)
    blocks, rows, model = x_all.shape
    lanes = q_all.shape[1]
    width = 4 * lanes
    first = place.t * width + place.c * lanes
    first = pl.ds(pl.multiple_of(first, lanes), lanes)

    cube.start(0)
    swap_a.start()
    xs.start()
    swap_m.start()
    key_grad[...] = jnp.zeros_like(key_grad)
    value_grad[...] = jnp.zeros_like(value_grad)
    cube.finish(0)
    cube.start(1)
    cube.finish(1)
    cube.start(2)
    cube.finish(2)
    swap_a.finish()
    chain_a.start()
    cube.start(3)
    xs.second()
    dys.start()
    chain_a.step(1)
    swap_m.finish()
    chain_m.start()
    cube.finish(3)
    cube.start(4)
    chain_a.step(2)
    xs.third()
    cube.finish(4)
    xs.finish()
    save_x = pltpu.make_async_copy(x_all, x_out, local.at[4])
    save_x.start()

    def norm(at, carry):
        normed, _ = layer_norm_parts(x_all[at].astype(f32))
        first_norm[at] = (normed * small_all[0:1] + small_all[1:2]).astype(bf16)
        return carry

    lax.fori_loop(0, blocks, norm, 0)
    dys.second()
    chain_a.step(3)

    def weights_of(j, count=1):
        return wa_all[:, :, :, j * lanes : (j + count) * lanes].reshape(model, count * lanes)

    def project(at, carry):
        here = pl.ds(pl.multiple_of(at * rows, rows), rows)
        both = jnp.dot(first_norm[at], weights_of(0, 3), preferred_element_type=f32)
        cos_here, sin_here = cosine[here], sine[here]
        parts = [both[:, j * lanes : (j + 1) * lanes] + small_all[6 + j : 7 + j, first] for j in range(3)]
        queries = turn_block(parts[0], cos_here, sin_here).astype(bf16)
        q_all[here] = (queries.astype(f32) * (HD ** (-0.5))).astype(bf16)
        k_all[here] = turn_block(parts[1], cos_here, sin_here).astype(bf16)
        v_all[here] = parts[2].astype(bf16)
        return carry

    lax.fori_loop(0, blocks, project, 0)
    dys.third()
    chain_m.step(1)
    dys.finish()
    save_dy = pltpu.make_async_copy(dy_all, dy_out, local.at[5])
    save_dy.start()

    def back(at, carry):
        here = pl.ds(pl.multiple_of(at * rows, rows), rows)
        g_all[here] = jnp.dot(
            dy_all[at], weights_of(3), preferred_element_type=f32
        ).astype(bf16)
        return carry

    lax.fori_loop(0, blocks, back, 0)
    for at in range(blocks):
        here = pl.ds(at * rows, rows)
        mixed, query_grad = attention_rows(
            at, rows, q_all, k_all, v_all, g_all, scores, key_grad, value_grad
        )
        mixed_all[here] = mixed.astype(bf16)
        query_grad = query_grad.astype(bf16).astype(f32)
        query_grad = turn_block(query_grad, cosine[here], -sine[here])
        grads_all[here, 0:lanes] = query_grad.astype(bf16)
        flipped[0:lanes, here] = query_grad.T.astype(bf16)
        flipped[3 * lanes : 4 * lanes, here] = mixed.T.astype(bf16)
        if at == 3:
            chain_m.step(2)

    for at in range(blocks):
        here = pl.ds(at * rows, rows)
        turned = key_grad[:, here].T.astype(bf16).astype(f32)
        turned = turn_block(turned, cosine[here], -sine[here])
        grads_all[here, lanes : 2 * lanes] = turned.astype(bf16)
        flipped[lanes : 2 * lanes, here] = turned.T.astype(bf16)
        grads_all[here, 2 * lanes : 3 * lanes] = value_grad[:, here].T.astype(bf16)
        flipped[2 * lanes : 3 * lanes, here] = value_grad[:, here].astype(bf16)
    piece = model // 4
    for d in range(4):
        cols = slice(d * piece, (d + 1) * piece)
        normed = first_norm[:, :, cols].reshape(blocks * rows, piece)
        ga_all[d, 0 : 3 * lanes] = jnp.dot(
            flipped[0 : 3 * lanes], normed, preferred_element_type=f32
        ).astype(bf16)
        grads = dy_all[:, :, cols].reshape(blocks * rows, piece)
        ga_all[d, 3 * lanes :] = jnp.dot(
            flipped[3 * lanes :], grads, preferred_element_type=f32
        ).astype(bf16)
    chain_m.step(3)
    for part in (xs, dys, swap_a, swap_m, chain_a, chain_m):
        part.drain()
    save_x.wait()
    save_dy.wait()


def gather_all(x_own, dy_own, w_qkv, w_out, w_up, w_down, nine, b_up, cosine, sine):
    rows, model = x_own.shape
    depth = w_up.shape[0]
    n_ctx = 4
    wide_a = 4 * w_out.shape[1] // n_ctx
    wide_m = 2 * w_down.shape[1] // n_ctx
    seq_len, lanes = cosine.shape
    anywhere = pl.BlockSpec(memory_space=pl.ANY)
    vmem = pl.BlockSpec(memory_space=pltpu.VMEM)
    dma = pltpu.SemaphoreType.DMA
    return pl.pallas_call(
        gather_kernel,
        out_shape=(
            jax.ShapeDtypeStruct((8, rows, model), bf16),
            jax.ShapeDtypeStruct((8, rows, model), bf16),
            jax.ShapeDtypeStruct((4, n_ctx, depth, wide_a), bf16),
            jax.ShapeDtypeStruct((4, n_ctx, depth, wide_m), bf16),
            jax.ShapeDtypeStruct((16, model), f32),
            jax.ShapeDtypeStruct((seq_len, lanes), bf16),
            jax.ShapeDtypeStruct((seq_len, 3 * lanes), bf16),
            jax.ShapeDtypeStruct((4, wide_a, model // 4), bf16),
        ),
        in_specs=[anywhere] * 2 + [vmem] * 8,
        out_specs=[anywhere] * 2 + [vmem] * 6,
        scratch_shapes=[
            pltpu.VMEM((8, rows, model), bf16),
            pltpu.VMEM((8, rows, model), bf16),
            pltpu.VMEM((n_ctx, depth, wide_a), bf16),
            pltpu.VMEM((n_ctx, depth, wide_m), bf16),
            pltpu.VMEM((5, 16, model), f32),
            pltpu.VMEM((8, rows, model), bf16),
            pltpu.VMEM((seq_len, lanes), bf16),
            pltpu.VMEM((seq_len, lanes), bf16),
            pltpu.VMEM((seq_len, lanes), bf16),
            pltpu.VMEM((seq_len, lanes), bf16),
            pltpu.VMEM((2 * rows, seq_len), f32),
            pltpu.VMEM((lanes, seq_len), f32),
            pltpu.VMEM((lanes, seq_len), f32),
            pltpu.VMEM((4 * lanes, seq_len), bf16),
        ]
        + [dma((8,))] * 4
        + [dma((3,))] * 4
        + [dma((4,))] * 6
        + [dma((5,))] * 2
        + [dma((6,))],
        compiler_params=pltpu.CompilerParams(
            collective_id=0, has_side_effects=True, vmem_limit_bytes=56 << 20
        ),
    )(x_own, dy_own, w_qkv, w_out, w_up, w_down, nine, b_up, cosine, sine)


class PlaneReduce:
    def __init__(self, place, parts, came, low_in, high_in, x_in, y_in, sends, recvs):
        self.place, self.parts, self.came = place, parts, came
        self.low_in, self.high_in, self.x_in, self.y_in = low_in, high_in, x_in, y_in
        x, t, k = place.x, place.t, place.k
        half = parts.shape[1] // 2
        self.half = half
        self.first = []
        for at in range(4):
            src = parts.at[4 * (at // 2) + 2 * (1 - k) + at % 2]
            self.first.append(remote(src, came.at[at], sends, recvs, at, place.core))
        self.sends, self.recvs = sends, recvs
        self.own = 4 * x + 2 * k + t
        self.of_x = 4 * (1 - x) + 2 * k + t
        self.of_y = 4 * x + 2 * k + (1 - t)
        self.of_d = 4 * (1 - x) + 2 * k + (1 - t)
        self.low = remote(
            parts.at[self.of_d, pl.ds(0, half)], low_in, sends, recvs, 4, place.across_x
        )
        self.high = remote(
            parts.at[self.of_d, pl.ds(half, half)], high_in, sends, recvs, 5, place.across_y
        )
        self.to_x = remote(parts.at[self.of_x], x_in, sends, recvs, 6, place.across_x)
        self.to_y = remote(parts.at[self.of_y], y_in, sends, recvs, 7, place.across_y)

    def source(self, at, core):
        return 4 * (at // 2) + 2 * core + at % 2

    def start_one(self, at):
        src = self.parts.at[self.source(at, 1 - self.place.k)]
        remote(src, self.came.at[at], self.sends, self.recvs, at, self.place.core).start()

    def second(self):
        k = self.place.k
        for copy in self.first:
            copy.wait_recv()

        def add(at, carry):
            mine = self.parts[4 * (at // 2) + 2 * k + at % 2].astype(f32)
            here = 4 * (at // 2) + 2 * k + at % 2
            self.parts[here] = (mine + self.came[at].astype(f32)).astype(bf16)
            return carry

        lax.fori_loop(0, 4, add, 0)
        self.low.start()
        self.high.start()

    def third(self):
        half = self.half
        self.low.wait_recv()
        low, high = pl.ds(0, half), pl.ds(half, half)
        self.parts[self.of_y, low] = (
            self.parts[self.of_y, low].astype(f32) + self.low_in[...].astype(f32)
        ).astype(bf16)
        self.to_y.start()
        self.high.wait_recv()
        self.parts[self.of_x, high] = (
            self.parts[self.of_x, high].astype(f32) + self.high_in[...].astype(f32)
        ).astype(bf16)
        self.to_x.start()

    def finish(self):
        self.to_x.wait_recv()
        self.to_y.wait_recv()

    def total(self, rows):
        return (
            self.parts[self.own, rows].astype(f32)
            + self.x_in[rows].astype(f32)
            + self.y_in[rows].astype(f32)
        )

    def drain(self):
        for copy in self.first + [self.low, self.high, self.to_x, self.to_y]:
            copy.wait_send()


class ChainReduce:
    def __init__(self, place, parts, slots, sums, sends, recvs):
        self.s = place.s
        self.parts, self.slots, self.sums = parts, slots, sums

        def copy(src, d, slot, dev):
            return pltpu.make_async_remote_copy(
                src_ref=src,
                dst_ref=slots.at[slot],
                send_sem=sends.at[d],
                recv_sem=recvs.at[slot],
                device_id=dev,
                device_id_type=pl.DeviceIdType.MESH,
            )

        right, left = place.along(1), place.along(-1)
        self.to_right = lambda src, d: copy(src.at[d], d, d, right)
        self.to_left = lambda src, d, k: copy(src.at[d], d, 4 if k == 1 else d, left)

    def step(self, k):
        s = self.s

        def add(d):
            def one(at, carry):
                self.sums[d, at] = (
                    self.parts[d, at].astype(f32) + self.slots[d, at].astype(f32)
                ).astype(bf16)
                return carry

            lax.fori_loop(0, self.parts.shape[1], one, 0)

        @pl.when((s > 0) & (s + k <= 3))
        def _():
            self.to_right(self.parts, s + k).wait_recv()
            add(s + k)
            self.to_right(self.sums, s + k).start()

        @pl.when((s < 3) & (s - k >= 0))
        def _():
            self.to_left(self.parts, s - k, 2).wait_recv()
            add(s - k)
            self.to_left(self.sums, s - k, k).start()

    def edge(self, k):
        s = self.s

        @pl.when(s == 0)
        def _():
            self.to_right(self.parts, s + k).start()

        @pl.when(s == 3)
        def _():
            self.to_left(self.parts, s - k, k).start()

    def finish(self, out):
        s = self.s

        @pl.when(s > 0)
        def _():
            self.to_right(self.parts, s).wait_recv()

        @pl.when(s < 3)
        def _():
            self.to_left(self.parts, s, 1).wait_recv()


        def one(at, carry):
            out[at] = self.parts[s, at]

            @pl.when(s > 0)
            def _():
                out[at] = (out[at].astype(f32) + self.slots[s, at].astype(f32)).astype(bf16)

            @pl.when(s < 3)
            def _():
                out[at] = (out[at].astype(f32) + self.slots[4, at].astype(f32)).astype(bf16)

            return carry

        lax.fori_loop(0, self.parts.shape[1], one, 0)

    def drain(self):
        s = self.s
        for k in (3, 2, 1):

            @pl.when(s + k <= 3)
            def _():
                self.to_right(self.parts, s + k).wait_send()

            @pl.when(s - k >= 0)
            def _():
                self.to_left(self.parts, s - k, k).wait_send()


def turn_parts(flat, turned):
    pieces, rows, wide = flat.shape
    n_ctx, depth, _ = turned.shape
    for at in range(pieces):
        part = flat[at].astype(f32).T.astype(bf16)
        turned[:, :, at * rows : (at + 1) * rows] = part.reshape(n_ctx, depth, rows)


def far_first(s, at):
    d = jnp.where(s == 1, (3, 2, 0, 1)[at], (0, 1, 3, 2)[at])
    return jnp.where(s == 0, 3 - at, jnp.where(s == 3, at, d))


def reduce_kernel(
    x_all, dy_all, wa, wm, small, mixed_all, grads_all, ga,
    output, grad_in, ga_back, gm_back, vec_sum,
    second_norm, grad_pre_all, flipped, gm,
    po, po_came, po_low, po_high, po_x, po_y,
    ps, ps_came, ps_low, ps_high, ps_x, ps_y,
    ga_slots, ga_sums, ga_flat, ga_total, gm_slots, gm_flat, gm_total, slots,
    po_send, po_recv, ps_send, ps_recv, ga_send, ga_recv, gm_send, gm_recv,
    sa_send, sa_recv, sm_send, sm_recv, cube_send, cube_recv, local,
):
    place = Place()
    place.meet()
    cube = CubeSum(place, vec_sum, slots, cube_send, cube_recv)
    outs = PlaneReduce(place, po, po_came, po_low, po_high, po_x, po_y, po_send, po_recv)
    scaled = PlaneReduce(place, ps, ps_came, ps_low, ps_high, ps_x, ps_y, ps_send, ps_recv)
    chain_a = ChainReduce(place, ga, ga_slots, ga_sums, ga_send, ga_recv)
    chain_m = ChainReduce(place, gm, gm_slots, gm, gm_send, gm_recv)
    swap_a = CtxSwap(place, ga_total, ga_back, sa_send, sa_recv, local.at[0])
    swap_m = CtxSwap(place, gm_total, gm_back, sm_send, sm_recv, local.at[1])
    blocks, rows, model = x_all.shape
    lanes = ga.shape[2]
    units = grad_pre_all.shape[2]
    s, c, t = place.s, place.c, place.t
    for k in (3, 2, 1):
        chain_a.edge(k)
    vec_sum[...] = jnp.zeros_like(vec_sum)
    up_row = pl.ds(8 + 2 * t + c // 2, 1)
    up_cols = pl.ds(pl.multiple_of((c % 2) * units, units), units)
    in_up_row = pl.ds(9 + 2 * t + c // 2, 1)

    def up():
        return wm[:, :, :, 0:units].reshape(model, units)

    def down_t():
        return wm[:, :, :, units : 2 * units].reshape(model, units)

    def block_of(at):
        late = at // 4
        core = late * place.k + (1 - late) * (1 - place.k)
        return outs.source(at - 4 * late, core)

    def forward(at, carry):
        b = block_of(at)
        here = pl.ds(pl.multiple_of(b * rows, rows), rows)
        normed, _ = layer_norm_parts(x_all[b].astype(f32))
        second = (normed * small[2:3] + small[3:4]).astype(bf16)
        second_norm[b] = second
        pre = jnp.dot(second, up(), preferred_element_type=f32) + small[in_up_row, up_cols]
        phi = 0.5 * (1.0 + lax.erf(pre * 0.7071067811865476))
        hidden = (pre * phi).astype(bf16)
        flipped[units : 2 * units, here] = hidden.astype(f32).T.astype(bf16)
        slope = phi + pre * jnp.exp(-0.5 * pre * pre) * 0.3989422804014327
        grad_hidden = jnp.dot(dy_all[b], down_t(), preferred_element_type=f32)
        grad_pre = grad_hidden * slope
        flipped[0:units, here] = grad_pre.T.astype(bf16)
        grad_pre = grad_pre.astype(bf16)
        grad_pre_all[b] = grad_pre
        vec_sum[up_row, up_cols] += jnp.sum(grad_pre.astype(f32), 0, keepdims=True)
        out_t = wa[:, :, :, 3 * lanes :].reshape(model, lanes)
        po[b] = (
            contract_last(hidden, down_t()) + contract_last(mixed_all[here], out_t)
        ).astype(bf16)

        @pl.when(at < 4)
        def _():
            outs.start_one(at)

        @pl.when(at == 1)
        def _():
            chain_a.step(2)

        @pl.when(at == 4)
        def _():
            chain_a.step(1)

        @pl.when(at == 7)
        def _():
            chain_a.finish(ga_flat)
            turn_parts(ga_flat, ga_total)
            swap_a.start()

        return carry

    lax.fori_loop(0, blocks, forward, 0)
    outs.second()
    piece = model // 4
    for at in range(4):
        d = far_first(s, at)
        cols = pl.ds(pl.multiple_of(d * piece, piece), piece)
        normed = second_norm[:, :, cols].reshape(blocks * rows, piece)
        grads = dy_all[:, :, cols].reshape(blocks * rows, piece)
        half = gm.shape[1] // 2
        shape = (half,) + gm.shape[2:]
        gm[d, 0:half] = (
            jnp.dot(flipped[0:units], normed, preferred_element_type=f32)
            .astype(bf16)
            .reshape(shape)
        )
        gm[d, half:] = (
            jnp.dot(flipped[units:], grads, preferred_element_type=f32)
            .astype(bf16)
            .reshape(shape)
        )
        if at < 3:
            chain_m.edge(3 - at)
    outs.third()

    def backward(at, carry):
        b = block_of(at)
        here = pl.ds(pl.multiple_of(b * rows, rows), rows)
        normed, _ = layer_norm_parts(x_all[b].astype(f32))
        grad_second = contract_last(grad_pre_all[b], up())
        vec_sum[2:3] += jnp.sum(grad_second * normed, 0, keepdims=True)
        vec_sum[3:4] += jnp.sum(grad_second, 0, keepdims=True)
        w_qkv = wa[:, :, :, 0 : 3 * lanes].reshape(model, 3 * lanes)
        grad_first = contract_last(grads_all[here], w_qkv)
        vec_sum[0:1] += jnp.sum(grad_first * normed, 0, keepdims=True)
        vec_sum[1:2] += jnp.sum(grad_first, 0, keepdims=True)
        ps[b] = (grad_first * small[0:1] + grad_second * small[2:3]).astype(bf16)

        @pl.when(at < 4)
        def _():
            scaled.start_one(at)

        @pl.when(at == 3)
        def _():
            chain_m.step(2)

        return carry

    lax.fori_loop(0, blocks, backward, 0)
    vec_sum[4:5] = jnp.sum(dy_all[place.block].astype(f32), 0, keepdims=True)
    first = pl.ds(pl.multiple_of((4 * t + c) * lanes, lanes), lanes)
    for j in range(3):
        part = grads_all[:, j * lanes : (j + 1) * lanes].astype(f32)
        vec_sum[5 + j : 6 + j, first] = jnp.sum(part, 0, keepdims=True)
    cube.start(0)
    scaled.second()
    cube.finish(0)
    cube.start(1)
    outs.finish()
    cube.finish(1)
    cube.start(2)
    scaled.third()
    chain_m.step(1)
    step = 64
    mine = place.block

    def final_out(at, carry):
        here = pl.ds(pl.multiple_of(at * step, step), step)
        bias = small[4:5] + small[5:6]
        output[here] = (x_all[mine, here].astype(f32) + outs.total(here) + bias).astype(bf16)
        return carry

    lax.fori_loop(0, rows // step, final_out, 0)
    swap_a.finish()
    cube.finish(2)
    cube.start(3)
    chain_m.finish(gm_flat)
    turn_parts(gm_flat, gm_total)
    swap_m.start()
    scaled.finish()
    cube.finish(3)
    cube.start(4)

    def final_in(at, carry):
        here = pl.ds(pl.multiple_of(at * step, step), step)
        normed, inv = layer_norm_parts(x_all[mine, here].astype(f32))
        part = scaled.total(here)
        inner = jnp.mean(part, -1, keepdims=True)
        aligned = jnp.mean(part * normed, -1, keepdims=True)
        grad_in[here] = dy_all[mine, here].astype(f32) + inv * (part - inner - normed * aligned)
        return carry

    lax.fori_loop(0, rows // step, final_in, 0)
    cube.finish(4)
    swap_m.finish()
    for part in (outs, scaled, chain_a, chain_m, swap_a, swap_m):
        part.drain()


def reduce_all(x_all, dy_all, wa, wm, small, mixed, grads, ga):
    blocks, rows, model = x_all.shape
    depth, wide_a = wa.shape[2:]
    wide_m = wm.shape[3]
    units, lanes = wide_m // 2, wide_a // 4
    seq_len = blocks * rows
    vmem = pl.BlockSpec(memory_space=pltpu.VMEM)
    dma = pltpu.SemaphoreType.DMA
    plane = [
        pltpu.VMEM((blocks, rows, model), bf16),
        pltpu.VMEM((4, rows, model), bf16),
        pltpu.VMEM((rows // 2, model), bf16),
        pltpu.VMEM((rows // 2, model), bf16),
        pltpu.VMEM((rows, model), bf16),
        pltpu.VMEM((rows, model), bf16),
    ]
    parts_a = ga.shape[1:]
    parts_m = (wide_m // lanes,) + ga.shape[2:]

    def swapped(wide):
        return [pltpu.VMEM((4, depth, wide), bf16)]

    vec = (16, model)
    return pl.pallas_call(
        reduce_kernel,
        out_shape=(
            jax.ShapeDtypeStruct((rows, model), bf16),
            jax.ShapeDtypeStruct((rows, model), f32),
            jax.ShapeDtypeStruct((4, depth, wide_a), bf16),
            jax.ShapeDtypeStruct((4, depth, wide_m), bf16),
            jax.ShapeDtypeStruct(vec, f32),
        ),
        in_specs=[vmem] * 8,
        out_specs=[vmem] * 5,
        scratch_shapes=[
            pltpu.VMEM((blocks, rows, model), bf16),
            pltpu.VMEM((blocks, rows, units), bf16),
            pltpu.VMEM((wide_m, seq_len), bf16),
            pltpu.VMEM((4,) + parts_m, bf16),
        ]
        + plane
        + plane
        + [
            pltpu.VMEM((5,) + parts_a, bf16),
            pltpu.VMEM((4,) + parts_a, bf16),
            pltpu.VMEM(parts_a, bf16),
        ]
        + swapped(wide_a)
        + [pltpu.VMEM((5,) + parts_m, bf16), pltpu.VMEM(parts_m, bf16)]
        + swapped(wide_m)
        + [pltpu.VMEM((5,) + vec, f32)]
        + [dma((8,))] * 4
        + [dma((4,)), dma((5,))] * 2
        + [dma((3,))] * 4
        + [dma((5,))] * 2
        + [dma((2,))],
        compiler_params=pltpu.CompilerParams(
            collective_id=1, has_side_effects=True, vmem_limit_bytes=60 << 20
        ),
    )(x_all, dy_all, wa, wm, small, mixed, grads, ga)


def finish_kernel(
    output, grad_in, ga_back, gm_back, vec,
    output_out, grad_in_out, g_qkv, g_out, g_up, g_down,
    gain_one, shift_one, gain_two, shift_two, b_out, b_down, b_qkv, b_up,
):
    place = Place()
    output_out[...] = output[...]
    grad_in_out[...] = grad_in[...]
    lanes, units = ga_back.shape[2] // 4, gm_back.shape[2] // 2
    for at in range(ga_back.shape[0]):
        cols = slice(at * lanes, (at + 1) * lanes)
        for j in range(3):
            g_qkv[j, :, cols] = ga_back[at, :, j * lanes : (j + 1) * lanes].astype(f32)
        g_out[:, cols] = ga_back[at, :, 3 * lanes :].astype(f32)
        cols = slice(at * units, (at + 1) * units)
        g_up[:, cols] = gm_back[at, :, :units].astype(f32)
        g_down[:, cols] = gm_back[at, :, units:].astype(f32)
    model = vec.shape[1]
    part = b_out.shape[1]
    group = 4 * place.s + place.c
    start = part * (2 * group + place.t)
    shifted = pltpu.roll(vec[0:8], lax.rem(model - start, model), 1)
    for row, ref in enumerate((gain_one, shift_one, gain_two, shift_two, b_out)):
        ref[...] = shifted[row : row + 1, :part]
    b_down[...] = shifted[4:5, :part]
    start = part * (16 * place.t + group)
    shifted = pltpu.roll(vec[0:8], lax.rem(model - start, model), 1)
    for j in range(3):
        b_qkv[j] = shifted[5 + j : 6 + j, :part]
    width = b_up.shape[1]
    start = width * (16 * place.t + group)
    four = vec[8:12]
    row = lax.broadcasted_iota(jnp.int32, four.shape, 0)
    one = jnp.sum(jnp.where(row == start // model, four, 0.0), 0, keepdims=True)
    one = jnp.broadcast_to(one, (8, model))
    shifted = pltpu.roll(one, lax.rem(model - lax.rem(start, model), model), 1)
    b_up[...] = shifted[0:1, :width]


def finish_all(output, grad_in, ga_back, gm_back, vec, piece, part):
    n_ctx, depth, wide_a = ga_back.shape
    wide_m = gm_back.shape[2]
    vmem = pl.BlockSpec(memory_space=pltpu.VMEM)
    vector = jax.ShapeDtypeStruct((1, piece), f32)
    return pl.pallas_call(
        finish_kernel,
        out_shape=(
            jax.ShapeDtypeStruct(output.shape, output.dtype),
            jax.ShapeDtypeStruct(grad_in.shape, grad_in.dtype),
            jax.ShapeDtypeStruct((3, depth, n_ctx * wide_a // 4), f32),
            jax.ShapeDtypeStruct((depth, n_ctx * wide_a // 4), f32),
            jax.ShapeDtypeStruct((depth, n_ctx * wide_m // 2), f32),
            jax.ShapeDtypeStruct((depth, n_ctx * wide_m // 2), f32),
        )
        + (vector,) * 6
        + (
            jax.ShapeDtypeStruct((3, 1, piece), f32),
            jax.ShapeDtypeStruct((1, part), f32),
        ),
        in_specs=[vmem] * 5,
        out_specs=[vmem] * 14,
        compiler_params=pltpu.CompilerParams(vmem_limit_bytes=60 << 20),
    )(output, grad_in, ga_back, gm_back, vec)


def rotary_lanes(seq_len, lanes):
    half = ROT // 2
    inverse = rope_base ** (-np.arange(half) / half)
    angles = np.arange(seq_len)[:, None] * inverse[None, :]
    plain = np.zeros((seq_len, HD - ROT))
    cosine = np.concatenate([np.cos(angles), np.cos(angles), plain + 1], 1)
    sine = np.concatenate([-np.sin(angles), np.sin(angles), plain], 1)
    heads = lanes // HD
    return (
        jnp.asarray(np.tile(cosine, (1, heads)), f32),
        jnp.asarray(np.tile(sine, (1, heads)), f32),
    )


def turn_lanes(value, cosine, sine):
    lane = lax.broadcasted_iota(jnp.int32, value.shape, 1) % HD
    half = ROT // 2
    swapped = jnp.where(lane < half, jnp.roll(value, -half, 1), jnp.roll(value, half, 1))
    return value * cosine + swapped * sine


def per_device_plane(
    inputs, ln1_gain, ln1_bias, ln2_gain, ln2_bias, w_qkv, b_qkv, w_out, b_out,
    w_up, b_up, w_down, b_down, cotangent,
):
    x_own, dy_own = inputs[0], cotangent[0]
    rows, model = x_own.shape
    seq_len = rows * 8
    lanes = w_out.shape[0] // 4
    vectors = jnp.stack([ln1_gain, ln1_bias, ln2_gain, ln2_bias, b_out, b_down])
    nine = jnp.concatenate([vectors, b_qkv[:, 0]]).astype(f32)
    cosine, sine = rotary_lanes(seq_len, lanes)
    x_all, dy_all, first, second, small, mixed, grad_projected, ga = gather_all(
        x_own, dy_own, w_qkv, w_out.T, w_up, w_down.T, nine, b_up, cosine, sine
    )
    output, grad_in, ga_back, gm_back, vec = reduce_all(
        x_all, dy_all, first, second, small, mixed, grad_projected,
        ga.reshape(4, 4, lanes, model // 4),
    )
    output, grad_in, g_qkv, g_out, g_up, g_down, *vectors, g_b_qkv, g_b_up = finish_all(
        output, grad_in, ga_back, gm_back, vec, b_out.shape[0], b_up.shape[1]
    )
    g_one, s_one, g_two, s_two, g_b_out, g_b_down = (v.reshape(-1) for v in vectors)
    return (
        output[None], grad_in[None], g_one, s_one, g_two, s_two, g_qkv, g_b_qkv, g_out.T,
        g_b_out, g_up, g_b_up, g_down.T, g_b_down,
    )


def fits_plane(mesh):
    return tuple(mesh.shape[name] for name in ("shard", "ctx", "tensor")) == (4, 4, 2)


def solution(mesh):
    placed = (
        P("shard", ("ctx", "tensor"), None),
        P(("shard", "ctx", "tensor")),
        P(("shard", "ctx", "tensor")),
        P(("shard", "ctx", "tensor")),
        P(("shard", "ctx", "tensor")),
        P(None, ("shard", "ctx"), "tensor"),
        P(None, "tensor", ("shard", "ctx")),
        P("tensor", ("shard", "ctx")),
        P(("shard", "ctx", "tensor")),
        P(("shard", "ctx"), "tensor"),
        P("tensor", ("shard", "ctx")),
        P("tensor", ("shard", "ctx")),
        P(("shard", "ctx", "tensor")),
        P("shard", ("ctx", "tensor"), None),
    )
    return jax.shard_map(
        per_device_plane if fits_plane(mesh) else per_device,
        mesh=mesh,
        in_specs=placed,
        out_specs=(
            P("shard", ("ctx", "tensor"), None),
            P("shard", ("ctx", "tensor"), None),
            P(("shard", "ctx", "tensor")),
            P(("shard", "ctx", "tensor")),
            P(("shard", "ctx", "tensor")),
            P(("shard", "ctx", "tensor")),
            P(None, ("shard", "ctx"), "tensor"),
            P(None, "tensor", ("shard", "ctx")),
            P("tensor", ("shard", "ctx")),
            P(("shard", "ctx", "tensor")),
            P(("shard", "ctx"), "tensor"),
            P("tensor", ("shard", "ctx")),
            P("tensor", ("shard", "ctx")),
            P(("shard", "ctx", "tensor")),
        ),
        check_vma=False,
    )
```

```python
import functools

import jax
import jax.numpy as jnp
import numpy as np
from jax import lax
from jax.experimental import pallas as pl
from jax.experimental.pallas import tpu as pltpu
from jax.sharding import PartitionSpec as P

HD = 64
ROT = 16


norm_eps = 1e-05
rope_base = 10000.0
bf16 = jnp.bfloat16
f32 = jnp.float32
GROUP = ("shard", "ctx")


def layer_norm_parts(values):
    centre = values - jnp.mean(values, -1, keepdims=True)
    spread = jnp.mean(centre * centre, -1, keepdims=True)
    inv_std = lax.rsqrt(spread + norm_eps)
    return (centre * inv_std, inv_std)


def rotary_tables(positions):
    half_dims = ROT // 2
    ladder = jnp.arange(half_dims, dtype=f32)
    inverse = jnp.exp(ladder * (-2.0 / ROT) * jnp.log(f32(rope_base)))
    angles = positions.astype(f32)[:, None] * inverse[None, :]
    angles = jnp.concatenate([angles, angles], -1)
    return (jnp.cos(angles)[:, None, :], jnp.sin(angles)[:, None, :])


def rotate(values, cosine, sine_table):
    rot_dims = cosine.shape[-1]
    half_dims = rot_dims // 2
    turned = values[..., :rot_dims]
    swapped = jnp.concatenate([-turned[..., half_dims:], turned[..., :half_dims]], -1)
    return jnp.concatenate([turned * cosine + swapped * sine_table, values[..., rot_dims:]], -1)


def gelu_slope(values):
    return (
        0.5 * (1.0 + lax.erf(values * 0.7071067811865476))
        + values * jnp.exp(-0.5 * values * values) * 0.3989422804014327
    )


def contract_last(left_side, right_side):
    return lax.dot_general(
        left_side, right_side, (((1,), (1,)), ((), ())), preferred_element_type=f32
    )


def contract_first(left_side, right_side):
    return lax.dot_general(
        left_side, right_side, (((0,), (0,)), ((), ())), preferred_element_type=f32
    )


def attention_kernel(lanes, wide, rows, in_ref, out_ref, key_grad, value_grad):
    seq_len = in_ref.shape[0]
    heads = lanes // HD
    parts = wide // rows
    scale = HD ** (-0.5)
    key_grad[...] = jnp.zeros_like(key_grad)
    value_grad[...] = jnp.zeros_like(value_grad)
    out_ref[...] = jnp.zeros_like(out_ref)
    for step in range(seq_len // wide):
        length = (step + 1) * wide

        def one_block(turn, carry, step=step, length=length):
            head = turn % heads
            start = pl.multiple_of(step * wide + (turn // heads) * rows, rows)
            here = pl.ds(start, rows)
            mine = lax.broadcasted_iota(jnp.int32, (rows, lanes), 1) // HD == head
            queries = in_ref[here, 0:lanes].astype(f32) * scale
            queries = jnp.where(mine, queries, 0.0).astype(bf16)
            grads = in_ref[here, 3 * lanes : 4 * lanes].astype(f32)
            grads = jnp.where(mine, grads, 0.0).astype(bf16)
            keys = in_ref[0:length, lanes : 2 * lanes]
            values = in_ref[0:length, 2 * lanes : 3 * lanes]
            scores = contract_last(queries, keys)
            key_at = lax.broadcasted_iota(jnp.int32, scores.shape, 1)
            query_at = start + lax.broadcasted_iota(jnp.int32, scores.shape, 0)
            scores = jnp.where(key_at <= query_at, scores, -1e30)
            exp_scores = jnp.exp(scores - jnp.max(scores, -1, keepdims=True))
            probs = exp_scores * (1.0 / jnp.sum(exp_scores, -1, keepdims=True))
            attn_prob = probs.astype(bf16)
            mixed = jnp.dot(attn_prob, values, preferred_element_type=f32)
            value_grad[0:length, :] += contract_first(attn_prob, grads)
            prob_grad = contract_last(grads, values)
            inner_sum = jnp.sum(probs * prob_grad, -1, keepdims=True)
            score_grad = (probs * (prob_grad - inner_sum)).astype(bf16)
            query_grad = jnp.dot(score_grad, keys, preferred_element_type=f32) * scale
            key_grad[0:length, :] += contract_first(score_grad, queries)
            out_ref[here, 0:lanes] = jnp.where(
                mine, mixed, out_ref[here, 0:lanes].astype(f32)
            ).astype(bf16)
            out_ref[here, lanes : 2 * lanes] = jnp.where(
                mine, query_grad, out_ref[here, lanes : 2 * lanes].astype(f32)
            ).astype(bf16)
            return carry

        lax.fori_loop(0, parts * heads, one_block, 0)
    out_ref[:, 2 * lanes : 3 * lanes] = key_grad[...].astype(bf16)
    out_ref[:, 3 * lanes : 4 * lanes] = value_grad[...].astype(bf16)


def attend(packed):
    seq_len, width = packed.shape
    lanes = width // 4
    wide = min(512, seq_len)
    rows = min(256, wide)
    return pl.pallas_call(
        functools.partial(attention_kernel, lanes, wide, rows),
        out_shape=jax.ShapeDtypeStruct((seq_len, width), bf16),
        in_specs=[pl.BlockSpec(memory_space=pltpu.VMEM)],
        out_specs=pl.BlockSpec(memory_space=pltpu.VMEM),
        scratch_shapes=[pltpu.VMEM((seq_len, lanes), f32), pltpu.VMEM((seq_len, lanes), f32)],
        compiler_params=pltpu.CompilerParams(vmem_limit_bytes=48 << 20),
        cost_estimate=pl.CostEstimate(
            flops=14 * seq_len * seq_len * lanes,
            bytes_accessed=4 * seq_len * width,
            transcendentals=seq_len * seq_len * lanes // HD,
        ),
    )(packed)


def per_device(
    inputs,
    ln1_gain,
    ln1_bias,
    ln2_gain,
    ln2_bias,
    w_qkv,
    b_qkv,
    w_out,
    b_out,
    w_up,
    b_up,
    w_down,
    b_down,
    cotangent,
):
    pair = lax.axis_index("tensor")
    first = pair == 0
    n_ctx = lax.axis_size("ctx")
    n_group = lax.axis_size("shard") * n_ctx
    swap = ((0, 1), (1, 0))

    def exchange(value):
        return lax.ppermute(value, "tensor", swap)

    def in_order(own, other, axis):
        return jnp.where(
            first,
            jnp.concatenate([own, other], axis),
            jnp.concatenate([other, own], axis),
        )

    small_own = jnp.stack([ln1_gain, ln1_bias, ln2_gain, ln2_bias, b_out, b_down])
    small = in_order(small_own, exchange(small_own), 1)
    piece = small.shape[1]
    depth = w_up.shape[0]
    ff_group = w_up.shape[1]
    width = w_qkv.shape[2]
    riders = jnp.concatenate([small.reshape(-1), b_qkv.reshape(-1), b_up.reshape(-1)])
    room = depth * 128
    riders = jnp.pad(riders, (0, room - riders.shape[0])).reshape(depth, 128)
    first_pack = jnp.concatenate([w_qkv[0], w_qkv[1], w_qkv[2], w_out.T, riders], 1)
    second_pack = jnp.concatenate([w_up, w_down.T], 1)
    first_whole = lax.all_gather(first_pack, GROUP, axis=0, tiled=True)
    second_whole = lax.all_gather(second_pack, GROUP, axis=0, tiled=True)
    model = first_whole.shape[0]
    whole_qkv = first_whole[:, : 3 * width]
    whole_out_t = first_whole[:, 3 * width : 4 * width]
    gathered = first_whole[:, 4 * width :].reshape(n_group, room).astype(f32)
    whole_up = second_whole[:, :ff_group]
    whole_down_t = second_whole[:, ff_group:]

    gain_one, shift_one, gain_two, shift_two, bias_out, bias_down = [
        gathered[:, at * piece : (at + 1) * piece].reshape(-1) for at in range(6)
    ]
    at = 6 * piece
    part = b_qkv.shape[2]
    bias_qkv = jnp.concatenate(
        [gathered[:, at + j * part : at + (j + 1) * part].reshape(-1) for j in range(3)]
    )
    at = at + 3 * part
    up_part = b_up.shape[1]
    bias_up = gathered[:, at : at + up_part].reshape(-1)

    both_own = jnp.concatenate([inputs, cotangent], 0)
    both = in_order(both_own, exchange(both_own), 1)
    grad_own = cotangent[0]
    own_rows = inputs[0].astype(f32)
    normed_own, inv_own = layer_norm_parts(own_rows)
    normed, _ = layer_norm_parts(both[0].astype(f32))
    grad_rows = both[1]
    first_norm = (normed * gain_one + shift_one).astype(bf16)
    second_norm = (normed * gain_two + shift_two).astype(bf16)
    block_len = first_norm.shape[0]
    half = block_len // 2

    def own_half(value):
        return jnp.where(first, value[:half], value[half:])

    def other_half(value):
        return jnp.where(first, value[half:], value[:half])

    positions = lax.axis_index("ctx") * block_len + jnp.arange(block_len, dtype=jnp.int32)
    cosine, sine_table = rotary_tables(positions)
    projected = jnp.dot(first_norm, whole_qkv, preferred_element_type=f32) + bias_qkv
    heads = width // HD

    def turned(value, sine):
        return (
            rotate(value.astype(f32).reshape(block_len, heads, HD), cosine, sine)
            .astype(bf16)
            .reshape(block_len, width)
        )

    queries = turned(projected[:, :width], sine_table)
    key_rows = turned(projected[:, width : 2 * width], sine_table)
    value_rows = projected[:, 2 * width :].astype(bf16)
    grad_mixed = jnp.dot(grad_rows, whole_out_t, preferred_element_type=f32).astype(bf16)
    lanes = width // n_ctx
    packed = jnp.stack([queries, key_rows, value_rows, grad_mixed])
    packed = packed.reshape(4, block_len, n_ctx, lanes).transpose(2, 1, 0, 3)
    packed = packed.reshape(n_ctx, block_len, 4 * lanes)
    there = lax.all_to_all(packed, "ctx", split_axis=0, concat_axis=0, tiled=True)

    hidden_pre = jnp.dot(second_norm, whole_up, preferred_element_type=f32) + bias_up
    hidden = jax.nn.gelu(hidden_pre, approximate=False).astype(bf16)
    feed_out = contract_last(hidden, whole_down_t)
    grad_hidden = jnp.dot(grad_rows, whole_down_t, preferred_element_type=f32)
    grad_pre = (grad_hidden * gelu_slope(hidden_pre)).astype(bf16)
    grad_up = contract_first(second_norm, grad_pre).astype(bf16)
    grad_down_t = contract_first(grad_rows, hidden).astype(bf16)
    second_grads = jnp.concatenate([grad_up, grad_down_t], 1)
    there, second_grads = lax.optimization_barrier((there, second_grads))
    second_sum = lax.psum_scatter(second_grads, GROUP, scatter_dimension=0, tiled=True)
    grad_b_up = jnp.sum(grad_pre, 0, dtype=f32)
    grad_second = contract_last(grad_pre, whole_up)

    attended = attend(there.reshape(n_ctx * block_len, 4 * lanes))
    back = lax.all_to_all(
        attended.reshape(n_ctx, block_len, 4 * lanes),
        "ctx",
        split_axis=0,
        concat_axis=0,
        tiled=True,
    )
    back = back.reshape(n_ctx, block_len, 4, lanes).transpose(2, 1, 0, 3)
    mixed_rows, query_back, key_back, value_back = back.reshape(4, block_len, width)
    grad_projected = jnp.concatenate(
        [turned(query_back, -sine_table), turned(key_back, -sine_table), value_back], 1
    )
    grad_qkv = contract_first(first_norm, grad_projected).astype(bf16)
    grad_out_t = contract_first(grad_rows, mixed_rows).astype(bf16)
    grad_b_qkv = jnp.sum(grad_projected, 0, dtype=f32)
    grad_first = contract_last(grad_projected, whole_qkv)

    vectors = jnp.stack(
        [
            jnp.sum(grad_first * normed, 0),
            jnp.sum(grad_first, 0),
            jnp.sum(grad_second * normed, 0),
            jnp.sum(grad_second, 0),
            jnp.sum(grad_own.astype(f32), 0),
        ]
    )
    back_riders = jnp.concatenate(
        [
            vectors.reshape(5, n_group, piece).transpose(1, 0, 2).reshape(n_group, -1),
            grad_b_qkv.reshape(3, n_group, part).transpose(1, 0, 2).reshape(n_group, -1),
            grad_b_up.reshape(n_group, up_part),
        ],
        1,
    )
    back_riders = jnp.pad(back_riders, ((0, 0), (0, room - back_riders.shape[1])))
    back_riders = back_riders.reshape(model, 128).astype(bf16)
    first_grads = jnp.concatenate([grad_qkv, grad_out_t, back_riders], 1)
    first_grads, second_sum = lax.optimization_barrier((first_grads, second_sum))
    first_sum = lax.psum_scatter(first_grads, GROUP, scatter_dimension=0, tiled=True)

    partial_sum = contract_last(mixed_rows, whole_out_t) + feed_out
    branches = own_half(partial_sum) + exchange(other_half(partial_sum).astype(bf16)).astype(f32)
    output = (own_rows + branches + bias_out + bias_down).astype(bf16)
    scaled = grad_first * gain_one + grad_second * gain_two
    scaled = own_half(scaled) + exchange(other_half(scaled).astype(bf16)).astype(f32)
    inner_sum = jnp.mean(scaled, -1, keepdims=True)
    aligned = jnp.mean(scaled * normed_own, -1, keepdims=True)
    grad_input = grad_own.astype(f32) + inv_own * (scaled - inner_sum - normed_own * aligned)

    second_sum = second_sum.astype(f32)
    first_sum = first_sum.astype(f32)
    grad_w_qkv = first_sum[:, : 3 * width].reshape(depth, 3, width).transpose(1, 0, 2)
    grad_w_out = first_sum[:, 3 * width : 4 * width].T
    summed = first_sum[:, 4 * width :].reshape(-1)
    vector_sum = summed[: 5 * piece].reshape(5, piece)
    own = piece // 2
    mine = jnp.where(first, vector_sum[:, :own], vector_sum[:, own:])
    theirs = jnp.where(first, vector_sum[:, own:], vector_sum[:, :own])
    vector_grads = mine + exchange(theirs)
    at = 5 * piece
    out_b_qkv = summed[at : at + 3 * part].reshape(3, 1, part)
    at = at + 3 * part
    out_b_up = summed[at : at + up_part].reshape(1, up_part)
    return (
        output[None],
        grad_input[None],
        vector_grads[0],
        vector_grads[1],
        vector_grads[2],
        vector_grads[3],
        grad_w_qkv,
        out_b_qkv,
        grad_w_out,
        vector_grads[4],
        second_sum[:, :ff_group],
        out_b_up,
        second_sum[:, ff_group:].T,
        vector_grads[4],
    )

def remote(src, dst, sends, recvs, at, to):
    return pltpu.make_async_remote_copy(
        src_ref=src,
        dst_ref=dst,
        send_sem=sends.at[at],
        recv_sem=recvs.at[at],
        device_id=to,
        device_id_type=pl.DeviceIdType.MESH,
    )


class Place:
    def __init__(self):
        self.s = lax.axis_index("shard")
        self.c = lax.axis_index("ctx")
        self.t = lax.axis_index("tensor")
        self.x = self.c // 2
        self.k = self.c % 2
        self.block = 2 * self.c + self.t
        self.core_c = 2 * self.x + (1 - self.k)
        self.x_c = 2 * (1 - self.x) + self.k
        self.far_c = 2 * (1 - self.x) + (1 - self.k)
        self.y_t = 1 - self.t
        self.core = {"ctx": self.core_c}
        self.across_x = {"ctx": self.x_c}
        self.far = {"ctx": self.far_c}
        self.across_y = {"tensor": self.y_t}

    def along(self, step):
        return {"shard": lax.rem(self.s + step + 4, 4)}

    def meet(self):
        barrier = pltpu.get_barrier_semaphore()
        others = [self.core, self.across_x, self.far, self.across_y]
        others += [self.along(step) for step in (1, 2, 3)]
        for other in others:
            pl.semaphore_signal(
                barrier, inc=1, device_id=other, device_id_type=pl.DeviceIdType.MESH
            )
        pl.semaphore_wait(barrier, len(others))

    def cube(self):
        pair = self.s + 1 - 2 * lax.rem(self.s, 2)
        return [
            self.core,
            {"shard": pair},
            self.along(2),
            self.across_x,
            self.across_y,
        ]


class PlaneGather:
    def __init__(self, place, own, full, sends, recvs, local):
        cut = own.shape[0] * 3 // 4
        b = place.block
        xb = 2 * place.x_c + place.t
        yb = 2 * place.c + place.y_t
        db = 2 * place.x_c + place.y_t
        low, high = pl.ds(0, cut), pl.ds(cut, own.shape[0] - cut)

        def to(src, dst, at, dev):
            return remote(src, dst, sends, recvs, at, dev)

        self.local = pltpu.make_async_copy(own, full.at[b], local)
        self.to_x = to(own, full.at[b], 0, place.across_x)
        self.to_y = to(own, full.at[b], 1, place.across_y)
        self.low_y = to(full.at[xb, low], full.at[xb, low], 2, place.across_y)
        self.high_x = to(full.at[yb, high], full.at[yb, high], 3, place.across_x)
        self.core_own = to(own, full.at[b], 4, place.core)
        self.core_x = to(full.at[xb], full.at[xb], 5, place.core)
        self.core_y = to(full.at[yb], full.at[yb], 6, place.core)
        self.core_d = to(full.at[db], full.at[db], 7, place.core)
        self.all = [
            self.to_x, self.to_y, self.low_y, self.high_x,
            self.core_own, self.core_x, self.core_y, self.core_d,
        ]

    def start(self):
        self.to_x.start()
        self.to_y.start()
        self.core_own.start()
        self.local.start()

    def second(self):
        self.to_x.wait_recv()
        self.low_y.start()
        self.core_x.start()
        self.to_y.wait_recv()
        self.high_x.start()
        self.core_y.start()

    def third(self):
        self.low_y.wait_recv()
        self.high_x.wait_recv()
        self.core_d.start()

    def finish(self):
        self.local.wait()
        for copy in (self.core_own, self.core_x, self.core_y, self.core_d):
            copy.wait_recv()

    def drain(self):
        for copy in self.all:
            copy.wait_send()


class CtxSwap:
    def __init__(self, place, own, dst, sends, recvs, local):
        c = place.c
        self.copies = []
        for at, (peer, dev) in enumerate(
            ((place.core_c, place.core), (place.x_c, place.across_x), (place.far_c, place.far))
        ):
            self.copies.append(remote(own.at[peer], dst.at[c], sends, recvs, at, dev))
        self.local = pltpu.make_async_copy(own.at[c], dst.at[c], local)

    def start(self):
        for copy in self.copies:
            copy.start()
        self.local.start()

    def finish(self):
        for copy in self.copies:
            copy.wait_recv()
        self.local.wait()

    def drain(self):
        for copy in self.copies:
            copy.wait_send()


class ChainGather:
    def __init__(self, place, full, right, left, recvs):
        self.s = place.s
        s = place.s

        def copy(j, sends, dev):
            return pltpu.make_async_remote_copy(
                src_ref=full.at[j],
                dst_ref=full.at[j],
                send_sem=sends.at[j],
                recv_sem=recvs.at[j],
                device_id=dev,
                device_id_type=pl.DeviceIdType.MESH,
            )

        self.to_right = lambda j: copy(j, right, place.along(1))
        self.to_left = lambda j: copy(j, left, place.along(-1))

    def start(self):
        s = self.s

        @pl.when(s < 3)
        def _():
            self.to_right(s).start()

        @pl.when(s > 0)
        def _():
            self.to_left(s).start()

    def step(self, distance):
        s = self.s

        @pl.when(s >= distance)
        def _():
            self.to_right(s - distance).wait_recv()

            @pl.when(s < 3)
            def _():
                self.to_right(s - distance).start()

        @pl.when(s + distance <= 3)
        def _():
            self.to_left(s + distance).wait_recv()

            @pl.when(s > 0)
            def _():
                self.to_left(s + distance).start()

    def drain(self):
        s = self.s
        for distance in range(4):

            @pl.when((s >= distance) & (s < 3))
            def _():
                self.to_right(s - distance).wait_send()

            @pl.when((s + distance <= 3) & (s > 0))
            def _():
                self.to_left(s + distance).wait_send()


class CubeSum:
    def __init__(self, place, total, slots, sends, recvs):
        self.total, self.slots = total, slots
        self.copies = [
            remote(total, slots.at[at], sends, recvs, at, dev)
            for at, dev in enumerate(place.cube())
        ]

    def start(self, at):
        self.copies[at].start()

    def finish(self, at):
        self.copies[at].wait()
        self.total[...] += self.slots[at]


def half_mask(rows, lanes, head):
    lane = lax.broadcasted_iota(jnp.int32, (rows, lanes), 1)
    return (lane < HD) if head == 0 else (lane >= HD)


def stack_heads(value):
    rows, lanes = value.shape
    parts = [jnp.where(half_mask(rows, lanes, head), value, 0.0) for head in range(2)]
    return jnp.concatenate(parts, 0)


def join_heads(value):
    rows, lanes = value.shape[0] // 2, value.shape[1]
    return jnp.where(half_mask(rows, lanes, 0), value[:rows], value[rows:])


def turn_block(value, cosine, sine):
    lanes = value.shape[1]
    lane = lax.broadcasted_iota(jnp.int32, value.shape, 1) % HD
    half = ROT // 2
    up = pltpu.roll(value, lanes - half, 1)
    down = pltpu.roll(value, half, 1)
    return value * cosine + jnp.where(lane < half, up, down) * sine


def attention_rows(at, rows, q_all, k_all, v_all, g_all, scores, key_grad, value_grad):
    length = (at + 1) * rows
    here = pl.ds(at * rows, rows)
    seen = pl.ds(0, length)
    queries = stack_heads(q_all[here].astype(f32)).astype(bf16)
    scores[:, seen] = contract_last(queries, k_all[seen])
    edge = pl.ds(at * rows, rows)
    key_at = lax.broadcasted_iota(jnp.int32, (rows, rows), 1)
    query_at = lax.broadcasted_iota(jnp.int32, (rows, rows), 0)
    keep = key_at <= query_at
    for head in range(2):
        part = pl.ds(head * rows, rows)
        scores[part, edge] = jnp.where(keep, scores[part, edge], -1e30)
    top = jnp.max(scores[:, seen], -1, keepdims=True)
    weights = jnp.exp(scores[:, seen] - top)
    scores[:, seen] = weights
    inverse = 1.0 / jnp.sum(weights, -1, keepdims=True)
    low = weights.astype(bf16)
    mixed = jnp.dot(low, v_all[seen], preferred_element_type=f32) * inverse
    grads = (stack_heads(g_all[here].astype(f32)) * inverse).astype(bf16)
    inner = jnp.sum(grads.astype(f32) * mixed, -1, keepdims=True)
    value_grad[:, seen] += contract_first(grads, low)
    prob_grad = contract_last(grads, v_all[seen])
    score_grad = (scores[:, seen] * (prob_grad - inner)).astype(bf16)
    key_grad[:, seen] += contract_first(queries, score_grad)
    query_grad = jnp.dot(score_grad, k_all[seen], preferred_element_type=f32)
    return join_heads(mixed), join_heads(query_grad) * (HD ** (-0.5))


def pack_weights(w_qkv, w_out, w_up, w_down, wa_own, wm_own):
    n_ctx, _, wide_a = wa_own.shape
    lanes, units = wide_a // 4, wm_own.shape[2] // 2
    for at in range(n_ctx):
        cols = slice(at * lanes, (at + 1) * lanes)
        for j in range(3):
            wa_own[at, :, j * lanes : (j + 1) * lanes] = w_qkv[j, :, cols]
        wa_own[at, :, 3 * lanes :] = w_out[:, cols]
        cols = slice(at * units, (at + 1) * units)
        wm_own[at, :, :units] = w_up[:, cols]
        wm_own[at, :, units:] = w_down[:, cols]


def place_vectors(place, nine, b_up, small):
    model = small.shape[1]
    group = 4 * place.s + place.c
    part = nine.shape[1]
    four = jnp.concatenate([nine[...]] * (128 // part), 1)
    spread = jnp.concatenate([four] * (model // 128), 1)
    slot = lax.broadcasted_iota(jnp.int32, spread.shape, 1) // part
    row = lax.broadcasted_iota(jnp.int32, spread.shape, 0)
    owner = jnp.where(row < 6, 2 * group + place.t, 16 * place.t + group)
    small[0:9] = jnp.where(slot == owner, spread, 0.0)
    width = b_up.shape[1]
    spread = jnp.concatenate([b_up[...].astype(f32)] * (model // width), 1)
    shape = (4, model)
    slot = lax.broadcasted_iota(jnp.int32, shape, 1) // width
    slot = slot + lax.broadcasted_iota(jnp.int32, shape, 0) * (model // width)
    small[9:13] = jnp.where(slot == 16 * place.t + group, spread, 0.0)
    small[13:16] = jnp.zeros((3, model), f32)


def gather_kernel(
    x_own, dy_own, w_qkv, w_out, w_up, w_down, nine, b_up, cosine, sine,
    x_out, dy_out, wa_all, wm_all, small_all, mixed_all, grads_all, ga_all,
    x_all, dy_all, wa_own, wm_own, slots, first_norm, q_all, k_all, v_all, g_all, scores, key_grad, value_grad, flipped,
    x_send, x_recv, dy_send, dy_recv, wa_send, wa_recv, wm_send, wm_recv,
    ca_right, ca_left, ca_recv, cm_right, cm_left, cm_recv, cube_send, cube_recv, local,
):
    place = Place()
    pack_weights(w_qkv, w_out, w_up, w_down, wa_own, wm_own)
    place_vectors(place, nine, b_up, small_all)
    place.meet()
    xs = PlaneGather(place, x_own, x_all, x_send, x_recv, local.at[0])
    dys = PlaneGather(place, dy_own, dy_all, dy_send, dy_recv, local.at[1])
    swap_a = CtxSwap(place, wa_own, wa_all.at[place.s], wa_send, wa_recv, local.at[2])
    swap_m = CtxSwap(place, wm_own, wm_all.at[place.s], wm_send, wm_recv, local.at[3])
    chain_a = ChainGather(place, wa_all, ca_right, ca_left, ca_recv)
    chain_m = ChainGather(place, wm_all, cm_right, cm_left, cm_recv)
    cube = CubeSum(place, small_all, slots, cube_send, cube_recv)
    blocks, rows, model = x_all.shape
    lanes = q_all.shape[1]
    width = 4 * lanes
    first = place.t * width + place.c * lanes
    first = pl.ds(pl.multiple_of(first, lanes), lanes)

    cube.start(0)
    swap_a.start()
    xs.start()
    swap_m.start()
    key_grad[...] = jnp.zeros_like(key_grad)
    value_grad[...] = jnp.zeros_like(value_grad)
    cube.finish(0)
    cube.start(1)
    cube.finish(1)
    cube.start(2)
    cube.finish(2)
    swap_a.finish()
    chain_a.start()
    cube.start(3)
    xs.second()
    dys.start()
    chain_a.step(1)
    swap_m.finish()
    chain_m.start()
    cube.finish(3)
    cube.start(4)
    chain_a.step(2)
    xs.third()
    cube.finish(4)
    xs.finish()
    save_x = pltpu.make_async_copy(x_all, x_out, local.at[4])
    save_x.start()

    def norm(at, carry):
        normed, _ = layer_norm_parts(x_all[at].astype(f32))
        first_norm[at] = (normed * small_all[0:1] + small_all[1:2]).astype(bf16)
        return carry

    lax.fori_loop(0, blocks, norm, 0)
    dys.second()
    chain_a.step(3)

    def weights_of(j, count=1):
        return wa_all[:, :, :, j * lanes : (j + count) * lanes].reshape(model, count * lanes)

    def project(at, carry):
        here = pl.ds(pl.multiple_of(at * rows, rows), rows)
        both = jnp.dot(first_norm[at], weights_of(0, 3), preferred_element_type=f32)
        cos_here, sin_here = cosine[here], sine[here]
        parts = [both[:, j * lanes : (j + 1) * lanes] + small_all[6 + j : 7 + j, first] for j in range(3)]
        queries = turn_block(parts[0], cos_here, sin_here).astype(bf16)
        q_all[here] = (queries.astype(f32) * (HD ** (-0.5))).astype(bf16)
        k_all[here] = turn_block(parts[1], cos_here, sin_here).astype(bf16)
        v_all[here] = parts[2].astype(bf16)
        return carry

    lax.fori_loop(0, blocks, project, 0)
    dys.third()
    chain_m.step(1)
    dys.finish()
    save_dy = pltpu.make_async_copy(dy_all, dy_out, local.at[5])
    save_dy.start()

    def back(at, carry):
        here = pl.ds(pl.multiple_of(at * rows, rows), rows)
        g_all[here] = jnp.dot(
            dy_all[at], weights_of(3), preferred_element_type=f32
        ).astype(bf16)
        return carry

    lax.fori_loop(0, blocks, back, 0)
    for at in range(blocks):
        here = pl.ds(at * rows, rows)
        mixed, query_grad = attention_rows(
            at, rows, q_all, k_all, v_all, g_all, scores, key_grad, value_grad
        )
        mixed_all[here] = mixed.astype(bf16)
        query_grad = query_grad.astype(bf16).astype(f32)
        query_grad = turn_block(query_grad, cosine[here], -sine[here])
        grads_all[here, 0:lanes] = query_grad.astype(bf16)
        flipped[0:lanes, here] = query_grad.T.astype(bf16)
        flipped[3 * lanes : 4 * lanes, here] = mixed.T.astype(bf16)
        if at == 3:
            chain_m.step(2)

    for at in range(blocks):
        here = pl.ds(at * rows, rows)
        turned = key_grad[:, here].T.astype(bf16).astype(f32)
        turned = turn_block(turned, cosine[here], -sine[here])
        grads_all[here, lanes : 2 * lanes] = turned.astype(bf16)
        flipped[lanes : 2 * lanes, here] = turned.T.astype(bf16)
        grads_all[here, 2 * lanes : 3 * lanes] = value_grad[:, here].T.astype(bf16)
        flipped[2 * lanes : 3 * lanes, here] = value_grad[:, here].astype(bf16)
    piece = model // 4
    for d in range(4):
        cols = slice(d * piece, (d + 1) * piece)
        normed = first_norm[:, :, cols].reshape(blocks * rows, piece)
        ga_all[d, 0 : 3 * lanes] = jnp.dot(
            flipped[0 : 3 * lanes], normed, preferred_element_type=f32
        ).astype(bf16)
        grads = dy_all[:, :, cols].reshape(blocks * rows, piece)
        ga_all[d, 3 * lanes :] = jnp.dot(
            flipped[3 * lanes :], grads, preferred_element_type=f32
        ).astype(bf16)
    chain_m.step(3)
    for part in (xs, dys, swap_a, swap_m, chain_a, chain_m):
        part.drain()
    save_x.wait()
    save_dy.wait()


def gather_all(x_own, dy_own, w_qkv, w_out, w_up, w_down, nine, b_up, cosine, sine):
    rows, model = x_own.shape
    depth = w_up.shape[0]
    n_ctx = 4
    wide_a = 4 * w_out.shape[1] // n_ctx
    wide_m = 2 * w_down.shape[1] // n_ctx
    seq_len, lanes = cosine.shape
    anywhere = pl.BlockSpec(memory_space=pl.ANY)
    vmem = pl.BlockSpec(memory_space=pltpu.VMEM)
    dma = pltpu.SemaphoreType.DMA
    return pl.pallas_call(
        gather_kernel,
        out_shape=(
            jax.ShapeDtypeStruct((8, rows, model), bf16),
            jax.ShapeDtypeStruct((8, rows, model), bf16),
            jax.ShapeDtypeStruct((4, n_ctx, depth, wide_a), bf16),
            jax.ShapeDtypeStruct((4, n_ctx, depth, wide_m), bf16),
            jax.ShapeDtypeStruct((16, model), f32),
            jax.ShapeDtypeStruct((seq_len, lanes), bf16),
            jax.ShapeDtypeStruct((seq_len, 3 * lanes), bf16),
            jax.ShapeDtypeStruct((4, wide_a, model // 4), bf16),
        ),
        in_specs=[anywhere] * 2 + [vmem] * 8,
        out_specs=[anywhere] * 2 + [vmem] * 6,
        scratch_shapes=[
            pltpu.VMEM((8, rows, model), bf16),
            pltpu.VMEM((8, rows, model), bf16),
            pltpu.VMEM((n_ctx, depth, wide_a), bf16),
            pltpu.VMEM((n_ctx, depth, wide_m), bf16),
            pltpu.VMEM((5, 16, model), f32),
            pltpu.VMEM((8, rows, model), bf16),
            pltpu.VMEM((seq_len, lanes), bf16),
            pltpu.VMEM((seq_len, lanes), bf16),
            pltpu.VMEM((seq_len, lanes), bf16),
            pltpu.VMEM((seq_len, lanes), bf16),
            pltpu.VMEM((2 * rows, seq_len), f32),
            pltpu.VMEM((lanes, seq_len), f32),
            pltpu.VMEM((lanes, seq_len), f32),
            pltpu.VMEM((4 * lanes, seq_len), bf16),
        ]
        + [dma((8,))] * 4
        + [dma((3,))] * 4
        + [dma((4,))] * 6
        + [dma((5,))] * 2
        + [dma((6,))],
        compiler_params=pltpu.CompilerParams(
            collective_id=0, has_side_effects=True, vmem_limit_bytes=56 << 20
        ),
    )(x_own, dy_own, w_qkv, w_out, w_up, w_down, nine, b_up, cosine, sine)


class PlaneReduce:
    def __init__(self, place, parts, came, low_in, high_in, x_in, y_in, sends, recvs):
        self.place, self.parts, self.came = place, parts, came
        self.low_in, self.high_in, self.x_in, self.y_in = low_in, high_in, x_in, y_in
        x, t, k = place.x, place.t, place.k
        half = parts.shape[1] // 2
        self.half = half
        self.first = []
        for at in range(4):
            src = parts.at[4 * (at // 2) + 2 * (1 - k) + at % 2]
            self.first.append(remote(src, came.at[at], sends, recvs, at, place.core))
        self.sends, self.recvs = sends, recvs
        self.own = 4 * x + 2 * k + t
        self.of_x = 4 * (1 - x) + 2 * k + t
        self.of_y = 4 * x + 2 * k + (1 - t)
        self.of_d = 4 * (1 - x) + 2 * k + (1 - t)
        self.low = remote(
            parts.at[self.of_d, pl.ds(0, half)], low_in, sends, recvs, 4, place.across_x
        )
        self.high = remote(
            parts.at[self.of_d, pl.ds(half, half)], high_in, sends, recvs, 5, place.across_y
        )
        self.to_x = remote(parts.at[self.of_x], x_in, sends, recvs, 6, place.across_x)
        self.to_y = remote(parts.at[self.of_y], y_in, sends, recvs, 7, place.across_y)

    def source(self, at, core):
        return 4 * (at // 2) + 2 * core + at % 2

    def start_one(self, at):
        src = self.parts.at[self.source(at, 1 - self.place.k)]
        remote(src, self.came.at[at], self.sends, self.recvs, at, self.place.core).start()

    def second(self):
        k = self.place.k
        for copy in self.first:
            copy.wait_recv()

        def add(at, carry):
            mine = self.parts[4 * (at // 2) + 2 * k + at % 2].astype(f32)
            here = 4 * (at // 2) + 2 * k + at % 2
            self.parts[here] = (mine + self.came[at].astype(f32)).astype(bf16)
            return carry

        lax.fori_loop(0, 4, add, 0)
        self.low.start()
        self.high.start()

    def third(self):
        half = self.half
        self.low.wait_recv()
        low, high = pl.ds(0, half), pl.ds(half, half)
        self.parts[self.of_y, low] = (
            self.parts[self.of_y, low].astype(f32) + self.low_in[...].astype(f32)
        ).astype(bf16)
        self.to_y.start()
        self.high.wait_recv()
        self.parts[self.of_x, high] = (
            self.parts[self.of_x, high].astype(f32) + self.high_in[...].astype(f32)
        ).astype(bf16)
        self.to_x.start()

    def finish(self):
        self.to_x.wait_recv()
        self.to_y.wait_recv()

    def total(self, rows):
        return (
            self.parts[self.own, rows].astype(f32)
            + self.x_in[rows].astype(f32)
            + self.y_in[rows].astype(f32)
        )

    def drain(self):
        for copy in self.first + [self.low, self.high, self.to_x, self.to_y]:
            copy.wait_send()


class ChainReduce:
    def __init__(self, place, parts, slots, sums, sends, recvs):
        self.s = place.s
        self.parts, self.slots, self.sums = parts, slots, sums

        def copy(src, d, slot, dev):
            return pltpu.make_async_remote_copy(
                src_ref=src,
                dst_ref=slots.at[slot],
                send_sem=sends.at[d],
                recv_sem=recvs.at[slot],
                device_id=dev,
                device_id_type=pl.DeviceIdType.MESH,
            )

        right, left = place.along(1), place.along(-1)
        self.to_right = lambda src, d: copy(src.at[d], d, d, right)
        self.to_left = lambda src, d, k: copy(src.at[d], d, 4 if k == 1 else d, left)

    def step(self, k):
        s = self.s

        def add(d):
            def one(at, carry):
                self.sums[d, at] = (
                    self.parts[d, at].astype(f32) + self.slots[d, at].astype(f32)
                ).astype(bf16)
                return carry

            lax.fori_loop(0, self.parts.shape[1], one, 0)

        @pl.when((s > 0) & (s + k <= 3))
        def _():
            self.to_right(self.parts, s + k).wait_recv()
            add(s + k)
            self.to_right(self.sums, s + k).start()

        @pl.when((s < 3) & (s - k >= 0))
        def _():
            self.to_left(self.parts, s - k, 2).wait_recv()
            add(s - k)
            self.to_left(self.sums, s - k, k).start()

    def edge(self, k):
        s = self.s

        @pl.when(s == 0)
        def _():
            self.to_right(self.parts, s + k).start()

        @pl.when(s == 3)
        def _():
            self.to_left(self.parts, s - k, k).start()

    def finish(self, out):
        s = self.s

        @pl.when(s > 0)
        def _():
            self.to_right(self.parts, s).wait_recv()

        @pl.when(s < 3)
        def _():
            self.to_left(self.parts, s, 1).wait_recv()


        def one(at, carry):
            out[at] = self.parts[s, at]

            @pl.when(s > 0)
            def _():
                out[at] = (out[at].astype(f32) + self.slots[s, at].astype(f32)).astype(bf16)

            @pl.when(s < 3)
            def _():
                out[at] = (out[at].astype(f32) + self.slots[4, at].astype(f32)).astype(bf16)

            return carry

        lax.fori_loop(0, self.parts.shape[1], one, 0)

    def drain(self):
        s = self.s
        for k in (3, 2, 1):

            @pl.when(s + k <= 3)
            def _():
                self.to_right(self.parts, s + k).wait_send()

            @pl.when(s - k >= 0)
            def _():
                self.to_left(self.parts, s - k, k).wait_send()


def turn_parts(flat, turned):
    pieces, rows, wide = flat.shape
    n_ctx, depth, _ = turned.shape
    for at in range(pieces):
        part = flat[at].astype(f32).T.astype(bf16)
        turned[:, :, at * rows : (at + 1) * rows] = part.reshape(n_ctx, depth, rows)


def far_first(s, at):
    d = jnp.where(s == 1, (3, 2, 0, 1)[at], (0, 1, 3, 2)[at])
    return jnp.where(s == 0, 3 - at, jnp.where(s == 3, at, d))


def reduce_kernel(
    x_all, dy_all, wa, wm, small, mixed_all, grads_all, ga,
    output, grad_in, ga_back, gm_back, vec_sum,
    second_norm, grad_pre_all, flipped, gm,
    po, po_came, po_low, po_high, po_x, po_y,
    ps, ps_came, ps_low, ps_high, ps_x, ps_y,
    ga_slots, ga_sums, ga_flat, ga_total, gm_slots, gm_flat, gm_total, slots,
    po_send, po_recv, ps_send, ps_recv, ga_send, ga_recv, gm_send, gm_recv,
    sa_send, sa_recv, sm_send, sm_recv, cube_send, cube_recv, local,
):
    place = Place()
    place.meet()
    cube = CubeSum(place, vec_sum, slots, cube_send, cube_recv)
    outs = PlaneReduce(place, po, po_came, po_low, po_high, po_x, po_y, po_send, po_recv)
    scaled = PlaneReduce(place, ps, ps_came, ps_low, ps_high, ps_x, ps_y, ps_send, ps_recv)
    chain_a = ChainReduce(place, ga, ga_slots, ga_sums, ga_send, ga_recv)
    chain_m = ChainReduce(place, gm, gm_slots, gm, gm_send, gm_recv)
    swap_a = CtxSwap(place, ga_total, ga_back, sa_send, sa_recv, local.at[0])
    swap_m = CtxSwap(place, gm_total, gm_back, sm_send, sm_recv, local.at[1])
    blocks, rows, model = x_all.shape
    lanes = ga.shape[2]
    units = grad_pre_all.shape[2]
    s, c, t = place.s, place.c, place.t
    for k in (3, 2, 1):
        chain_a.edge(k)
    vec_sum[...] = jnp.zeros_like(vec_sum)
    up_row = pl.ds(8 + 2 * t + c // 2, 1)
    up_cols = pl.ds(pl.multiple_of((c % 2) * units, units), units)
    in_up_row = pl.ds(9 + 2 * t + c // 2, 1)

    def up():
        return wm[:, :, :, 0:units].reshape(model, units)

    def down_t():
        return wm[:, :, :, units : 2 * units].reshape(model, units)

    def block_of(at):
        late = at // 4
        core = late * place.k + (1 - late) * (1 - place.k)
        return outs.source(at - 4 * late, core)

    def forward(at, carry):
        b = block_of(at)
        here = pl.ds(pl.multiple_of(b * rows, rows), rows)
        normed, _ = layer_norm_parts(x_all[b].astype(f32))
        second = (normed * small[2:3] + small[3:4]).astype(bf16)
        second_norm[b] = second
        pre = jnp.dot(second, up(), preferred_element_type=f32) + small[in_up_row, up_cols]
        phi = 0.5 * (1.0 + lax.erf(pre * 0.7071067811865476))
        hidden = (pre * phi).astype(bf16)
        flipped[units : 2 * units, here] = hidden.astype(f32).T.astype(bf16)
        slope = phi + pre * jnp.exp(-0.5 * pre * pre) * 0.3989422804014327
        grad_hidden = jnp.dot(dy_all[b], down_t(), preferred_element_type=f32)
        grad_pre = grad_hidden * slope
        flipped[0:units, here] = grad_pre.T.astype(bf16)
        grad_pre = grad_pre.astype(bf16)
        grad_pre_all[b] = grad_pre
        vec_sum[up_row, up_cols] += jnp.sum(grad_pre.astype(f32), 0, keepdims=True)
        out_t = wa[:, :, :, 3 * lanes :].reshape(model, lanes)
        po[b] = (
            contract_last(hidden, down_t()) + contract_last(mixed_all[here], out_t)
        ).astype(bf16)

        @pl.when(at < 4)
        def _():
            outs.start_one(at)

        @pl.when(at == 2)
        def _():
            chain_a.step(2)

        @pl.when(at == 5)
        def _():
            chain_a.step(1)

        return carry

    lax.fori_loop(0, blocks, forward, 0)
    outs.second()
    piece = model // 4
    for at in range(4):
        d = far_first(s, at)
        cols = pl.ds(pl.multiple_of(d * piece, piece), piece)
        normed = second_norm[:, :, cols].reshape(blocks * rows, piece)
        grads = dy_all[:, :, cols].reshape(blocks * rows, piece)
        half = gm.shape[1] // 2
        shape = (half,) + gm.shape[2:]
        gm[d, 0:half] = (
            jnp.dot(flipped[0:units], normed, preferred_element_type=f32)
            .astype(bf16)
            .reshape(shape)
        )
        gm[d, half:] = (
            jnp.dot(flipped[units:], grads, preferred_element_type=f32)
            .astype(bf16)
            .reshape(shape)
        )
        if at < 3:
            chain_m.edge(3 - at)
    chain_a.finish(ga_flat)
    turn_parts(ga_flat, ga_total)
    swap_a.start()
    outs.third()

    def backward(at, carry):
        b = block_of(at)
        here = pl.ds(pl.multiple_of(b * rows, rows), rows)
        normed, _ = layer_norm_parts(x_all[b].astype(f32))
        grad_second = contract_last(grad_pre_all[b], up())
        vec_sum[2:3] += jnp.sum(grad_second * normed, 0, keepdims=True)
        vec_sum[3:4] += jnp.sum(grad_second, 0, keepdims=True)
        w_qkv = wa[:, :, :, 0 : 3 * lanes].reshape(model, 3 * lanes)
        grad_first = contract_last(grads_all[here], w_qkv)
        vec_sum[0:1] += jnp.sum(grad_first * normed, 0, keepdims=True)
        vec_sum[1:2] += jnp.sum(grad_first, 0, keepdims=True)
        ps[b] = (grad_first * small[0:1] + grad_second * small[2:3]).astype(bf16)

        @pl.when(at < 4)
        def _():
            scaled.start_one(at)

        @pl.when(at == 3)
        def _():
            chain_m.step(2)

        return carry

    lax.fori_loop(0, blocks, backward, 0)
    vec_sum[4:5] = jnp.sum(dy_all[place.block].astype(f32), 0, keepdims=True)
    first = pl.ds(pl.multiple_of((4 * t + c) * lanes, lanes), lanes)
    for j in range(3):
        part = grads_all[:, j * lanes : (j + 1) * lanes].astype(f32)
        vec_sum[5 + j : 6 + j, first] = jnp.sum(part, 0, keepdims=True)
    cube.start(0)
    scaled.second()
    chain_m.step(1)
    scaled.third()
    cube.finish(0)
    cube.start(1)
    outs.finish()
    cube.finish(1)
    cube.start(2)
    step = 64
    mine = place.block

    def final_out(at, carry):
        here = pl.ds(pl.multiple_of(at * step, step), step)
        bias = small[4:5] + small[5:6]
        output[here] = (x_all[mine, here].astype(f32) + outs.total(here) + bias).astype(bf16)
        return carry

    lax.fori_loop(0, rows // step, final_out, 0)
    swap_a.finish()
    cube.finish(2)
    cube.start(3)
    chain_m.finish(gm_flat)
    turn_parts(gm_flat, gm_total)
    swap_m.start()
    scaled.finish()
    cube.finish(3)
    cube.start(4)

    def final_in(at, carry):
        here = pl.ds(pl.multiple_of(at * step, step), step)
        normed, inv = layer_norm_parts(x_all[mine, here].astype(f32))
        part = scaled.total(here)
        inner = jnp.mean(part, -1, keepdims=True)
        aligned = jnp.mean(part * normed, -1, keepdims=True)
        grad_in[here] = dy_all[mine, here].astype(f32) + inv * (part - inner - normed * aligned)
        return carry

    lax.fori_loop(0, rows // step, final_in, 0)
    cube.finish(4)
    swap_m.finish()
    for part in (outs, scaled, chain_a, chain_m, swap_a, swap_m):
        part.drain()


def reduce_all(x_all, dy_all, wa, wm, small, mixed, grads, ga):
    blocks, rows, model = x_all.shape
    depth, wide_a = wa.shape[2:]
    wide_m = wm.shape[3]
    units, lanes = wide_m // 2, wide_a // 4
    seq_len = blocks * rows
    vmem = pl.BlockSpec(memory_space=pltpu.VMEM)
    dma = pltpu.SemaphoreType.DMA
    plane = [
        pltpu.VMEM((blocks, rows, model), bf16),
        pltpu.VMEM((4, rows, model), bf16),
        pltpu.VMEM((rows // 2, model), bf16),
        pltpu.VMEM((rows // 2, model), bf16),
        pltpu.VMEM((rows, model), bf16),
        pltpu.VMEM((rows, model), bf16),
    ]
    parts_a = ga.shape[1:]
    parts_m = (wide_m // lanes,) + ga.shape[2:]

    def swapped(wide):
        return [pltpu.VMEM((4, depth, wide), bf16)]

    vec = (16, model)
    return pl.pallas_call(
        reduce_kernel,
        out_shape=(
            jax.ShapeDtypeStruct((rows, model), bf16),
            jax.ShapeDtypeStruct((rows, model), f32),
            jax.ShapeDtypeStruct((4, depth, wide_a), bf16),
            jax.ShapeDtypeStruct((4, depth, wide_m), bf16),
            jax.ShapeDtypeStruct(vec, f32),
        ),
        in_specs=[vmem] * 8,
        out_specs=[vmem] * 5,
        scratch_shapes=[
            pltpu.VMEM((blocks, rows, model), bf16),
            pltpu.VMEM((blocks, rows, units), bf16),
            pltpu.VMEM((wide_m, seq_len), bf16),
            pltpu.VMEM((4,) + parts_m, bf16),
        ]
        + plane
        + plane
        + [
            pltpu.VMEM((5,) + parts_a, bf16),
            pltpu.VMEM((4,) + parts_a, bf16),
            pltpu.VMEM(parts_a, bf16),
        ]
        + swapped(wide_a)
        + [pltpu.VMEM((5,) + parts_m, bf16), pltpu.VMEM(parts_m, bf16)]
        + swapped(wide_m)
        + [pltpu.VMEM((5,) + vec, f32)]
        + [dma((8,))] * 4
        + [dma((4,)), dma((5,))] * 2
        + [dma((3,))] * 4
        + [dma((5,))] * 2
        + [dma((2,))],
        compiler_params=pltpu.CompilerParams(
            collective_id=1, has_side_effects=True, vmem_limit_bytes=60 << 20
        ),
    )(x_all, dy_all, wa, wm, small, mixed, grads, ga)


def finish_kernel(
    output, grad_in, ga_back, gm_back, vec,
    output_out, grad_in_out, g_qkv, g_out, g_up, g_down,
    gain_one, shift_one, gain_two, shift_two, b_out, b_down, b_qkv, b_up,
):
    place = Place()
    output_out[...] = output[...]
    grad_in_out[...] = grad_in[...]
    lanes, units = ga_back.shape[2] // 4, gm_back.shape[2] // 2
    for at in range(ga_back.shape[0]):
        cols = slice(at * lanes, (at + 1) * lanes)
        for j in range(3):
            g_qkv[j, :, cols] = ga_back[at, :, j * lanes : (j + 1) * lanes].astype(f32)
        g_out[:, cols] = ga_back[at, :, 3 * lanes :].astype(f32)
        cols = slice(at * units, (at + 1) * units)
        g_up[:, cols] = gm_back[at, :, :units].astype(f32)
        g_down[:, cols] = gm_back[at, :, units:].astype(f32)
    model = vec.shape[1]
    part = b_out.shape[1]
    group = 4 * place.s + place.c
    start = part * (2 * group + place.t)
    shifted = pltpu.roll(vec[0:8], lax.rem(model - start, model), 1)
    for row, ref in enumerate((gain_one, shift_one, gain_two, shift_two, b_out)):
        ref[...] = shifted[row : row + 1, :part]
    b_down[...] = shifted[4:5, :part]
    start = part * (16 * place.t + group)
    shifted = pltpu.roll(vec[0:8], lax.rem(model - start, model), 1)
    for j in range(3):
        b_qkv[j] = shifted[5 + j : 6 + j, :part]
    width = b_up.shape[1]
    start = width * (16 * place.t + group)
    four = vec[8:12]
    row = lax.broadcasted_iota(jnp.int32, four.shape, 0)
    one = jnp.sum(jnp.where(row == start // model, four, 0.0), 0, keepdims=True)
    one = jnp.broadcast_to(one, (8, model))
    shifted = pltpu.roll(one, lax.rem(model - lax.rem(start, model), model), 1)
    b_up[...] = shifted[0:1, :width]


def finish_all(output, grad_in, ga_back, gm_back, vec, piece, part):
    n_ctx, depth, wide_a = ga_back.shape
    wide_m = gm_back.shape[2]
    vmem = pl.BlockSpec(memory_space=pltpu.VMEM)
    vector = jax.ShapeDtypeStruct((1, piece), f32)
    return pl.pallas_call(
        finish_kernel,
        out_shape=(
            jax.ShapeDtypeStruct(output.shape, output.dtype),
            jax.ShapeDtypeStruct(grad_in.shape, grad_in.dtype),
            jax.ShapeDtypeStruct((3, depth, n_ctx * wide_a // 4), f32),
            jax.ShapeDtypeStruct((depth, n_ctx * wide_a // 4), f32),
            jax.ShapeDtypeStruct((depth, n_ctx * wide_m // 2), f32),
            jax.ShapeDtypeStruct((depth, n_ctx * wide_m // 2), f32),
        )
        + (vector,) * 6
        + (
            jax.ShapeDtypeStruct((3, 1, piece), f32),
            jax.ShapeDtypeStruct((1, part), f32),
        ),
        in_specs=[vmem] * 5,
        out_specs=[vmem] * 14,
        compiler_params=pltpu.CompilerParams(vmem_limit_bytes=60 << 20),
    )(output, grad_in, ga_back, gm_back, vec)


def rotary_lanes(seq_len, lanes):
    half = ROT // 2
    inverse = rope_base ** (-np.arange(half) / half)
    angles = np.arange(seq_len)[:, None] * inverse[None, :]
    plain = np.zeros((seq_len, HD - ROT))
    cosine = np.concatenate([np.cos(angles), np.cos(angles), plain + 1], 1)
    sine = np.concatenate([-np.sin(angles), np.sin(angles), plain], 1)
    heads = lanes // HD
    return (
        jnp.asarray(np.tile(cosine, (1, heads)), f32),
        jnp.asarray(np.tile(sine, (1, heads)), f32),
    )


def turn_lanes(value, cosine, sine):
    lane = lax.broadcasted_iota(jnp.int32, value.shape, 1) % HD
    half = ROT // 2
    swapped = jnp.where(lane < half, jnp.roll(value, -half, 1), jnp.roll(value, half, 1))
    return value * cosine + swapped * sine


def per_device_plane(
    inputs, ln1_gain, ln1_bias, ln2_gain, ln2_bias, w_qkv, b_qkv, w_out, b_out,
    w_up, b_up, w_down, b_down, cotangent,
):
    x_own, dy_own = inputs[0], cotangent[0]
    rows, model = x_own.shape
    seq_len = rows * 8
    lanes = w_out.shape[0] // 4
    vectors = jnp.stack([ln1_gain, ln1_bias, ln2_gain, ln2_bias, b_out, b_down])
    nine = jnp.concatenate([vectors, b_qkv[:, 0]]).astype(f32)
    cosine, sine = rotary_lanes(seq_len, lanes)
    x_all, dy_all, first, second, small, mixed, grad_projected, ga = gather_all(
        x_own, dy_own, w_qkv, w_out.T, w_up, w_down.T, nine, b_up, cosine, sine
    )
    output, grad_in, ga_back, gm_back, vec = reduce_all(
        x_all, dy_all, first, second, small, mixed, grad_projected,
        ga.reshape(4, 4, lanes, model // 4),
    )
    output, grad_in, g_qkv, g_out, g_up, g_down, *vectors, g_b_qkv, g_b_up = finish_all(
        output, grad_in, ga_back, gm_back, vec, b_out.shape[0], b_up.shape[1]
    )
    g_one, s_one, g_two, s_two, g_b_out, g_b_down = (v.reshape(-1) for v in vectors)
    return (
        output[None], grad_in[None], g_one, s_one, g_two, s_two, g_qkv, g_b_qkv, g_out.T,
        g_b_out, g_up, g_b_up, g_down.T, g_b_down,
    )


def fits_plane(mesh):
    return tuple(mesh.shape[name] for name in ("shard", "ctx", "tensor")) == (4, 4, 2)


def solution(mesh):
    placed = (
        P("shard", ("ctx", "tensor"), None),
        P(("shard", "ctx", "tensor")),
        P(("shard", "ctx", "tensor")),
        P(("shard", "ctx", "tensor")),
        P(("shard", "ctx", "tensor")),
        P(None, ("shard", "ctx"), "tensor"),
        P(None, "tensor", ("shard", "ctx")),
        P("tensor", ("shard", "ctx")),
        P(("shard", "ctx", "tensor")),
        P(("shard", "ctx"), "tensor"),
        P("tensor", ("shard", "ctx")),
        P("tensor", ("shard", "ctx")),
        P(("shard", "ctx", "tensor")),
        P("shard", ("ctx", "tensor"), None),
    )
    return jax.shard_map(
        per_device_plane if fits_plane(mesh) else per_device,
        mesh=mesh,
        in_specs=placed,
        out_specs=(
            P("shard", ("ctx", "tensor"), None),
            P("shard", ("ctx", "tensor"), None),
            P(("shard", "ctx", "tensor")),
            P(("shard", "ctx", "tensor")),
            P(("shard", "ctx", "tensor")),
            P(("shard", "ctx", "tensor")),
            P(None, ("shard", "ctx"), "tensor"),
            P(None, "tensor", ("shard", "ctx")),
            P("tensor", ("shard", "ctx")),
            P(("shard", "ctx", "tensor")),
            P(("shard", "ctx"), "tensor"),
            P("tensor", ("shard", "ctx")),
            P("tensor", ("shard", "ctx")),
            P(("shard", "ctx", "tensor")),
        ),
        check_vma=False,
    )
```
